32 devices in a mesh: dp: 8 (over z, y), slot: 4 (over x, core).
Axes of the slice: x: 2, y: 2, z: 4, core: 2. Of those that a mesh axis runs over, the one named last changes fastest.
Arguments:
- tokens: bfloat16 [65536, 512], P(('dp', 'slot')), may hold values from -6 to 6
- memory: bfloat16 [8, 64, 512], P('dp', 'slot'), may hold values from -6 to 6
- pad_mask: int32 [65536], P(('dp', 'slot')), may hold values 0 or 1
- doc_lengths: int32 [12], replicated, may hold values from 1 to 8192, 65536 in all
- first_gain: float32 [512], replicated, may hold values from 0.1 to 1.9
- query_weight: bfloat16 [512, 512], replicated, may hold values from -0.25 to 0.25
- key_weight: bfloat16 [512, 512], replicated, may hold values from -0.25 to 0.25
- value_weight: bfloat16 [512, 512], replicated, may hold values from -0.25 to 0.25
- out_weight: bfloat16 [512, 512], replicated, may hold values from -1 to 1
- second_gain: float32 [512], replicated, may hold values from 0.1 to 1.9
- up_weight: bfloat16 [512, 2048], replicated, may hold values from -0.25 to 0.25
- down_weight: bfloat16 [2048, 512], replicated, may hold values from -0.1875 to 0.1875
- memory_gain: float32 [512], replicated, may hold values from 0.1 to 1.9
- slot_query_weight: bfloat16 [512, 512], replicated, may hold values from -0.25 to 0.25
- gate_weight: bfloat16 [512, 512], replicated, may hold values from -6 to 6
- gate_bias: float32 [512], replicated, may hold values from -2 to 2
- write_weight: bfloat16 [512, 512], replicated, may hold values from -6 to 6
- out_cotangent: bfloat16 [65536, 512], P(('dp', 'slot')), may hold values from -6 to 6
- memory_cotangent: bfloat16 [8, 64, 512], P('dp', 'slot'), may hold values from -6 to 6
Outputs:
- layer_out: bfloat16 [65536, 512], P(('dp', 'slot'))
- new_memory: float32 [8, 64, 512], P('dp', 'slot')
- input_grad: float32 [65536, 512], P(('dp', 'slot'))
- memory_grad: float32 [8, 64, 512], P('dp', 'slot')
- first_gain_grad: float32 [512], replicated
- query_weight_grad: float32 [512, 512], replicated
- key_weight_grad: float32 [512, 512], replicated
- value_weight_grad: float32 [512, 512], replicated
- out_weight_grad: float32 [512, 512], replicated
- second_gain_grad: float32 [512], replicated
- up_weight_grad: float32 [512, 2048], replicated
- down_weight_grad: float32 [2048, 512], replicated
- memory_gain_grad: float32 [512], replicated
- slot_query_weight_grad: float32 [512, 512], replicated
- gate_weight_grad: float32 [512, 512], replicated
- gate_bias_grad: float32 [512], replicated
- write_weight_grad: float32 [512, 512], replicated
The draws below stay inside these ranges and needn't reach their ends.
Inputs may be any that keep to these rules, and one draw needn't show every extreme that they name: `doc_lengths`: the lengths sum to 65536 and the largest is exactly 8192.
All inputs are finite; a program needn't handle non-finite values. No bound on the sum of `pad_mask` on one device may be relied on, other than what follows from the above.
Results may differ from the reference program's by a relative error of at most 0.03.
Values may be sent and summed in bfloat16 or wider, within the bound.
A program may use at most 256 MiB of HBM per device.

```python
import math
import jax
import jax.numpy as jnp
import numpy as np
from jax import lax

D = 512
H = 8
DH = 64
FF = 2048
MEM = 64
SEG = 512
DOC_MAX = 8192
STREAM = 8192
STREAMS = 8
TOKENS = 65536
DOCS = 12
N_DP = 8


def touch_ends(drawn, own_key, least, top_value):
    shape = drawn.shape
    spot = [jax.random.randint(jax.random.fold_in(own_key, axis), (), 0, shape[axis]) for axis in range(len(shape))]
    drawn = drawn.at[tuple(spot)].set(least)
    longest = shape.index(max(shape))
    spot[longest] = (spot[longest] + 1) % shape[longest]
    return drawn.at[tuple(spot)].set(top_value)


def block_levels(stream_key, shape, cuts, smallest, high):
    level, own = 1.0, jax.random.fold_in(stream_key, 6)
    for dim, blocks in cuts:
        heights = jnp.exp(jax.random.uniform(jax.random.fold_in(own, dim), (blocks,), jnp.float32, smallest / len(cuts), high / len(cuts)))
        level = level * jnp.repeat(heights, shape[dim] // blocks).reshape([-1 if axis == dim else 1 for axis in range(len(shape))])
    return level


def profile(amount, total, most, slope):
    loads = [(1 << 20) // math.isqrt(standing ** slope) + 1 for standing in range(2, amount + 1)]
    rest, given = total - most - (amount - 1), [1] * (amount - 1)
    while rest > 0:
        free = [i for i in range(amount - 1) if given[i] < most]
        pool, budget = sum([loads[i] for i in free]), rest
        for i in free:
            extra = min(most - given[i], max(1, budget * loads[i] // pool), rest)
            given[i] = given[i] + extra
            rest = rest - extra
    return np.array([most] + given)


def ragged_sizes(own_key, amount, total, reach, skew):
    if amount == 2:
        one = jax.random.randint(own_key, (), max(1, total - reach), min(reach, total - 1) + 1)
        return jnp.stack([one, total - one])
    sizes = jnp.asarray(profile(amount, total, reach, skew), jnp.int32)
    couples = (amount - 1) // 2
    donor, sink = sizes[1:1 + 2 * couples:2], sizes[2:2 + 2 * couples:2]
    slack = jnp.minimum(donor - 1, reach - sink)
    shifted = jax.random.randint(jax.random.fold_in(own_key, 1), (couples,), 0, 1 << 20) % (slack + 1)
    sizes = sizes.at[1:1 + 2 * couples:2].set(donor - shifted).at[2:2 + 2 * couples:2].set(sink + shifted)
    return sizes[jax.random.permutation(jax.random.fold_in(own_key, 2), amount)]


def noise(own_key, extent, deviation, limit, cuts=(), kind=jnp.bfloat16):
    result = jax.random.normal(own_key, extent, jnp.float32) * deviation
    if len(cuts) > 0:
        result = block_levels(own_key, extent, cuts, -0.22, 0.18) * result
    return jnp.clip(result, min=-limit, max=limit).astype(kind)


def setup_inputs(seed: int = 0) -> dict:
    key_of = jax.random.split(jax.random.key(seed), 20)
    return {
        "tokens": noise(key_of[0], (TOKENS, D), 1.0, 6.0, ((0, 32),)),
        "memory": noise(key_of[1], (STREAMS, MEM, D), 1.0, 6.0, ((0, 8), (1, 4))),
        "pad_mask": touch_ends((jax.random.randint(key_of[2], (TOKENS,), 0, 8) < 7).astype(jnp.int32), jax.random.fold_in(key_of[2], 1), 0, 1),
        "doc_lengths": ragged_sizes(key_of[3], DOCS, TOKENS, DOC_MAX, 1).astype(jnp.int32),
        "first_gain": jnp.clip(1.0 + 0.18 * jax.random.normal(key_of[4], (D,), jnp.float32), 0.1, 1.9),
        "query_weight": noise(key_of[5], (D, D), D ** -0.5, 0.25),
        "key_weight": noise(key_of[6], (D, D), D ** -0.5, 0.25),
        "value_weight": noise(key_of[7], (D, D), D ** -0.5, 0.25),
        "out_weight": noise(key_of[8], (D, D), (D // 16) ** -0.5, 1.0),
        "second_gain": jnp.clip(1.0 + 0.18 * jax.random.normal(key_of[9], (D,), jnp.float32), 0.1, 1.9),
        "up_weight": noise(key_of[10], (D, FF), D ** -0.5, 0.25),
        "down_weight": noise(key_of[11], (FF, D), (FF // 2) ** -0.5, 0.1875),
        "memory_gain": jnp.clip(1.0 + 0.18 * jax.random.normal(key_of[12], (D,), jnp.float32), 0.1, 1.9),
        "slot_query_weight": noise(key_of[13], (D, D), D ** -0.5, 0.25),
        "gate_weight": noise(key_of[14], (D, D), (max(1, D * 4 // STREAM)) ** -0.5, 6.0),
        "gate_bias": jnp.clip(jax.random.uniform(key_of[15], (D,), jnp.float32, -2.0, 2.0), -2.0, 2.0),
        "write_weight": noise(key_of[16], (D, D), (max(1, D * 4 // STREAM)) ** -0.5, 6.0),
        "out_cotangent": noise(key_of[17], (TOKENS, D), 1.0, 6.0, ((0, 32),)),
        "memory_cotangent": noise(key_of[18], (STREAMS, MEM, D), 1.0, 6.0, ((0, 8), (1, 4))),
    }


@jax.custom_vjp
def lower_precision(v):
    return lax.optimization_barrier(v.astype(jnp.bfloat16)).astype(jnp.float32)

@jax.custom_vjp
def reduced_backward(v):
    return v

def low_keep(v):
    return (lower_precision(v), None)

def low_pass(kept, grad):
    return (grad,)

def back_keep(v):
    return (v, None)

def back_low(kept, grad):
    return (lower_precision(grad),)
lower_precision.defvjp(low_keep, low_pass)
reduced_backward.defvjp(back_keep, back_low)

def layer_norm(value, gain):
    center = value - lax.optimization_barrier(jnp.mean(value, -1, keepdims=True))
    return center * lax.rsqrt(lax.optimization_barrier(jnp.mean(center * center, -1, keepdims=True)) + 1e-05) * gain

def matmul(left, right):
    return jnp.dot(left, right, precision=lax.Precision.HIGHEST)

def split(matrix):
    return matrix.reshape(matrix.shape[:-1] + (H, DH))

def stream_layer(weights, tokens, memory, pad, document):
    first_gain, query_weight, key_weight, value_weight, out_weight, second_gain, up_weight, down_weight, memory_gain, slot_query_weight, gate_weight, gate_bias, write_weight = weights
    upper_precision = lax.Precision.HIGHEST
    score_scale = DH ** (-0.5)
    count = STREAM // SEG
    normed = lower_precision(layer_norm(tokens, first_gain))
    query_rows = lower_precision(reduced_backward(matmul(normed, query_weight)))
    keys = lower_precision(reduced_backward(matmul(normed, key_weight)))
    values = lower_precision(reduced_backward(matmul(normed, value_weight)))
    slot_normed = lower_precision(layer_norm(memory, memory_gain))
    slot_keys = lower_precision(reduced_backward(matmul(slot_normed, key_weight)))
    slot_values = lower_precision(reduced_backward(matmul(slot_normed, value_weight)))
    stored_memory_keys = split(slot_keys)
    stored_memory_values = split(slot_values)
    query_block_rows = split(query_rows).reshape(count, SEG, H, DH)
    block_keys = split(keys).reshape(count, SEG, H, DH)
    block_values = split(values).reshape(count, SEG, H, DH)
    slot_logit_scores = reduced_backward(jnp.einsum('ztxq,ixq->zxti', query_block_rows, stored_memory_keys, precision=upper_precision)) * score_scale
    token_scores = reduced_backward(jnp.einsum('nshd,nthd->nhst', query_block_rows, block_keys, precision=upper_precision)) * score_scale
    block_document = document.reshape(count, SEG)
    block_pad = pad.reshape(count, SEG)
    rows = lax.broadcasted_iota(jnp.int32, (SEG, SEG), 0)
    columns = lax.broadcasted_iota(jnp.int32, (SEG, SEG), 1)
    mask = (rows >= columns)[None] & (block_document[:, :, None] == block_document[:, None, :]) & (block_pad[:, None, :] > 0)
    token_scores = jnp.where(mask[:, None], token_scores, -1e+30)
    top = jnp.maximum(lax.optimization_barrier(jnp.max(slot_logit_scores, -1, keepdims=True)), lax.optimization_barrier(jnp.max(token_scores, -1, keepdims=True)))
    slot_exponent_sum = jnp.exp(slot_logit_scores - top)
    token_power = jnp.exp(token_scores - top)
    grand_total = lax.optimization_barrier(jnp.sum(slot_exponent_sum, -1, keepdims=True)) + lax.optimization_barrier(jnp.sum(token_power, -1, keepdims=True))
    blended_output = jnp.einsum('gtfz,ztp->gftp', lower_precision(slot_exponent_sum / grand_total), stored_memory_values, precision=upper_precision)
    blended_output = blended_output + jnp.einsum('nhst,nthd->nshd', lower_precision(token_power / grand_total), block_values, precision=upper_precision)
    blended_output = lower_precision(reduced_backward(blended_output.reshape(STREAM, H * DH)))
    residual = tokens + reduced_backward(matmul(blended_output, out_weight))
    second = lower_precision(layer_norm(residual, second_gain))
    up_input = reduced_backward(matmul(second, up_weight))
    active = lower_precision(jax.nn.gelu(up_input, approximate=False))
    layer_out = residual + matmul(active, down_weight)
    slot_query_rows = split(lower_precision(reduced_backward(matmul(slot_normed, slot_query_weight))))
    self_scores = reduced_backward(lax.optimization_barrier(jnp.sum(slot_query_rows * stored_memory_keys, -1))) * score_scale
    key_head_count = split(keys)
    value_head_count = split(values)
    writer_logit_scores = reduced_backward(jnp.einsum('unb,lnb->unl', slot_query_rows, key_head_count, precision=upper_precision)) * score_scale
    writer_logit_scores = jnp.where(pad[None, None, :] > 0, writer_logit_scores, -1e+30)
    peak = jnp.maximum(self_scores, lax.optimization_barrier(jnp.max(writer_logit_scores, -1)))
    self_power = jnp.exp(self_scores - peak)
    writer_exponent_sum = jnp.exp(writer_logit_scores - peak[..., None])
    write_total = self_power + lax.optimization_barrier(jnp.sum(writer_exponent_sum, -1))
    weighted_values = lower_precision(self_power)[..., None] * stored_memory_values
    weighted_values = weighted_values + jnp.einsum('izq,qzc->izc', lower_precision(writer_exponent_sum), value_head_count, precision=upper_precision)
    update = lower_precision(reduced_backward((weighted_values / write_total[..., None]).reshape(MEM, H * DH)))
    gate = jax.nn.sigmoid(reduced_backward(matmul(update, gate_weight)) + gate_bias)
    written = reduced_backward(matmul(update, write_weight))
    new_memory = (1.0 - gate) * memory + gate * written
    return (layer_out, new_memory)

def reference(tokens, memory, pad_mask, doc_lengths, first_gain, query_weight, key_weight, value_weight, out_weight, second_gain, up_weight, down_weight, memory_gain, slot_query_weight, gate_weight, gate_bias, write_weight, out_cotangent, memory_cotangent):
    ends = jnp.cumsum(doc_lengths)
    places = jnp.arange(TOKENS, dtype=jnp.int32)
    document = lax.optimization_barrier(jnp.sum((places[:, None] >= ends[None, :]).astype(jnp.int32), 1))
    weights = tuple((value.astype(jnp.float32) for value in (first_gain, query_weight, key_weight, value_weight, out_weight, second_gain, up_weight, down_weight, memory_gain, slot_query_weight, gate_weight, gate_bias, write_weight)))

    def forward(inputs, state, *params):

        def one(item):
            return stream_layer(params, item[0], item[1], item[2], item[3])
        outs, fresh = lax.map(jax.checkpoint(one), (inputs.reshape(N_DP, STREAM, D), state, pad_mask.reshape(N_DP, STREAM), document.reshape(N_DP, STREAM)))
        return (outs.reshape(TOKENS, D), fresh)
    (layer_out, new_memory), pull = jax.vjp(forward, tokens.astype(jnp.float32), memory.astype(jnp.float32), *weights)
    grads = pull((out_cotangent.astype(jnp.float32), memory_cotangent.astype(jnp.float32)))
    return (layer_out.astype(jnp.bfloat16), new_memory, grads[0], grads[1], grads[2], grads[3], grads[4], grads[5], grads[6], grads[7], grads[8], grads[9], grads[10], grads[11], grads[12], grads[13], grads[14])
```

```python
import jax
import jax.numpy as jnp
from jax import lax
from jax.experimental import pallas as pl
from jax.experimental.pallas import tpu as pltpu
from jax.sharding import PartitionSpec as P

H = 8
DH = 64
SEG = 512
HALF = 256
FILL = -1e30
EPS = 1e-05
SCALE = DH ** (-0.5)
F32 = jnp.float32
BF16 = jnp.bfloat16

TAIL = (
    0.11962928145668905,
    0.12075423000729175,
    0.09991172819365436,
    0.12856765411993218,
    -0.053695489964182386,
    0.20636694099934239,
    -0.15721125090545032,
    0.035676834162404004,
)


def nn(a, b, precision=None):
    return lax.dot_general(
        a, b, (((1,), (0,)), ((), ())), preferred_element_type=F32, precision=precision
    )


def nt(a, b):
    return lax.dot_general(a, b, (((1,), (1,)), ((), ())), preferred_element_type=F32)


def norm(value):
    center = value - jnp.mean(value, -1, keepdims=True)
    inverse = lax.rsqrt(jnp.mean(center * center, -1, keepdims=True) + EPS)
    return center * inverse, inverse


def norm_back(grad, unit, inverse, gain):
    inner = grad * gain
    value_grad = inverse * (
        inner
        - jnp.mean(inner, -1, keepdims=True)
        - unit * jnp.mean(inner * unit, -1, keepdims=True)
    )
    return value_grad, jnp.sum(grad * unit, 0, keepdims=True)


def gelu_pair(x):
    t = 1.0 / (1.0 + 0.3 * jnp.abs(x))
    poly = TAIL[7]
    for c in TAIL[6::-1]:
        poly = poly * t + c
    bell = jnp.exp(-0.5 * (x * x))
    tail = bell * (poly * t)
    cdf = jnp.where(x >= 0, 1.0 - tail, tail)
    return x * cdf, cdf + x * (bell * 0.3989422804014327)


def segment_bias(doc_row, pad_row):
    code = jnp.where(pad_row > 0, doc_row, -1.0)
    key_code = jnp.transpose(jnp.broadcast_to(code, (SEG, SEG)))
    rows = lax.broadcasted_iota(jnp.int32, (SEG, SEG), 0)
    columns = lax.broadcasted_iota(jnp.int32, (SEG, SEG), 1)
    seen = (rows <= columns) & (key_code == doc_row)
    return jnp.where(seen, 0.0, FILL)


def head_rows(pair, odd):
    zero = jnp.zeros((DH, pair.shape[1]), pair.dtype)
    if odd:
        return jnp.concatenate([zero, pair[DH:]], 0)
    return jnp.concatenate([pair[:DH], zero], 0)


def head_lanes(pair, odd):
    lane = lax.broadcasted_iota(jnp.int32, pair.shape, 1)
    keep = (lane >= DH) if odd else (lane < DH)
    return jnp.where(keep, pair, jnp.zeros_like(pair))


def two(p):
    return slice(p * 2 * DH, (p + 1) * 2 * DH)


def one(h):
    return slice(h * DH, (h + 1) * DH)


BLOCKS = ((0, HALF), (HALF, SEG))


def project_kernel(x, gain, wq, wk, wv, q_t, k, k_t, v, v_t):
    unit, _ = norm(x[...].astype(F32))
    low = (unit * gain[...]).astype(BF16)
    q_t[...] = jnp.transpose((nn(low, wq[...]) * SCALE).astype(BF16))
    key = nn(low, wk[...]).astype(BF16)
    k[...] = key
    k_t[...] = jnp.transpose(key)
    value = nn(low, wv[...]).astype(BF16)
    v[...] = value
    v_t[...] = jnp.transpose(value)


def writer_kernel(
    mem, gain, wk, wv, wsq, k_t, v, pad,
    slot_k, slot_k_t, slot_v, slot_v_t, slot_q, slot_q_t, stats,
):
    unit, _ = norm(mem[...].astype(F32))
    low = (unit * gain[...]).astype(BF16)
    sk = nn(low, wk[...]).astype(BF16)
    sv = nn(low, wv[...]).astype(BF16)
    sq = (nn(low, wsq[...]) * SCALE).astype(BF16)
    slot_k[...] = sk
    slot_k_t[...] = jnp.transpose(sk)
    slot_v[...] = sv
    slot_v_t[...] = jnp.transpose(sv)
    slot_q[...] = sq
    slot_q_t[...] = jnp.transpose(sq)
    bias = jnp.where(pad[...] > 0, 0.0, FILL)
    slots = mem.shape[0]
    lane = lax.broadcasted_iota(jnp.int32, (slots, 2 * DH), 1) < DH
    for p in range(H // 2):
        parts = []
        for odd in range(2):
            c = nn(head_lanes(sq[:, two(p)], odd), k_t[two(p), :]) + bias
            top = jnp.max(c, 1, keepdims=True)
            w = jnp.exp(c - top)
            parts.append((nn(w.astype(BF16), v[:, two(p)]), top, jnp.sum(w, 1, keepdims=True)))
        for n in range(3):
            stats[n, :, two(p)] = jnp.where(lane, parts[0][n], parts[1][n])


def middle_kernel(
    x, q_t, k, v_t, doc, pad, slot_k, slot_v_t, wo, gain, wup, wdown, cot,
    out, res_grad, d_t, lse, inner, dwo_out, dwup_out, dwdown_out, dgain_out,
    bias, o_t, dwo, dwup, dwdown_t, dgain,
):
    step = pl.program_id(0)

    @pl.when(step == 0)
    def _():
        dwo[...] = jnp.zeros_like(dwo)
        dwup[...] = jnp.zeros_like(dwup)
        dwdown_t[...] = jnp.zeros_like(dwdown_t)
        dgain[...] = jnp.zeros_like(dgain)

    bias[...] = segment_bias(doc[...], pad[...])
    for h in range(H):
        p, odd = h // 2, h % 2
        qm = head_rows(q_t[two(p), :], odd)
        for lo, hi in BLOCKS:
            qb = qm[:, lo:hi]
            s = nn(k[:hi, two(p)], qb) + bias[:hi, lo:hi]
            sm = nn(slot_k[:, two(p)], qb)
            top = jnp.maximum(jnp.max(s, 0, keepdims=True), jnp.max(sm, 0, keepdims=True))
            e = jnp.exp(s - top)
            em = jnp.exp(sm - top)
            total = jnp.sum(e, 0, keepdims=True) + jnp.sum(em, 0, keepdims=True)
            o = nn(v_t[one(h), :hi], e.astype(BF16)) + nn(slot_v_t[one(h), :], em.astype(BF16))
            o_t[one(h), lo:hi] = o / total
            lse[h : h + 1, lo:hi] = top + jnp.log(total)
    mixed_t = o_t[...].astype(BF16)
    residual = x[...].astype(F32) + nn(jnp.transpose(mixed_t), wo[...])
    unit, inverse = norm(residual)
    second = (unit * gain[...]).astype(BF16)
    second_t = jnp.transpose(second)
    cot_low = cot[...]
    cot_t = jnp.transpose(cot_low)
    total_out = residual
    grad = jnp.zeros_like(residual)
    width = SEG
    for c in range(wup.shape[1] // width):
        cs = slice(c * width, (c + 1) * width)
        act, slope = gelu_pair(nn(second, wup[:, cs]))
        act = act.astype(BF16)
        total_out = total_out + nn(act, wdown[cs, :])
        up_grad = (nt(cot_low, wdown[cs, :]) * slope).astype(BF16)
        dwdown_t[:, cs] += nn(cot_t, act)
        dwup[:, cs] += nn(second_t, up_grad)
        grad = grad + nt(up_grad, wup[:, cs])
    out[...] = total_out.astype(BF16)
    back, gain_part = norm_back(grad, unit, inverse, gain[...])
    dgain[...] += gain_part
    back = back + cot_low.astype(F32)
    res_grad[...] = back
    low = back.astype(BF16)
    dwo[...] += nn(mixed_t, low)
    d = nt(wo[...], low).astype(BF16)
    d_t[...] = d
    prod = d.astype(F32) * o_t[...]
    for h in range(H):
        inner[h : h + 1, :] = jnp.sum(prod[one(h), :], 0, keepdims=True)

    @pl.when(step == pl.num_programs(0) - 1)
    def _():
        dwo_out[...] = dwo[...].astype(BF16)
        dwup_out[...] = dwup[...].astype(BF16)
        dwdown_out[...] = jnp.transpose(dwdown_t[...].astype(BF16))
        dgain_out[...] = jnp.broadcast_to(dgain[...], dgain_out.shape).astype(BF16)


def update_kernel(
    place, stats, mem, cot, slot_q, slot_k, slot_v, wgate, bgate, wwrite,
    new_memory, g_out, g_t, lse, inner_out, self_q_t, self_k_t, self_v_t, direct_out,
    dwgate, dwwrite, dbias, fresh,
):
    slots, width = mem.shape
    rows = new_memory.shape[0]
    same = (
        lax.broadcasted_iota(jnp.int32, (width, width), 0) // DH
        == lax.broadcasted_iota(jnp.int32, (width, width), 1) // DH
    ).astype(F32)
    def head_sum(value):
        return nn(value, same, lax.Precision.HIGHEST)
    start = place[0, 0] * rows
    row = lax.broadcasted_iota(jnp.int32, (slots, width), 0)
    own = (row >= start) & (row < start + rows)
    sq, sk, sv = (r[...].astype(F32) for r in (slot_q, slot_k, slot_v))
    state = mem[...].astype(F32)
    memory_out = cot[...].astype(F32)
    own_score = head_sum(sq * sk)
    count = stats.shape[0]
    top = own_score
    for n in range(count):
        top = jnp.maximum(top, stats[n, 1])
    power = jnp.exp(own_score - top)
    total = power
    weighted = power.astype(BF16).astype(F32) * sv
    for n in range(count):
        factor = jnp.exp(stats[n, 1] - top)
        total = total + factor * stats[n, 2]
        weighted = weighted + factor * stats[n, 0]
    update = weighted / total
    low = update.astype(BF16)
    gate = jax.nn.sigmoid(nn(low, wgate[...]) + bgate[...])
    written = nn(low, wwrite[...])
    fresh[...] = (1.0 - gate) * state + gate * written
    new_memory[...] = fresh[pl.ds(pl.multiple_of(start, rows), rows), :]
    gate_grad = memory_out * (written - state) * gate * (1.0 - gate)
    gate_low = gate_grad.astype(BF16)
    written_low = (memory_out * gate).astype(BF16)
    zero = jnp.zeros((slots, width), F32)
    direct_out[...] = jnp.where(own, memory_out * (1.0 - gate), zero)
    mine = jnp.where(own, gate_grad, zero)
    dbias[...] = jnp.broadcast_to(jnp.sum(mine, 0, keepdims=True), dbias.shape).astype(BF16)
    low_t = jnp.transpose(low)
    dwgate[...] = nn(low_t, mine.astype(BF16)).astype(BF16)
    dwwrite[...] = nn(low_t, jnp.where(own, memory_out * gate, zero).astype(BF16)).astype(BF16)
    g_low = (nt(gate_low, wgate[...]) + nt(written_low, wwrite[...])).astype(BF16)
    g = g_low.astype(F32)
    g_out[...] = g_low
    g_t[...] = jnp.transpose(g_low)
    inner = head_sum(g * update)
    inner_out[...] = inner
    lse[...] = top + jnp.log(total)
    delta = (power / total * (head_sum(g * sv) - inner)).astype(BF16).astype(F32)
    self_q_t[...] = jnp.transpose(jnp.where(own, delta * sk, zero))
    self_k_t[...] = jnp.transpose(jnp.where(own, delta * sq, zero))
    self_v_t[...] = jnp.transpose(
        jnp.where(own, power.astype(BF16).astype(F32) / total * g, zero)
    )


def last_kernel(
    x, gain, q_t, k, k_t, v, v_t, d_t, lse, inner, doc, pad, res_grad,
    slot_k, slot_k_t, slot_v, slot_q, slot_q_t, g, g_t, wlse, winner,
    self_q_t, self_k_t, self_v_t, direct, mem, mgain, wq, wk, wv, wsq,
    input_grad, dwq_out, dwk_out, dwv_out, dwsq_out, dgain_out, slot_part,
    bias, dq_t, dk_t, dv_t, dwq_t, dwk_t, dwv_t, sq_acc, sk_acc, sv_acc, dgain,
):
    step = pl.program_id(0)

    @pl.when(step == 0)
    def _():
        dwq_t[...] = jnp.zeros_like(dwq_t)
        dwk_t[...] = jnp.zeros_like(dwk_t)
        dwv_t[...] = jnp.zeros_like(dwv_t)
        dgain[...] = jnp.zeros_like(dgain)
        sq_acc[...] = self_q_t[...]
        sk_acc[...] = self_k_t[...]
        sv_acc[...] = self_v_t[...]

    bias[...] = segment_bias(doc[...], pad[...])
    pad_bias = jnp.where(pad[...] > 0, 0.0, FILL)
    for h in range(H):
        p, odd = h // 2, h % 2
        qm = head_rows(q_t[two(p), :], odd)
        dm = head_rows(d_t[two(p), :], odd)
        c = nn(head_lanes(slot_q[:, two(p)], odd), k_t[two(p), :]) + pad_bias
        share = jnp.exp(c - wlse[:, h * DH : h * DH + 1])
        dotted = nn(head_lanes(g[:, two(p)], odd), v_t[two(p), :])
        change = (share * (dotted - winner[:, h * DH : h * DH + 1])).astype(BF16)
        dk = nn(slot_q_t[one(h), :], change)
        dv = nn(g_t[one(h), :], share.astype(BF16))
        sq_acc[one(h), :] += nt(k_t[one(h), :], change)
        for lo, hi in BLOCKS:
            qb = qm[:, lo:hi]
            db = dm[:, lo:hi]
            qh = q_t[one(h), lo:hi]
            dh = d_t[one(h), lo:hi]
            l = lse[h : h + 1, lo:hi]
            i = inner[h : h + 1, lo:hi]
            e = jnp.exp(nn(k[:hi, two(p)], qb) + bias[:hi, lo:hi] - l)
            em = jnp.exp(nn(slot_k[:, two(p)], qb) - l)
            ds = (e * (nn(v[:hi, two(p)], db) - i)).astype(BF16)
            dsm = (em * (nn(slot_v[:, two(p)], db) - i)).astype(BF16)
            dq_t[one(h), lo:hi] = (
                (nn(k_t[one(h), :hi], ds) + nn(slot_k_t[one(h), :], dsm)) * SCALE
            ).astype(BF16)
            dvp = nt(dh, e.astype(BF16))
            dkp = nt(qh, ds)
            if hi < SEG:
                dvp = jnp.concatenate([dvp, jnp.zeros((DH, SEG - hi), F32)], 1)
                dkp = jnp.concatenate([dkp, jnp.zeros((DH, SEG - hi), F32)], 1)
            dv = dv + dvp
            dk = dk + dkp
            sv_acc[one(h), :] += nt(dh, em.astype(BF16))
            sk_acc[one(h), :] += nt(qh, dsm)
        dk_t[one(h), :] = dk.astype(BF16)
        dv_t[one(h), :] = dv.astype(BF16)
    unit, inverse = norm(x[...].astype(F32))
    low = (unit * gain[...]).astype(BF16)
    grad_t = nn(wq[...], dq_t[...]) + nn(wk[...], dk_t[...]) + nn(wv[...], dv_t[...])
    part, gain_part = norm_back(jnp.transpose(grad_t), unit, inverse, gain[...])
    dgain[...] += gain_part
    input_grad[...] = res_grad[...] + part
    dwq_t[...] += nn(dq_t[...], low)
    dwk_t[...] += nn(dk_t[...], low)
    dwv_t[...] += nn(dv_t[...], low)

    @pl.when(step == pl.num_programs(0) - 1)
    def _():
        unit, inverse = norm(mem[...].astype(F32))
        low = (unit * mgain[...]).astype(BF16)
        sq_low = (sq_acc[...] * SCALE).astype(BF16)
        sk_low = sk_acc[...].astype(BF16)
        sv_low = sv_acc[...].astype(BF16)
        dwq_out[...] = jnp.transpose(dwq_t[...]).astype(BF16)
        dwk_out[...] = jnp.transpose(dwk_t[...] + nn(sk_low, low)).astype(BF16)
        dwv_out[...] = jnp.transpose(dwv_t[...] + nn(sv_low, low)).astype(BF16)
        dwsq_out[...] = jnp.transpose(nn(sq_low, low)).astype(BF16)
        grad_t = nn(wk[...], sk_low) + nn(wv[...], sv_low) + nn(wsq[...], sq_low)
        part, gain_part = norm_back(jnp.transpose(grad_t), unit, inverse, mgain[...])
        slot_part[...] = part + direct[...]
        dgain_out[0:8, :] = jnp.broadcast_to(dgain[...], (8, dgain.shape[1]))
        dgain_out[8:16, :] = jnp.broadcast_to(gain_part, (8, dgain.shape[1]))


def struct(shape, dtype):
    return jax.ShapeDtypeStruct(shape, dtype)


def full(shape):
    return pl.BlockSpec(shape, lambda i: (0,) * len(shape))


def rows_of(width):
    return pl.BlockSpec((SEG, width), lambda i: (i, 0))


def lanes_of(height):
    return pl.BlockSpec((height, SEG), lambda i: (0, i))


PARAMS = pltpu.CompilerParams(dimension_semantics=("arbitrary",), vmem_limit_bytes=60 << 20)
PLAIN = pltpu.CompilerParams(vmem_limit_bytes=60 << 20)


def body(
    tokens,
    memory,
    pad_mask,
    doc_lengths,
    first_gain,
    query_weight,
    key_weight,
    value_weight,
    out_weight,
    second_gain,
    up_weight,
    down_weight,
    memory_gain,
    slot_query_weight,
    gate_weight,
    gate_bias,
    write_weight,
    out_cotangent,
    memory_cotangent,
):
    rows, width = tokens.shape
    hidden = up_weight.shape[1]
    count = rows // SEG
    slots_here = memory.shape[1]
    group = lax.axis_size("slot")
    slots = slots_here * group
    place = lax.axis_index("slot")
    begin = (lax.axis_index("dp") * group + place) * rows
    places = begin + jnp.arange(rows, dtype=jnp.int32)
    ends = jnp.cumsum(doc_lengths)
    document = jnp.sum((places[:, None] >= ends[None, :]).astype(jnp.int32), 1)
    doc = document.astype(F32)[None, :]
    pad = pad_mask.astype(F32)[None, :]
    gain1, gain2, gain3 = (g[None, :] for g in (first_gain, second_gain, memory_gain))

    both = lax.all_gather(
        jnp.concatenate([memory[0], memory_cotangent[0]], 1), "slot", axis=0, tiled=True
    )
    mem, mem_cot = both[:, :width], both[:, width:]

    square = (width, width)
    q_t, k, k_t, v, v_t = pl.pallas_call(
        project_kernel,
        grid=(count,),
        in_specs=[rows_of(width), full((1, width)), full(square), full(square), full(square)],
        out_specs=[lanes_of(width), rows_of(width), lanes_of(width), rows_of(width), lanes_of(width)],
        out_shape=[
            struct((width, rows), BF16), struct((rows, width), BF16), struct((width, rows), BF16),
            struct((rows, width), BF16), struct((width, rows), BF16),
        ],
        compiler_params=PARAMS,
        name="project",
    )(tokens, gain1, query_weight, key_weight, value_weight)

    tall, wide = (slots, width), (width, slots)
    slot_k, slot_k_t, slot_v, slot_v_t, slot_q, slot_q_t, stats = pl.pallas_call(
        writer_kernel,
        out_shape=[
            struct(tall, BF16), struct(wide, BF16), struct(tall, BF16), struct(wide, BF16),
            struct(tall, BF16), struct(wide, BF16), struct((3,) + tall, F32),
        ],
        compiler_params=PLAIN,
        name="writer",
    )(mem, gain3, key_weight, value_weight, slot_query_weight, k_t, v, pad)
    all_stats = lax.all_gather(stats, "slot", axis=0)

    layer_out, res_grad, d_t, lse, inner, dwo, dwup, dwdown, dgain2 = pl.pallas_call(
        middle_kernel,
        grid=(count,),
        in_specs=[
            rows_of(width), lanes_of(width), rows_of(width), lanes_of(width), lanes_of(1), lanes_of(1),
            full(tall), full(wide), full(square), full((1, width)), full((width, hidden)),
            full((hidden, width)), rows_of(width),
        ],
        out_specs=[
            rows_of(width), rows_of(width), lanes_of(width), lanes_of(H), lanes_of(H),
            full(square), full((width, hidden)), full((hidden, width)), full((16, width)),
        ],
        out_shape=[
            struct((rows, width), BF16), struct((rows, width), F32), struct((width, rows), BF16),
            struct((H, rows), F32), struct((H, rows), F32), struct(square, BF16),
            struct((width, hidden), BF16), struct((hidden, width), BF16), struct((16, width), BF16),
        ],
        scratch_shapes=[
            pltpu.VMEM((SEG, SEG), F32), pltpu.VMEM((width, SEG), F32), pltpu.VMEM(square, F32),
            pltpu.VMEM((width, hidden), F32), pltpu.VMEM((width, hidden), F32), pltpu.VMEM((1, width), F32),
        ],
        compiler_params=PARAMS,
        name="middle",
    )(
        tokens, q_t, k, v_t, doc, pad, slot_k, slot_v_t, out_weight, gain2, up_weight, down_weight,
        out_cotangent,
    )

    vm = pl.BlockSpec(memory_space=pltpu.VMEM)
    (
        new_memory, g, g_t, wlse, winner, self_q_t, self_k_t, self_v_t, direct, dwgate, dwwrite, dbias,
    ) = pl.pallas_call(
        update_kernel,
        in_specs=[pl.BlockSpec(memory_space=pltpu.SMEM)] + [vm] * 9,
        out_specs=[vm] * 12,
        out_shape=[
            struct((slots_here, width), F32), struct(tall, BF16), struct(wide, BF16), struct(tall, F32),
            struct(tall, F32), struct(wide, F32), struct(wide, F32), struct(wide, F32), struct(tall, F32),
            struct(square, BF16), struct(square, BF16), struct((16, width), BF16),
        ],
        scratch_shapes=[pltpu.VMEM(tall, F32)],
        compiler_params=PLAIN,
        name="update",
    )(
        place.astype(jnp.int32).reshape(1, 1), all_stats, mem, mem_cot, slot_q, slot_k, slot_v,
        gate_weight, gate_bias[None, :], write_weight,
    )

    axes = ("dp", "slot")
    dwo, dwup, dwdown, dwgate, dwwrite, dgain2, dbias = lax.psum(
        (dwo, dwup, dwdown, dwgate, dwwrite, dgain2, dbias), axes
    )

    input_grad, dwq, dwk, dwv, dwsq, dgains, slot_part = pl.pallas_call(
        last_kernel,
        grid=(count,),
        in_specs=[
            rows_of(width), full((1, width)), lanes_of(width), rows_of(width), lanes_of(width),
            rows_of(width), lanes_of(width), lanes_of(width), lanes_of(H), lanes_of(H), lanes_of(1),
            lanes_of(1), rows_of(width),
            full(tall), full(wide), full(tall), full(tall), full(wide), full(tall), full(wide),
            full(tall), full(tall), full(wide), full(wide), full(wide), full(tall), full(tall),
            full((1, width)), full(square), full(square), full(square), full(square),
        ],
        out_specs=[
            rows_of(width), full(square), full(square), full(square), full(square), full((16, width)),
            full(tall),
        ],
        out_shape=[
            struct((rows, width), F32), struct(square, BF16), struct(square, BF16), struct(square, BF16),
            struct(square, BF16), struct((16, width), F32), struct(tall, F32),
        ],
        scratch_shapes=[
            pltpu.VMEM((SEG, SEG), F32), pltpu.VMEM((width, SEG), BF16), pltpu.VMEM((width, SEG), BF16),
            pltpu.VMEM((width, SEG), BF16), pltpu.VMEM(square, F32), pltpu.VMEM(square, F32),
            pltpu.VMEM(square, F32), pltpu.VMEM(wide, F32), pltpu.VMEM(wide, F32), pltpu.VMEM(wide, F32),
            pltpu.VMEM((1, width), F32),
        ],
        compiler_params=PARAMS,
        name="last",
    )(
        tokens, gain1, q_t, k, k_t, v, v_t, d_t, lse, inner, doc, pad, res_grad,
        slot_k, slot_k_t, slot_v, slot_q, slot_q_t, g, g_t, wlse, winner,
        self_q_t, self_k_t, self_v_t, direct, mem, gain3,
        query_weight, key_weight, value_weight, slot_query_weight,
    )
    memory_grad = lax.psum_scatter(slot_part, "slot", scatter_dimension=0, tiled=True)[None]
    dwq, dwk, dwv, dwsq, dgains = lax.psum((dwq, dwk, dwv, dwsq, dgains.astype(BF16)), axes)

    return (
        layer_out,
        new_memory[None],
        input_grad,
        memory_grad,
        dgains[0].astype(F32),
        dwq.astype(F32),
        dwk.astype(F32),
        dwv.astype(F32),
        dwo.astype(F32),
        dgain2[0].astype(F32),
        dwup.astype(F32),
        dwdown.astype(F32),
        dgains[8].astype(F32),
        dwsq.astype(F32),
        dwgate.astype(F32),
        dbias[0].astype(F32),
        dwwrite.astype(F32),
    )


def solution(mesh):
    token = P(("dp", "slot"), None)
    slot = P("dp", "slot", None)
    in_specs = (
        (token, slot, P(("dp", "slot"))) + (P(),) * 14 + (token, slot)
    )
    out_specs = (token, slot, token, slot) + (P(),) * 13
    return jax.shard_map(body, mesh=mesh, in_specs=in_specs, out_specs=out_specs, check_vma=False)
```

```python
import jax
import jax.numpy as jnp
from jax import lax
from jax.experimental import pallas as pl
from jax.experimental.pallas import tpu as pltpu
from jax.sharding import PartitionSpec as P

H = 8
DH = 64
SEG = 512
HALF = 256
FILL = -1e30
EPS = 1e-05
SCALE = DH ** (-0.5)
F32 = jnp.float32
BF16 = jnp.bfloat16

TAIL = (
    0.11962928145668905,
    0.12075423000729175,
    0.09991172819365436,
    0.12856765411993218,
    -0.053695489964182386,
    0.20636694099934239,
    -0.15721125090545032,
    0.035676834162404004,
)


def nn(a, b, precision=None):
    return lax.dot_general(
        a, b, (((1,), (0,)), ((), ())), preferred_element_type=F32, precision=precision
    )


def nt(a, b):
    return lax.dot_general(a, b, (((1,), (1,)), ((), ())), preferred_element_type=F32)


def norm(value):
    center = value - jnp.mean(value, -1, keepdims=True)
    inverse = lax.rsqrt(jnp.mean(center * center, -1, keepdims=True) + EPS)
    return center * inverse, inverse


def norm_back(grad, unit, inverse, gain):
    inner = grad * gain
    value_grad = inverse * (
        inner
        - jnp.mean(inner, -1, keepdims=True)
        - unit * jnp.mean(inner * unit, -1, keepdims=True)
    )
    return value_grad, jnp.sum(grad * unit, 0, keepdims=True)


def gelu_pair(x):
    t = 1.0 / (1.0 + 0.3 * jnp.abs(x))
    poly = TAIL[7]
    for c in TAIL[6::-1]:
        poly = poly * t + c
    bell = jnp.exp(-0.5 * (x * x))
    tail = bell * (poly * t)
    cdf = jnp.where(x >= 0, 1.0 - tail, tail)
    return x * cdf, cdf + x * (bell * 0.3989422804014327)


def segment_bias(doc_row, pad_row):
    code = jnp.where(pad_row > 0, doc_row, -1.0)
    key_code = jnp.transpose(jnp.broadcast_to(code, (SEG, SEG)))
    rows = lax.broadcasted_iota(jnp.int32, (SEG, SEG), 0)
    columns = lax.broadcasted_iota(jnp.int32, (SEG, SEG), 1)
    seen = (rows <= columns) & (key_code == doc_row)
    return jnp.where(seen, 0.0, FILL)


def head_rows(pair, odd):
    zero = jnp.zeros((DH, pair.shape[1]), pair.dtype)
    if odd:
        return jnp.concatenate([zero, pair[DH:]], 0)
    return jnp.concatenate([pair[:DH], zero], 0)


def head_lanes(pair, odd):
    lane = lax.broadcasted_iota(jnp.int32, pair.shape, 1)
    keep = (lane >= DH) if odd else (lane < DH)
    return jnp.where(keep, pair, jnp.zeros_like(pair))


def two(p):
    return slice(p * 2 * DH, (p + 1) * 2 * DH)


def one(h):
    return slice(h * DH, (h + 1) * DH)


BLOCKS = ((0, HALF), (HALF, SEG))


def project_kernel(x, gain, wq, wk, wv, q_t, k, k_t, v, v_t):
    unit, _ = norm(x[...].astype(F32))
    low = (unit * gain[...]).astype(BF16)
    q_t[...] = jnp.transpose((nn(low, wq[...]) * SCALE).astype(BF16))
    key = nn(low, wk[...]).astype(BF16)
    k[...] = key
    k_t[...] = jnp.transpose(key)
    value = nn(low, wv[...]).astype(BF16)
    v[...] = value
    v_t[...] = jnp.transpose(value)


def writer_kernel(
    mem, gain, wk, wv, wsq, k_t, v, pad,
    slot_k, slot_k_t, slot_v, slot_v_t, slot_q, slot_q_t, stats,
):
    unit, _ = norm(mem[...].astype(F32))
    low = (unit * gain[...]).astype(BF16)
    sk = nn(low, wk[...]).astype(BF16)
    sv = nn(low, wv[...]).astype(BF16)
    sq = (nn(low, wsq[...]) * SCALE).astype(BF16)
    slot_k[...] = sk
    slot_k_t[...] = jnp.transpose(sk)
    slot_v[...] = sv
    slot_v_t[...] = jnp.transpose(sv)
    slot_q[...] = sq
    slot_q_t[...] = jnp.transpose(sq)
    bias = jnp.where(pad[...] > 0, 0.0, FILL)
    slots = mem.shape[0]
    lane = lax.broadcasted_iota(jnp.int32, (slots, 2 * DH), 1) < DH
    for p in range(H // 2):
        parts = []
        for odd in range(2):
            c = nn(head_lanes(sq[:, two(p)], odd), k_t[two(p), :]) + bias
            top = jnp.max(c, 1, keepdims=True)
            w = jnp.exp(c - top)
            parts.append((nn(w.astype(BF16), v[:, two(p)]), top, jnp.sum(w, 1, keepdims=True)))
        for n in range(3):
            stats[n, :, two(p)] = jnp.where(lane, parts[0][n], parts[1][n])


def middle_kernel(
    x, q_t, k, v_t, doc, pad, slot_k, slot_v_t, wo, gain, wup, wdown, cot,
    out, res_grad, d_t, lse, inner, dwo_out, dwup_out, dwdown_out, dgain_out,
    bias, o_t, dwo, dwup, dwdown_t, dgain,
):
    step = pl.program_id(0)

    @pl.when(step == 0)
    def _():
        dwo[...] = jnp.zeros_like(dwo)
        dwup[...] = jnp.zeros_like(dwup)
        dwdown_t[...] = jnp.zeros_like(dwdown_t)
        dgain[...] = jnp.zeros_like(dgain)

    bias[...] = segment_bias(doc[...], pad[...])
    for h in range(H):
        p, odd = h // 2, h % 2
        qm = head_rows(q_t[two(p), :], odd)
        for lo, hi in BLOCKS:
            qb = qm[:, lo:hi]
            s = nn(k[:hi, two(p)], qb) + bias[:hi, lo:hi]
            sm = nn(slot_k[:, two(p)], qb)
            top = jnp.maximum(jnp.max(s, 0, keepdims=True), jnp.max(sm, 0, keepdims=True))
            e = jnp.exp(s - top)
            em = jnp.exp(sm - top)
            total = jnp.sum(e, 0, keepdims=True) + jnp.sum(em, 0, keepdims=True)
            o = nn(v_t[one(h), :hi], e.astype(BF16)) + nn(slot_v_t[one(h), :], em.astype(BF16))
            o_t[one(h), lo:hi] = o / total
            lse[h : h + 1, lo:hi] = top + jnp.log(total)
    mixed_t = o_t[...].astype(BF16)
    residual = x[...].astype(F32) + nn(jnp.transpose(mixed_t), wo[...])
    unit, inverse = norm(residual)
    second = (unit * gain[...]).astype(BF16)
    second_t = jnp.transpose(second)
    cot_low = cot[...]
    cot_t = jnp.transpose(cot_low)
    total_out = residual
    grad = jnp.zeros_like(residual)
    width = SEG
    for c in range(wup.shape[1] // width):
        cs = slice(c * width, (c + 1) * width)
        act, slope = gelu_pair(nn(second, wup[:, cs]))
        act = act.astype(BF16)
        total_out = total_out + nn(act, wdown[cs, :])
        up_grad = (nt(cot_low, wdown[cs, :]) * slope).astype(BF16)
        dwdown_t[:, cs] += nn(cot_t, act)
        dwup[:, cs] += nn(second_t, up_grad)
        grad = grad + nt(up_grad, wup[:, cs])
    out[...] = total_out.astype(BF16)
    back, gain_part = norm_back(grad, unit, inverse, gain[...])
    dgain[...] += gain_part
    back = back + cot_low.astype(F32)
    res_grad[...] = back
    low = back.astype(BF16)
    dwo[...] += nn(mixed_t, low)
    d = nt(wo[...], low).astype(BF16)
    d_t[...] = d
    prod = d.astype(F32) * o_t[...]
    for h in range(H):
        inner[h : h + 1, :] = jnp.sum(prod[one(h), :], 0, keepdims=True)

    @pl.when(step == pl.num_programs(0) - 1)
    def _():
        dwo_out[...] = dwo[...].astype(BF16)
        for c in range(dwup_out.shape[0]):
            dwup_out[c] = dwup[:, c * SEG : (c + 1) * SEG].astype(BF16)
        dwdown_out[...] = jnp.transpose(dwdown_t[...].astype(BF16))
        dgain_out[...] = jnp.broadcast_to(dgain[...], dgain_out.shape).astype(BF16)


def update_kernel(
    place, stats, mem, cot, slot_q, slot_k, slot_v, wgate, bgate, wwrite,
    new_memory, g_out, g_t, lse, inner_out, self_q_t, self_k_t, self_v_t, direct_out,
    dwgate, dwwrite, dbias, fresh,
):
    slots, width = mem.shape
    rows = new_memory.shape[0]
    same = (
        lax.broadcasted_iota(jnp.int32, (width, width), 0) // DH
        == lax.broadcasted_iota(jnp.int32, (width, width), 1) // DH
    ).astype(F32)
    def head_sum(value):
        return nn(value, same, lax.Precision.HIGHEST)
    start = place[0, 0] * rows
    row = lax.broadcasted_iota(jnp.int32, (slots, width), 0)
    own = (row >= start) & (row < start + rows)
    sq, sk, sv = (r[...].astype(F32) for r in (slot_q, slot_k, slot_v))
    state = mem[...].astype(F32)
    memory_out = cot[...].astype(F32)
    own_score = head_sum(sq * sk)
    count = stats.shape[0]
    top = own_score
    for n in range(count):
        top = jnp.maximum(top, stats[n, 1])
    power = jnp.exp(own_score - top)
    total = power
    weighted = power.astype(BF16).astype(F32) * sv
    for n in range(count):
        factor = jnp.exp(stats[n, 1] - top)
        total = total + factor * stats[n, 2]
        weighted = weighted + factor * stats[n, 0]
    update = weighted / total
    low = update.astype(BF16)
    gate = jax.nn.sigmoid(nn(low, wgate[...]) + bgate[...])
    written = nn(low, wwrite[...])
    fresh[...] = (1.0 - gate) * state + gate * written
    new_memory[...] = fresh[pl.ds(pl.multiple_of(start, rows), rows), :]
    gate_grad = memory_out * (written - state) * gate * (1.0 - gate)
    gate_low = gate_grad.astype(BF16)
    written_low = (memory_out * gate).astype(BF16)
    zero = jnp.zeros((slots, width), F32)
    direct_out[...] = jnp.where(own, memory_out * (1.0 - gate), zero)
    mine = jnp.where(own, gate_grad, zero)
    dbias[...] = jnp.broadcast_to(jnp.sum(mine, 0, keepdims=True), dbias.shape).astype(BF16)
    low_t = jnp.transpose(low)
    dwgate[...] = nn(low_t, mine.astype(BF16)).astype(BF16)
    dwwrite[...] = nn(low_t, jnp.where(own, memory_out * gate, zero).astype(BF16)).astype(BF16)
    g_low = (nt(gate_low, wgate[...]) + nt(written_low, wwrite[...])).astype(BF16)
    g = g_low.astype(F32)
    g_out[...] = g_low
    g_t[...] = jnp.transpose(g_low)
    inner = head_sum(g * update)
    inner_out[...] = inner
    lse[...] = top + jnp.log(total)
    delta = (power / total * (head_sum(g * sv) - inner)).astype(BF16).astype(F32)
    self_q_t[...] = jnp.transpose(jnp.where(own, delta * sk, zero))
    self_k_t[...] = jnp.transpose(jnp.where(own, delta * sq, zero))
    self_v_t[...] = jnp.transpose(
        jnp.where(own, power.astype(BF16).astype(F32) / total * g, zero)
    )


def last_kernel(
    x, gain, q_t, k, k_t, v, v_t, d_t, lse, inner, doc, pad, res_grad,
    slot_k, slot_k_t, slot_v, slot_q, slot_q_t, g, g_t, wlse, winner,
    self_q_t, self_k_t, self_v_t, direct, mem, mgain, wq, wk, wv, wsq,
    input_grad, dwq_out, dwk_out, dwv_out, dwsq_out, dgain_out, slot_part,
    bias, dq_t, dk_t, dv_t, dwq_t, dwk_t, dwv_t, sq_acc, sk_acc, sv_acc, dgain,
):
    step = pl.program_id(0)

    @pl.when(step == 0)
    def _():
        dwq_t[...] = jnp.zeros_like(dwq_t)
        dwk_t[...] = jnp.zeros_like(dwk_t)
        dwv_t[...] = jnp.zeros_like(dwv_t)
        dgain[...] = jnp.zeros_like(dgain)
        sq_acc[...] = self_q_t[...]
        sk_acc[...] = self_k_t[...]
        sv_acc[...] = self_v_t[...]

    bias[...] = segment_bias(doc[...], pad[...])
    pad_bias = jnp.where(pad[...] > 0, 0.0, FILL)
    for h in range(H):
        p, odd = h // 2, h % 2
        qm = head_rows(q_t[two(p), :], odd)
        dm = head_rows(d_t[two(p), :], odd)
        c = nn(head_lanes(slot_q[:, two(p)], odd), k_t[two(p), :]) + pad_bias
        share = jnp.exp(c - wlse[:, h * DH : h * DH + 1])
        dotted = nn(head_lanes(g[:, two(p)], odd), v_t[two(p), :])
        change = (share * (dotted - winner[:, h * DH : h * DH + 1])).astype(BF16)
        dk = nn(slot_q_t[one(h), :], change)
        dv = nn(g_t[one(h), :], share.astype(BF16))
        sq_acc[one(h), :] += nt(k_t[one(h), :], change)
        for lo, hi in BLOCKS:
            qb = qm[:, lo:hi]
            db = dm[:, lo:hi]
            qh = q_t[one(h), lo:hi]
            dh = d_t[one(h), lo:hi]
            l = lse[h : h + 1, lo:hi]
            i = inner[h : h + 1, lo:hi]
            e = jnp.exp(nn(k[:hi, two(p)], qb) + bias[:hi, lo:hi] - l)
            em = jnp.exp(nn(slot_k[:, two(p)], qb) - l)
            ds = (e * (nn(v[:hi, two(p)], db) - i)).astype(BF16)
            dsm = (em * (nn(slot_v[:, two(p)], db) - i)).astype(BF16)
            dq_t[one(h), lo:hi] = (
                (nn(k_t[one(h), :hi], ds) + nn(slot_k_t[one(h), :], dsm)) * SCALE
            ).astype(BF16)
            dvp = nt(dh, e.astype(BF16))
            dkp = nt(qh, ds)
            if hi < SEG:
                dvp = jnp.concatenate([dvp, jnp.zeros((DH, SEG - hi), F32)], 1)
                dkp = jnp.concatenate([dkp, jnp.zeros((DH, SEG - hi), F32)], 1)
            dv = dv + dvp
            dk = dk + dkp
            sv_acc[one(h), :] += nt(dh, em.astype(BF16))
            sk_acc[one(h), :] += nt(qh, dsm)
        dk_t[one(h), :] = dk.astype(BF16)
        dv_t[one(h), :] = dv.astype(BF16)
    unit, inverse = norm(x[...].astype(F32))
    low = (unit * gain[...]).astype(BF16)
    grad_t = nn(wq[...], dq_t[...]) + nn(wk[...], dk_t[...]) + nn(wv[...], dv_t[...])
    part, gain_part = norm_back(jnp.transpose(grad_t), unit, inverse, gain[...])
    dgain[...] += gain_part
    input_grad[...] = res_grad[...] + part
    dwq_t[...] += nn(dq_t[...], low)
    dwk_t[...] += nn(dk_t[...], low)
    dwv_t[...] += nn(dv_t[...], low)

    @pl.when(step == pl.num_programs(0) - 1)
    def _():
        unit, inverse = norm(mem[...].astype(F32))
        low = (unit * mgain[...]).astype(BF16)
        sq_low = (sq_acc[...] * SCALE).astype(BF16)
        sk_low = sk_acc[...].astype(BF16)
        sv_low = sv_acc[...].astype(BF16)
        dwq_out[...] = jnp.transpose(dwq_t[...]).astype(BF16)
        dwk_out[...] = jnp.transpose(dwk_t[...] + nn(sk_low, low)).astype(BF16)
        dwv_out[...] = jnp.transpose(dwv_t[...] + nn(sv_low, low)).astype(BF16)
        dwsq_out[...] = jnp.transpose(nn(sq_low, low)).astype(BF16)
        grad_t = nn(wk[...], sk_low) + nn(wv[...], sv_low) + nn(wsq[...], sq_low)
        part, gain_part = norm_back(jnp.transpose(grad_t), unit, inverse, mgain[...])
        slot_part[...] = part + direct[...]
        dgain_out[0:8, :] = jnp.broadcast_to(dgain[...], (8, dgain.shape[1]))
        dgain_out[8:16, :] = jnp.broadcast_to(gain_part, (8, dgain.shape[1]))


def struct(shape, dtype):
    return jax.ShapeDtypeStruct(shape, dtype)


TILE = 16


def bit_orders(sizes):
    dp = [("dp", 1 << n) for n in range(sizes["dp"].bit_length() - 1)]
    slot = [("slot", 1 << n) for n in range(sizes["slot"].bit_length() - 1)]
    first, other = slot[:1], slot[1:]
    return first + other + dp, first + dp[:1] + other + dp[1:]


def plan(blocks, orders):
    half = blocks // 2
    steps, recv = [], 0
    for n, order in enumerate(orders):
        size, row = half, []
        for axis, stride in order:
            halves = size % 2 == 0
            sent = size // 2 if halves else size
            row.append((axis, stride, halves, sent, recv))
            recv += sent
            size = sent
        steps.append((n * half, half, row))
    return steps, recv


def receive_blocks(blocks, orders):
    return plan(blocks, orders)[1]


class Reduction:
    def __init__(self, buf, recv, sems, free, base, orders, index):
        self.buf, self.recv, self.sems, self.free = buf, recv, sems, free
        self.base, self.index = base, index
        self.steps, _ = plan(buf.shape[0], orders)
        self.depth = len(orders[0])
        self.stages = 2 * self.depth + 1
        self.state = [(start, size) for start, size, _ in self.steps]
        self.flying = []
        self.done = 0

    def partner(self, axis, stride):
        at = self.index[axis]
        bit = (at // stride) % 2
        peer = dict(self.index)
        peer[axis] = at + stride - 2 * bit * stride
        return bit, (peer["dp"], peer["slot"])

    def advance(self):
        stage = self.done
        if stage >= self.stages:
            return
        self.done += 1
        for copy, finish in self.flying:
            copy.wait()
            finish()
        self.flying = []
        if stage == self.stages - 1:
            return
        for n, (_, _, row) in enumerate(self.steps):
            down = stage < self.depth
            level = stage if down else 2 * self.depth - 1 - stage
            axis, stride, halves, sent, at = row[level]
            bit, peer = self.partner(axis, stride)
            start, size = self.state[n]
            slot = self.base + n * self.depth + level
            if down:
                keep = start + bit * sent if halves else start
                give = start + sent - bit * sent if halves else start
                copy = pltpu.make_async_remote_copy(
                    self.buf.at[pl.ds(give, sent)], self.recv.at[pl.ds(at, sent)],
                    self.sems.at[0, slot], self.sems.at[1, slot],
                    device_id=peer, device_id_type=pl.DeviceIdType.MESH,
                )
                self.flying.append((copy, self.adder(keep, sent, at, halves, slot, peer)))
                self.state[n] = (keep, sent)
            elif halves:
                pl.semaphore_wait(self.free.at[slot], 1)
                copy = pltpu.make_async_remote_copy(
                    self.buf.at[pl.ds(start, sent)], self.buf.at[pl.ds(start, sent)],
                    self.sems.at[2, slot], self.sems.at[3, slot],
                    device_id=peer, device_id_type=pl.DeviceIdType.MESH,
                )
                self.flying.append((copy, lambda: None))
                self.state[n] = (start - bit * sent, 2 * sent)
            else:
                continue
            copy.start()

    def adder(self, keep, sent, at, halves, slot, peer):
        def add():
            if halves:
                pl.semaphore_signal(
                    self.free.at[slot], inc=1, device_id=peer, device_id_type=pl.DeviceIdType.MESH
                )
            mine = self.buf[pl.ds(keep, sent)].astype(F32)
            self.buf[pl.ds(keep, sent)] = (mine + self.recv[pl.ds(at, sent)].astype(F32)).astype(BF16)

        return add


def greet(orders, index):
    barrier = pltpu.get_barrier_semaphore()
    for axis, stride in orders[0]:
        at = index[axis]
        bit = (at // stride) % 2
        peer = dict(index)
        peer[axis] = at + stride - 2 * bit * stride
        pl.semaphore_signal(
            barrier, inc=1, device_id=(peer["dp"], peer["slot"]), device_id_type=pl.DeviceIdType.MESH
        )
    pl.semaphore_wait(barrier, len(orders[0]))


def sum_kernel(orders, groups, lag, *refs):
    n_in = sum(len(g) for g in groups)
    ins, outs = refs[:n_in], refs[n_in : 2 * n_in]
    rest = refs[2 * n_in :]
    n = len(groups)
    bufs, recvs, (sems, free, loads, stores) = rest[:n], rest[n : 2 * n], rest[2 * n :]
    index = {"dp": lax.axis_index("dp"), "slot": lax.axis_index("slot")}
    pieces, at = [], 0
    for i, group in enumerate(groups):
        row = 0
        for blocks in group:
            pieces.append((i, row, blocks))
            row += blocks
    load = [
        pltpu.make_async_copy(ins[j], bufs[i].at[pl.ds(row, blocks)], loads.at[j])
        for j, (i, row, blocks) in enumerate(pieces)
    ]
    store = [
        pltpu.make_async_copy(bufs[i].at[pl.ds(row, blocks)], outs[j], stores.at[j])
        for j, (i, row, blocks) in enumerate(pieces)
    ]
    for copy in load:
        copy.start()
    greet(orders, index)
    depth = len(orders[0])
    work = [
        Reduction(bufs[i], recvs[i], sems, free, i * 2 * depth, orders, index) for i in range(n)
    ]
    for tick in range(lag * (n - 1) + work[0].stages):
        for i in range(n):
            stage = tick - lag * i
            if 0 <= stage < work[i].stages:
                if stage == 0:
                    for j, piece in enumerate(pieces):
                        if piece[0] == i:
                            load[j].wait()
                work[i].advance()
                if stage == work[i].stages - 1:
                    for j, piece in enumerate(pieces):
                        if piece[0] == i:
                            store[j].start()
    for copy in store:
        copy.wait()


def sum_all(groups, orders, lag, collective_id):
    width = groups[0][0].shape[1]
    flat = [a.reshape(a.shape[0] // TILE, TILE, width) for g in groups for a in g]
    blocks = [[a.shape[0] // TILE for a in g] for g in groups]
    sizes = [sum(b) for b in blocks]
    depth = len(orders[0])
    anywhere = pl.BlockSpec(memory_space=pl.ANY)
    outs = pl.pallas_call(
        lambda *refs: sum_kernel(orders, blocks, lag, *refs),
        in_specs=[anywhere] * len(flat),
        out_specs=[anywhere] * len(flat),
        out_shape=[struct(a.shape, BF16) for a in flat],
        scratch_shapes=[pltpu.VMEM((s, TILE, width), BF16) for s in sizes]
        + [pltpu.VMEM((receive_blocks(s, orders), TILE, width), BF16) for s in sizes]
        + [
            pltpu.SemaphoreType.DMA((4, len(groups) * 2 * depth)),
            pltpu.SemaphoreType.REGULAR((len(groups) * 2 * depth,)),
            pltpu.SemaphoreType.DMA((len(flat),)),
            pltpu.SemaphoreType.DMA((len(flat),)),
        ],
        compiler_params=pltpu.CompilerParams(
            vmem_limit_bytes=60 << 20, collective_id=collective_id, has_side_effects=True
        ),
        name="sum_all",
    )(*flat)
    outs = [o.reshape(-1, width) for o in outs]
    result, at = [], 0
    for g in groups:
        result.append(outs[at : at + len(g)])
        at += len(g)
    return result


def full(shape):
    return pl.BlockSpec(shape, lambda i: (0,) * len(shape))


def rows_of(width):
    return pl.BlockSpec((SEG, width), lambda i: (i, 0))


def lanes_of(height):
    return pl.BlockSpec((height, SEG), lambda i: (0, i))


PARAMS = pltpu.CompilerParams(dimension_semantics=("arbitrary",), vmem_limit_bytes=60 << 20)
PLAIN = pltpu.CompilerParams(vmem_limit_bytes=60 << 20)


def body(
    tokens,
    memory,
    pad_mask,
    doc_lengths,
    first_gain,
    query_weight,
    key_weight,
    value_weight,
    out_weight,
    second_gain,
    up_weight,
    down_weight,
    memory_gain,
    slot_query_weight,
    gate_weight,
    gate_bias,
    write_weight,
    out_cotangent,
    memory_cotangent,
):
    rows, width = tokens.shape
    hidden = up_weight.shape[1]
    count = rows // SEG
    slots_here = memory.shape[1]
    group = lax.axis_size("slot")
    slots = slots_here * group
    place = lax.axis_index("slot")
    begin = (lax.axis_index("dp") * group + place) * rows
    places = begin + jnp.arange(rows, dtype=jnp.int32)
    ends = jnp.cumsum(doc_lengths)
    document = jnp.sum((places[:, None] >= ends[None, :]).astype(jnp.int32), 1)
    doc = document.astype(F32)[None, :]
    pad = pad_mask.astype(F32)[None, :]
    gain1, gain2, gain3 = (g[None, :] for g in (first_gain, second_gain, memory_gain))

    both = lax.all_gather(
        jnp.concatenate([memory[0], memory_cotangent[0]], 1), "slot", axis=0, tiled=True
    )
    mem, mem_cot = both[:, :width], both[:, width:]

    square = (width, width)
    q_t, k, k_t, v, v_t = pl.pallas_call(
        project_kernel,
        grid=(count,),
        in_specs=[rows_of(width), full((1, width)), full(square), full(square), full(square)],
        out_specs=[lanes_of(width), rows_of(width), lanes_of(width), rows_of(width), lanes_of(width)],
        out_shape=[
            struct((width, rows), BF16), struct((rows, width), BF16), struct((width, rows), BF16),
            struct((rows, width), BF16), struct((width, rows), BF16),
        ],
        compiler_params=PARAMS,
        name="project",
    )(tokens, gain1, query_weight, key_weight, value_weight)

    tall, wide = (slots, width), (width, slots)
    slot_k, slot_k_t, slot_v, slot_v_t, slot_q, slot_q_t, stats = pl.pallas_call(
        writer_kernel,
        out_shape=[
            struct(tall, BF16), struct(wide, BF16), struct(tall, BF16), struct(wide, BF16),
            struct(tall, BF16), struct(wide, BF16), struct((3,) + tall, F32),
        ],
        compiler_params=PLAIN,
        name="writer",
    )(mem, gain3, key_weight, value_weight, slot_query_weight, k_t, v, pad)
    all_stats = lax.all_gather(stats, "slot", axis=0)

    layer_out, res_grad, d_t, lse, inner, dwo, dwup, dwdown, dgain2 = pl.pallas_call(
        middle_kernel,
        grid=(count,),
        in_specs=[
            rows_of(width), lanes_of(width), rows_of(width), lanes_of(width), lanes_of(1), lanes_of(1),
            full(tall), full(wide), full(square), full((1, width)), full((width, hidden)),
            full((hidden, width)), rows_of(width),
        ],
        out_specs=[
            rows_of(width), rows_of(width), lanes_of(width), lanes_of(H), lanes_of(H),
            full(square), full((hidden // SEG, width, SEG)), full((hidden, width)), full((16, width)),
        ],
        out_shape=[
            struct((rows, width), BF16), struct((rows, width), F32), struct((width, rows), BF16),
            struct((H, rows), F32), struct((H, rows), F32), struct(square, BF16),
            struct((hidden // SEG, width, SEG), BF16), struct((hidden, width), BF16), struct((16, width), BF16),
        ],
        scratch_shapes=[
            pltpu.VMEM((SEG, SEG), F32), pltpu.VMEM((width, SEG), F32), pltpu.VMEM(square, F32),
            pltpu.VMEM((width, hidden), F32), pltpu.VMEM((width, hidden), F32), pltpu.VMEM((1, width), F32),
        ],
        compiler_params=PARAMS,
        name="middle",
    )(
        tokens, q_t, k, v_t, doc, pad, slot_k, slot_v_t, out_weight, gain2, up_weight, down_weight,
        out_cotangent,
    )

    vm = pl.BlockSpec(memory_space=pltpu.VMEM)
    (
        new_memory, g, g_t, wlse, winner, self_q_t, self_k_t, self_v_t, direct, dwgate, dwwrite, dbias,
    ) = pl.pallas_call(
        update_kernel,
        in_specs=[pl.BlockSpec(memory_space=pltpu.SMEM)] + [vm] * 9,
        out_specs=[vm] * 12,
        out_shape=[
            struct((slots_here, width), F32), struct(tall, BF16), struct(wide, BF16), struct(tall, F32),
            struct(tall, F32), struct(wide, F32), struct(wide, F32), struct(wide, F32), struct(tall, F32),
            struct(square, BF16), struct(square, BF16), struct((16, width), BF16),
        ],
        scratch_shapes=[pltpu.VMEM(tall, F32)],
        compiler_params=PLAIN,
        name="update",
    )(
        place.astype(jnp.int32).reshape(1, 1), all_stats, mem, mem_cot, slot_q, slot_k, slot_v,
        gate_weight, gate_bias[None, :], write_weight,
    )

    input_grad, dwq, dwk, dwv, dwsq, dgains, slot_part = pl.pallas_call(
        last_kernel,
        grid=(count,),
        in_specs=[
            rows_of(width), full((1, width)), lanes_of(width), rows_of(width), lanes_of(width),
            rows_of(width), lanes_of(width), lanes_of(width), lanes_of(H), lanes_of(H), lanes_of(1),
            lanes_of(1), rows_of(width),
            full(tall), full(wide), full(tall), full(tall), full(wide), full(tall), full(wide),
            full(tall), full(tall), full(wide), full(wide), full(wide), full(tall), full(tall),
            full((1, width)), full(square), full(square), full(square), full(square),
        ],
        out_specs=[
            rows_of(width), full(square), full(square), full(square), full(square), full((16, width)),
            full(tall),
        ],
        out_shape=[
            struct((rows, width), F32), struct(square, BF16), struct(square, BF16), struct(square, BF16),
            struct(square, BF16), struct((16, width), F32), struct(tall, F32),
        ],
        scratch_shapes=[
            pltpu.VMEM((SEG, SEG), F32), pltpu.VMEM((width, SEG), BF16), pltpu.VMEM((width, SEG), BF16),
            pltpu.VMEM((width, SEG), BF16), pltpu.VMEM(square, F32), pltpu.VMEM(square, F32),
            pltpu.VMEM(square, F32), pltpu.VMEM(wide, F32), pltpu.VMEM(wide, F32), pltpu.VMEM(wide, F32),
            pltpu.VMEM((1, width), F32),
        ],
        compiler_params=PARAMS,
        name="last",
    )(
        tokens, gain1, q_t, k, k_t, v, v_t, d_t, lse, inner, doc, pad, res_grad,
        slot_k, slot_k_t, slot_v, slot_q, slot_q_t, g, g_t, wlse, winner,
        self_q_t, self_k_t, self_v_t, direct, mem, gain3,
        query_weight, key_weight, value_weight, slot_query_weight,
    )
    memory_grad = lax.psum_scatter(slot_part, "slot", scatter_dimension=0, tiled=True)[None]
    gains = jnp.concatenate([dgains.astype(BF16), dgain2[:8], dbias[:8]], 0)
    orders = bit_orders({"dp": lax.axis_size("dp"), "slot": group})
    parts = [
        [dwup[c], dwdown[c * width : (c + 1) * width]] for c in range(hidden // width)
    ]
    (*parts, (dwo, dwgate), (dwwrite, dwq), (dwk, dwv), (dwsq,), (gains,)) = sum_all(
        parts + [[dwo, dwgate], [dwwrite, dwq], [dwk, dwv], [dwsq], [gains]], orders, 1, 0
    )
    dwup = jnp.concatenate([p[0] for p in parts], 1)
    dwdown = jnp.concatenate([p[1] for p in parts], 0)

    return (
        layer_out,
        new_memory[None],
        input_grad,
        memory_grad,
        gains[0].astype(F32),
        dwq.astype(F32),
        dwk.astype(F32),
        dwv.astype(F32),
        dwo.astype(F32),
        gains[16].astype(F32),
        dwup.astype(F32),
        dwdown.astype(F32),
        gains[8].astype(F32),
        dwsq.astype(F32),
        dwgate.astype(F32),
        gains[24].astype(F32),
        dwwrite.astype(F32),
    )


def solution(mesh):
    token = P(("dp", "slot"), None)
    slot = P("dp", "slot", None)
    in_specs = (
        (token, slot, P(("dp", "slot"))) + (P(),) * 14 + (token, slot)
    )
    out_specs = (token, slot, token, slot) + (P(),) * 13
    return jax.shard_map(body, mesh=mesh, in_specs=in_specs, out_specs=out_specs, check_vma=False)
```

```python
import jax
import jax.numpy as jnp
from jax import lax
from jax.experimental import pallas as pl
from jax.experimental.pallas import tpu as pltpu
from jax.sharding import PartitionSpec as P

H = 8
DH = 64
SEG = 512
HALF = 256
FILL = -1e30
EPS = 1e-05
SCALE = DH ** (-0.5)
F32 = jnp.float32
BF16 = jnp.bfloat16

TAIL = (
    0.11962928145668905,
    0.12075423000729175,
    0.09991172819365436,
    0.12856765411993218,
    -0.053695489964182386,
    0.20636694099934239,
    -0.15721125090545032,
    0.035676834162404004,
)


def nn(a, b, precision=None):
    return lax.dot_general(
        a, b, (((1,), (0,)), ((), ())), preferred_element_type=F32, precision=precision
    )


def nt(a, b):
    return lax.dot_general(a, b, (((1,), (1,)), ((), ())), preferred_element_type=F32)


def norm(value):
    center = value - jnp.mean(value, -1, keepdims=True)
    inverse = lax.rsqrt(jnp.mean(center * center, -1, keepdims=True) + EPS)
    return center * inverse, inverse


def norm_back(grad, unit, inverse, gain):
    inner = grad * gain
    value_grad = inverse * (
        inner
        - jnp.mean(inner, -1, keepdims=True)
        - unit * jnp.mean(inner * unit, -1, keepdims=True)
    )
    return value_grad, jnp.sum(grad * unit, 0, keepdims=True)


def gelu_pair(x):
    t = 1.0 / (1.0 + 0.3 * jnp.abs(x))
    poly = TAIL[7]
    for c in TAIL[6::-1]:
        poly = poly * t + c
    bell = jnp.exp(-0.5 * (x * x))
    tail = bell * (poly * t)
    cdf = jnp.where(x >= 0, 1.0 - tail, tail)
    return x * cdf, cdf + x * (bell * 0.3989422804014327)


def segment_bias(doc_row, pad_row):
    code = jnp.where(pad_row > 0, doc_row, -1.0)
    key_code = jnp.transpose(jnp.broadcast_to(code, (SEG, SEG)))
    rows = lax.broadcasted_iota(jnp.int32, (SEG, SEG), 0)
    columns = lax.broadcasted_iota(jnp.int32, (SEG, SEG), 1)
    seen = (rows <= columns) & (key_code == doc_row)
    return jnp.where(seen, 0.0, FILL)


def head_rows(pair, odd):
    zero = jnp.zeros((DH, pair.shape[1]), pair.dtype)
    if odd:
        return jnp.concatenate([zero, pair[DH:]], 0)
    return jnp.concatenate([pair[:DH], zero], 0)


def head_lanes(pair, odd):
    lane = lax.broadcasted_iota(jnp.int32, pair.shape, 1)
    keep = (lane >= DH) if odd else (lane < DH)
    return jnp.where(keep, pair, jnp.zeros_like(pair))


def two(p):
    return slice(p * 2 * DH, (p + 1) * 2 * DH)


def one(h):
    return slice(h * DH, (h + 1) * DH)


BLOCKS = ((0, HALF), (HALF, SEG))


def project_kernel(x, gain, wq, wk, wv, normed, q_t, k, k_t, v, v_t):
    unit, _ = norm(x[...].astype(F32))
    low = (unit * gain[...]).astype(BF16)
    normed[...] = low
    q_t[...] = jnp.transpose((nn(low, wq[...]) * SCALE).astype(BF16))
    key = nn(low, wk[...]).astype(BF16)
    k[...] = key
    k_t[...] = jnp.transpose(key)
    value = nn(low, wv[...]).astype(BF16)
    v[...] = value
    v_t[...] = jnp.transpose(value)


def writer_kernel(
    mem, gain, wk, wv, wsq, k_t, v, pad,
    slot_k, slot_k_t, slot_v, slot_v_t, slot_q, slot_q_t, stats,
):
    unit, _ = norm(mem[...].astype(F32))
    low = (unit * gain[...]).astype(BF16)
    sk = nn(low, wk[...]).astype(BF16)
    sv = nn(low, wv[...]).astype(BF16)
    sq = (nn(low, wsq[...]) * SCALE).astype(BF16)
    slot_k[...] = sk
    slot_k_t[...] = jnp.transpose(sk)
    slot_v[...] = sv
    slot_v_t[...] = jnp.transpose(sv)
    slot_q[...] = sq
    slot_q_t[...] = jnp.transpose(sq)
    bias = jnp.where(pad[...] > 0, 0.0, FILL)
    slots = mem.shape[0]
    lane = lax.broadcasted_iota(jnp.int32, (slots, 2 * DH), 1) < DH
    for p in range(H // 2):
        parts = []
        for odd in range(2):
            c = nn(head_lanes(sq[:, two(p)], odd), k_t[two(p), :]) + bias
            top = jnp.max(c, 1, keepdims=True)
            w = jnp.exp(c - top)
            parts.append((nn(w.astype(BF16), v[:, two(p)]), top, jnp.sum(w, 1, keepdims=True)))
        for n in range(3):
            stats[n, :, two(p)] = jnp.where(lane, parts[0][n], parts[1][n])


TILE = 16
MESH = pl.DeviceIdType.MESH


def bit_orders(sizes):
    dp = [("dp", 1 << n) for n in range(sizes["dp"].bit_length() - 1)]
    slot = [("slot", 1 << n) for n in range(sizes["slot"].bit_length() - 1)]
    first, other = slot[:1], slot[1:]
    return first + other + dp, first + dp[:1] + other + dp[1:]


def plan(blocks, orders):
    half = blocks // 2
    steps, recv = [], 0
    for n, order in enumerate(orders):
        size, row = half, []
        for axis, stride in order:
            halves = size % 2 == 0
            sent = size // 2 if halves else size
            row.append((axis, stride, halves, sent, recv))
            recv += sent
            size = sent
        steps.append((n * half, row))
    return steps, recv


def here():
    return {"dp": lax.axis_index("dp"), "slot": lax.axis_index("slot")}


def across(index, axis, stride):
    bit = (index[axis] // stride) % 2
    peer = dict(index)
    peer[axis] = index[axis] + stride - 2 * bit * stride
    return bit, (peer["dp"], peer["slot"])


def greet(orders, index):
    barrier = pltpu.get_barrier_semaphore()
    for axis, stride in orders[0]:
        _, peer = across(index, axis, stride)
        pl.semaphore_signal(barrier, inc=1, device_id=peer, device_id_type=MESH)
    pl.semaphore_wait(barrier, len(orders[0]))


class Reduction:
    def __init__(self, buf, recv, sems, free, base, orders, index):
        self.buf, self.recv, self.sems, self.free = buf, recv, sems, free
        self.base, self.index = base, index
        self.steps, _ = plan(buf.shape[0], orders)
        self.depth = len(orders[0])
        up = [
            (level, False)
            for level in reversed(range(self.depth))
            if any(row[level][2] for _, row in self.steps)
        ]
        self.moves = [(level, True) for level in range(self.depth)] + up
        self.stages = len(self.moves) + 1

    def copies(self, move):
        level, down = self.moves[move]
        found = []
        for n, (start, row) in enumerate(self.steps):
            for axis, stride, halves, sent, _ in row[: level if down else level + 1]:
                if halves:
                    start = start + across(self.index, axis, stride)[0] * sent
            axis, stride, halves, sent, at = row[level]
            bit, peer = across(self.index, axis, stride)
            slot = self.base + n * self.depth + level
            if down:
                keep = start + bit * sent if halves else start
                give = start + sent - bit * sent if halves else start
                target, ends = self.recv.at[pl.ds(at, sent)], 0
            elif halves:
                keep, give = None, start
                target, ends = self.buf.at[pl.ds(give, sent)], 2
            else:
                continue
            copy = pltpu.make_async_remote_copy(
                self.buf.at[pl.ds(give, sent)], target,
                self.sems.at[ends, slot], self.sems.at[ends + 1, slot],
                device_id=peer, device_id_type=MESH,
            )
            found.append((copy, halves, keep, sent, at, slot, peer))
        return found

    def tick(self, stage):
        if stage > 0:
            down = self.moves[stage - 1][1]
            for copy, halves, keep, sent, at, slot, peer in self.copies(stage - 1):
                copy.wait()
                if not down:
                    continue
                if halves:
                    pl.semaphore_signal(
                        self.free.at[slot], inc=1, device_id=peer, device_id_type=MESH
                    )
                mine = self.buf[pl.ds(keep, sent)].astype(F32)
                self.buf[pl.ds(keep, sent)] = (
                    mine + self.recv[pl.ds(at, sent)].astype(F32)
                ).astype(BF16)
        if stage < len(self.moves):
            down = self.moves[stage][1]
            for copy, halves, keep, sent, at, slot, peer in self.copies(stage):
                if not down:
                    pl.semaphore_wait(self.free.at[slot], 1)
                copy.start()


def reduction_scratch(sizes, orders, width):
    depth = len(orders[0])
    return (
        [pltpu.VMEM((s, TILE, width), BF16) for s in sizes]
        + [pltpu.VMEM((plan(s, orders)[1], TILE, width), BF16) for s in sizes]
        + [
            pltpu.SemaphoreType.DMA((4, len(sizes) * 2 * depth)),
            pltpu.SemaphoreType.REGULAR((len(sizes) * 2 * depth,)),
        ]
    )


def reductions(refs, count, orders, index):
    bufs, recvs, (sems, free) = refs[:count], refs[count : 2 * count], refs[2 * count :]
    return [
        Reduction(bufs[n], recvs[n], sems, free, n * 2 * len(orders[0]), orders, index)
        for n in range(count)
    ]


def tiles(value):
    return value.reshape(value.shape[0] // TILE, TILE, value.shape[1])


EARLY = 2


def middle_kernel(
    count, chunks, orders,
    x, q_t, k, v_t, doc, pad, slot_k, slot_v_t, wo, gain, wup, wdown, cot,
    out, res_grad, d_t, lse, inner, dwo_out, late, dgain_out, *rest,
):
    sums, rest = rest[:EARLY], rest[EARLY:]
    bias, o_t, residual, second, second_t, cot_t, ffn, grad, dwo, dwup, dwdown_t, dgain = rest[:12]
    stores = rest[-1]
    step = pl.program_id(0)
    index = here()
    work = reductions(rest[12:-1], EARLY, orders, index)

    @pl.when(step == 0)
    def _():
        greet(orders, index)
        dwo[...] = jnp.zeros_like(dwo)
        dgain[...] = jnp.zeros_like(dgain)

    @pl.when(step < count)
    def _():
        bias[...] = segment_bias(doc[...], pad[...])
        for h in range(H):
            p, odd = h // 2, h % 2
            qm = head_rows(q_t[two(p), :], odd)
            for lo, hi in BLOCKS:
                qb = qm[:, lo:hi]
                s = nn(k[:hi, two(p)], qb) + bias[:hi, lo:hi]
                sm = nn(slot_k[:, two(p)], qb)
                top = jnp.maximum(jnp.max(s, 0, keepdims=True), jnp.max(sm, 0, keepdims=True))
                e = jnp.exp(s - top)
                em = jnp.exp(sm - top)
                total = jnp.sum(e, 0, keepdims=True) + jnp.sum(em, 0, keepdims=True)
                o = nn(v_t[one(h), :hi], e.astype(BF16)) + nn(slot_v_t[one(h), :], em.astype(BF16))
                o_t[step, one(h), lo:hi] = (o / total).astype(BF16)
                lse[p, odd : odd + 1, lo:hi] = top + jnp.log(total)
        res = x[...].astype(F32) + nn(jnp.transpose(o_t[step]), wo[...])
        residual[step] = res
        unit, _ = norm(res)
        low = (unit * gain[...]).astype(BF16)
        second[step] = low
        second_t[step] = jnp.transpose(low)
        cot_t[step] = jnp.transpose(cot[step])

    @pl.when((step >= count) & (step < count + chunks * count))
    def _():
        chunk = step // count - 1
        i = step % count
        act, slope = gelu_pair(nn(second[i], wup[...]))
        act = act.astype(BF16)
        plus = nn(act, wdown[...])
        up_grad = (nt(cot[i], wdown[...]) * slope).astype(BF16)
        back = nt(up_grad, wup[...])
        down_part = nn(cot_t[i], act)
        up_part = nn(second_t[i], up_grad)

        @pl.when(chunk == 0)
        def _():
            ffn[i] = plus
            grad[i] = back

        @pl.when(chunk > 0)
        def _():
            ffn[i] += plus
            grad[i] += back

        @pl.when(i == 0)
        def _():
            dwdown_t[...] = down_part
            dwup[...] = up_part

        @pl.when(i > 0)
        def _():
            dwdown_t[...] += down_part
            dwup[...] += up_part

        half = SEG // TILE
        for n in range(chunks):

            @pl.when((i == count - 1) & (chunk == n))
            def _():
                target = work[n].buf if n < EARLY else late.at[n - EARLY]
                target[:half] = tiles(dwup[...].astype(BF16))
                target[half:] = tiles(jnp.transpose(dwdown_t[...].astype(BF16)))

    @pl.when(step >= count + chunks * count)
    def _():
        i = step - count - chunks * count
        res = residual[i]
        unit, inverse = norm(res)
        out[...] = (res + ffn[i]).astype(BF16)
        back, gain_part = norm_back(grad[i], unit, inverse, gain[...])
        dgain[...] += gain_part
        back = back + cot[i].astype(F32)
        res_grad[...] = back
        low = back.astype(BF16)
        dwo[...] += nn(o_t[i], low)
        d = nt(wo[...], low).astype(BF16)
        d_t[...] = d
        prod = d.astype(F32) * o_t[i].astype(F32)
        for h in range(H):
            inner[h // 2, h % 2 : h % 2 + 1, :] = jnp.sum(prod[one(h), :], 0, keepdims=True)

        @pl.when(i == count - 1)
        def _():
            dwo_out[...] = dwo[...].astype(BF16)
            dgain_out[...] = jnp.broadcast_to(dgain[...], dgain_out.shape).astype(BF16)

    last = 2 * count + chunks * count - 1
    events = {}
    for n, item in enumerate(work):
        first = 2 * count - 1 + n * count
        for stage in range(item.stages):
            events.setdefault(min(first + stage, last), []).append((n, stage))
    for when, todo in sorted(events.items()):

        @pl.when(step == when)
        def _():
            for n, stage in todo:
                work[n].tick(stage)
                if stage == work[n].stages - 1:
                    pltpu.make_async_copy(work[n].buf, sums[n], stores.at[n]).start()

    @pl.when(step == last)
    def _():
        for n in range(EARLY):
            pltpu.make_async_copy(work[n].buf, sums[n], stores.at[n]).wait()


def update_kernel(
    place, stats, mem, cot, slot_q, slot_k, slot_v, wgate, bgate, wwrite,
    new_memory, g_out, g_t, lse, inner_out, self_q_t, self_k_t, self_v_t, direct_out,
    dwgate, dwwrite, dbias, fresh,
):
    slots, width = mem.shape
    rows = new_memory.shape[0]
    same = (
        lax.broadcasted_iota(jnp.int32, (width, width), 0) // DH
        == lax.broadcasted_iota(jnp.int32, (width, width), 1) // DH
    ).astype(F32)
    def head_sum(value):
        return nn(value, same, lax.Precision.HIGHEST)
    start = place[0, 0] * rows
    row = lax.broadcasted_iota(jnp.int32, (slots, width), 0)
    own = (row >= start) & (row < start + rows)
    sq, sk, sv = (r[...].astype(F32) for r in (slot_q, slot_k, slot_v))
    state = mem[...].astype(F32)
    memory_out = cot[...].astype(F32)
    own_score = head_sum(sq * sk)
    count = stats.shape[0]
    top = own_score
    for n in range(count):
        top = jnp.maximum(top, stats[n, 1])
    power = jnp.exp(own_score - top)
    total = power
    weighted = power.astype(BF16).astype(F32) * sv
    for n in range(count):
        factor = jnp.exp(stats[n, 1] - top)
        total = total + factor * stats[n, 2]
        weighted = weighted + factor * stats[n, 0]
    update = weighted / total
    low = update.astype(BF16)
    gate = jax.nn.sigmoid(nn(low, wgate[...]) + bgate[...])
    written = nn(low, wwrite[...])
    fresh[...] = (1.0 - gate) * state + gate * written
    new_memory[...] = fresh[pl.ds(pl.multiple_of(start, rows), rows), :]
    gate_grad = memory_out * (written - state) * gate * (1.0 - gate)
    gate_low = gate_grad.astype(BF16)
    written_low = (memory_out * gate).astype(BF16)
    zero = jnp.zeros((slots, width), F32)
    direct_out[...] = jnp.where(own, memory_out * (1.0 - gate), zero)
    mine = jnp.where(own, gate_grad, zero)
    dbias[...] = jnp.broadcast_to(jnp.sum(mine, 0, keepdims=True), dbias.shape).astype(BF16)
    low_t = jnp.transpose(low)
    dwgate[...] = nn(low_t, mine.astype(BF16)).astype(BF16)
    dwwrite[...] = nn(low_t, jnp.where(own, memory_out * gate, zero).astype(BF16)).astype(BF16)
    g_low = (nt(gate_low, wgate[...]) + nt(written_low, wwrite[...])).astype(BF16)
    g = g_low.astype(F32)
    g_out[...] = g_low
    g_t[...] = jnp.transpose(g_low)
    inner = head_sum(g * update)
    inner_out[...] = inner
    lse[...] = top + jnp.log(total)
    delta = (power / total * (head_sum(g * sv) - inner)).astype(BF16).astype(F32)
    self_q_t[...] = jnp.transpose(jnp.where(own, delta * sk, zero))
    self_k_t[...] = jnp.transpose(jnp.where(own, delta * sq, zero))
    self_v_t[...] = jnp.transpose(
        jnp.where(own, power.astype(BF16).astype(F32) / total * g, zero)
    )


def last_kernel(
    count, orders, sizes,
    x, gain, low, q_t, k, k_t, v, v_t, d_t, lse, inner, doc, pad, res_grad,
    slot_k, slot_k_t, slot_v, slot_q, slot_q_t, g, g_t, wlse, winner,
    self_q_t, self_k_t, self_v_t, direct, mem, mgain, wq, wk, wv, wsq, gains_in, *rest,
):
    early = len(sizes)
    ready, rest = rest[:early], rest[early:]
    input_grad, dwq_out, dwk_out, dwv_out, dwsq_out, gains_out, memory_grad = rest[:7]
    sums, rest = rest[7 : 7 + early], rest[7 + early :]
    bias, grads, acc, w_all, sq_acc, sk_acc, sv_acc, sq_all, sk_all, sv_all, slot_low, dgain = rest[:12]
    part, part_in, part_sems, loads, stores = rest[12:17]
    pairs = H // 2
    step = pl.program_id(0)
    index = here()
    work = reductions(rest[17:], early + pairs + 1, orders, index)
    wide = 2 * DH
    busy = step < pairs * count
    p = jnp.minimum(step // count, pairs - 1)
    i = step % count

    @pl.when(step == 0)
    def _():
        for n in range(early):
            pltpu.make_async_copy(ready[n], work[n].buf, loads.at[n]).start()
        greet(orders, index)
        for n in range(pairs):
            for m, w in enumerate((wq, wk, wv)):
                at = (3 * n + m) * wide
                w_all[:, at : at + wide] = w[:, two(n)]
        unit, _ = norm(mem[...].astype(F32))
        slot_low[...] = (unit * mgain[...]).astype(BF16)
        dgain[...] = jnp.zeros_like(dgain)

    @pl.when(busy)
    def _():
        @pl.when(i == 0)
        def _():
            sq_acc[...] = self_q_t[...]
            sk_acc[...] = self_k_t[...]
            sv_acc[...] = self_v_t[...]

        bias[...] = segment_bias(doc[...], pad[...])
        pad_bias = jnp.where(pad[...] > 0, 0.0, FILL)
        for odd in range(2):
            own = one(odd)
            qm = head_rows(q_t[...], odd)
            dm = head_rows(d_t[...], odd)
            c = nn(head_lanes(slot_q[...], odd), k_t[...]) + pad_bias
            share = jnp.exp(c - wlse[:, odd * DH : odd * DH + 1])
            dotted = nn(head_lanes(g[...], odd), v_t[...])
            change = (share * (dotted - winner[:, odd * DH : odd * DH + 1])).astype(BF16)
            dk = nn(slot_q_t[own, :], change)
            dv = nn(g_t[own, :], share.astype(BF16))
            sq_acc[own, :] += nt(k_t[own, :], change)
            for lo, hi in BLOCKS:
                qb = qm[:, lo:hi]
                db = dm[:, lo:hi]
                qh = q_t[own, lo:hi]
                dh = d_t[own, lo:hi]
                l = lse[0, odd : odd + 1, lo:hi]
                t = inner[0, odd : odd + 1, lo:hi]
                e = jnp.exp(nn(k[:hi, :], qb) + bias[:hi, lo:hi] - l)
                em = jnp.exp(nn(slot_k[...], qb) - l)
                ds = (e * (nn(v[:hi, :], db) - t)).astype(BF16)
                dsm = (em * (nn(slot_v[...], db) - t)).astype(BF16)
                dq = (nn(k_t[own, :hi], ds) + nn(slot_k_t[own, :], dsm)) * SCALE
                grads[i, p, own, lo:hi] = dq.astype(BF16)
                dvp = nt(dh, e.astype(BF16))
                dkp = nt(qh, ds)
                if hi < SEG:
                    dvp = jnp.concatenate([dvp, jnp.zeros((DH, SEG - hi), F32)], 1)
                    dkp = jnp.concatenate([dkp, jnp.zeros((DH, SEG - hi), F32)], 1)
                dv = dv + dvp
                dk = dk + dkp
                sv_acc[own, :] += nt(dh, em.astype(BF16))
                sk_acc[own, :] += nt(qh, dsm)
            grads[i, p, wide + odd * DH : wide + (odd + 1) * DH, :] = dk.astype(BF16)
            grads[i, p, 2 * wide + odd * DH : 2 * wide + (odd + 1) * DH, :] = dv.astype(BF16)
        more = nn(grads[i, p], low[...])

        @pl.when(i == 0)
        def _():
            acc[...] = more

        @pl.when(i > 0)
        def _():
            acc[...] += more

        @pl.when(i == count - 1)
        def _():
            sq_all[p] = (sq_acc[...] * SCALE).astype(BF16)
            sk_all[p] = sk_acc[...].astype(BF16)
            sv_all[p] = sv_acc[...].astype(BF16)
            rows = jnp.concatenate(
                [
                    acc[:wide],
                    acc[wide : 2 * wide] + nn(sk_all[p], slot_low[...]),
                    acc[2 * wide :] + nn(sv_all[p], slot_low[...]),
                    nn(sq_all[p], slot_low[...]),
                ],
                0,
            )
            rows = tiles(rows.astype(BF16))
            for n in range(pairs):

                @pl.when(p == n)
                def _():
                    work[early + n].buf[...] = rows

    @pl.when(step >= pairs * count)
    def _():
        unit, inverse = norm(x[...].astype(F32))
        grad_t = nn(w_all[...], grads[i].reshape(3 * pairs * wide, SEG))
        back, gain_part = norm_back(jnp.transpose(grad_t), unit, inverse, gain[...])
        dgain[...] += gain_part
        input_grad[...] = res_grad[...] + back

    group = part.shape[0]
    strides = [1 << n for n in reversed(range(group.bit_length() - 1))]

    def scatter(level):
        stride = strides[level]
        start, at = 0, 0
        for s in strides[:level]:
            start = start + across(index, "slot", s)[0] * s
            at += s
        bit, peer = across(index, "slot", stride)
        copy = pltpu.make_async_remote_copy(
            part.at[pl.ds(start + stride - bit * stride, stride)], part_in.at[pl.ds(at, stride)],
            part_sems.at[0, level], part_sems.at[1, level], device_id=peer, device_id_type=MESH,
        )
        return copy, start + bit * stride, at, stride

    def slots(stage):
        if stage == 0:
            unit, inverse = norm(mem[...].astype(F32))
            rows = mem.shape[1]
            sq, sk, sv = (a[...].reshape(rows, mem.shape[0]) for a in (sq_all, sk_all, sv_all))
            grad_t = nn(wk[...], sk) + nn(wv[...], sv) + nn(wsq[...], sq)
            back, gain_part = norm_back(jnp.transpose(grad_t), unit, inverse, mgain[...])
            part[...] = (back + direct[...]).reshape(part.shape)
            gains_out[0:8, :] = jnp.broadcast_to(gain_part, (8, gain_part.shape[1]))
        else:
            copy, keep, at, size = scatter(stage - 1)
            copy.wait()
            part[pl.ds(keep, size)] += part_in[pl.ds(at, size)]
        if stage < len(strides):
            scatter(stage)[0].start()
        else:
            memory_grad[...] = part[index["slot"]]

    def gains(stage):
        item = work[early + pairs]
        if stage == 0:
            buf = item.buf
            eight = jnp.broadcast_to(dgain[...], (8, dgain.shape[1]))
            buf[0] = jnp.concatenate([eight, gains_out[0:8, :]], 0).astype(BF16)
            buf[1] = gains_in[...]
        item.tick(stage)
        if stage == item.stages - 1:
            gains_out[...] = item.buf[...].reshape(gains_out.shape).astype(F32)

    def summed(n, stage):
        item = work[n]
        if n < early and stage == 0:
            pltpu.make_async_copy(ready[n], item.buf, loads.at[n]).wait()
        item.tick(stage)
        if stage < item.stages - 1:
            return
        if n < early:
            pltpu.make_async_copy(item.buf, sums[n], stores.at[n]).start()
            return
        per = wide // TILE
        for m, out in enumerate((dwq_out, dwk_out, dwv_out, dwsq_out)):
            block = item.buf[m * per : (m + 1) * per].reshape(wide, out.shape[0])
            out[:, two(n - early)] = jnp.transpose(block)

    last = pairs * count + count - 1
    events = []
    for n in range(early):
        events += [(1 + n // 2 + stage, summed, (n, stage)) for stage in range(work[n].stages)]
    for n in range(pairs):
        events += [
            ((n + 1) * count - 1 + stage, summed, (early + n, stage))
            for stage in range(work[early + n].stages)
        ]
    events += [(pairs * count + stage, slots, (stage,)) for stage in range(len(strides) + 1)]
    events += [(last + stage, gains, (stage,)) for stage in range(work[early + pairs].stages)]
    events.sort(key=lambda event: event[0])
    for when in range(last + 1):
        todo = [e for e in events if e[0] == when or (when == last and e[0] > last)]
        if not todo:
            continue

        @pl.when(step == when)
        def _():
            for _, act, args in todo:
                act(*args)

    @pl.when(step == last)
    def _():
        for n in range(early):
            pltpu.make_async_copy(work[n].buf, sums[n], stores.at[n]).wait()


def struct(shape, dtype):
    return jax.ShapeDtypeStruct(shape, dtype)


def full(shape):
    return pl.BlockSpec(shape, lambda i: (0,) * len(shape))


def rows_of(width, at=lambda i: i):
    return pl.BlockSpec((SEG, width), lambda i: (at(i), 0))


def lanes_of(height, at=lambda i: i):
    return pl.BlockSpec((height, SEG), lambda i: (0, at(i)))


def params(collective_id=None):
    grid = dict(dimension_semantics=("arbitrary",), vmem_limit_bytes=62 << 20)
    if collective_id is None:
        return pltpu.CompilerParams(**grid)
    return pltpu.CompilerParams(collective_id=collective_id, has_side_effects=True, **grid)


PLAIN = pltpu.CompilerParams(vmem_limit_bytes=60 << 20)


def body(
    tokens,
    memory,
    pad_mask,
    doc_lengths,
    first_gain,
    query_weight,
    key_weight,
    value_weight,
    out_weight,
    second_gain,
    up_weight,
    down_weight,
    memory_gain,
    slot_query_weight,
    gate_weight,
    gate_bias,
    write_weight,
    out_cotangent,
    memory_cotangent,
):
    rows, width = tokens.shape
    hidden = up_weight.shape[1]
    count = rows // SEG
    slots_here = memory.shape[1]
    group = lax.axis_size("slot")
    slots = slots_here * group
    place = lax.axis_index("slot")
    begin = (lax.axis_index("dp") * group + place) * rows
    places = begin + jnp.arange(rows, dtype=jnp.int32)
    ends = jnp.cumsum(doc_lengths)
    document = jnp.sum((places[:, None] >= ends[None, :]).astype(jnp.int32), 1)
    doc = document.astype(F32)[None, :]
    pad = pad_mask.astype(F32)[None, :]
    gain1, gain2, gain3 = (g[None, :] for g in (first_gain, second_gain, memory_gain))

    both = lax.all_gather(
        jnp.concatenate([memory[0], memory_cotangent[0]], 1), "slot", axis=0, tiled=True
    )
    mem, mem_cot = both[:, :width], both[:, width:]

    square = (width, width)
    normed, q_t, k, k_t, v, v_t = pl.pallas_call(
        project_kernel,
        grid=(count,),
        in_specs=[rows_of(width), full((1, width)), full(square), full(square), full(square)],
        out_specs=[
            rows_of(width), lanes_of(width), rows_of(width), lanes_of(width), rows_of(width),
            lanes_of(width),
        ],
        out_shape=[
            struct((rows, width), BF16),
            struct((width, rows), BF16), struct((rows, width), BF16), struct((width, rows), BF16),
            struct((rows, width), BF16), struct((width, rows), BF16),
        ],
        compiler_params=params(),
        name="project",
    )(tokens, gain1, query_weight, key_weight, value_weight)

    tall, wide = (slots, width), (width, slots)
    slot_k, slot_k_t, slot_v, slot_v_t, slot_q, slot_q_t, stats = pl.pallas_call(
        writer_kernel,
        out_shape=[
            struct(tall, BF16), struct(wide, BF16), struct(tall, BF16), struct(wide, BF16),
            struct(tall, BF16), struct(wide, BF16), struct((3,) + tall, F32),
        ],
        compiler_params=PLAIN,
        name="writer",
    )(mem, gain3, key_weight, value_weight, slot_query_weight, k_t, v, pad)
    all_stats = lax.all_gather(stats, "slot", axis=0)

    axes = {"dp": lax.axis_size("dp"), "slot": group}
    orders = bit_orders(axes)
    chunks = hidden // SEG
    pairs = H // 2
    anywhere = pl.BlockSpec(memory_space=pl.ANY)
    begin_at = lambda i: jnp.minimum(i, count - 1)
    chunk_at = lambda i: jnp.clip(i // count - 1, 0, chunks - 1)
    end_at = lambda i: jnp.maximum(i - count - chunks * count, 0)
    blocks = 2 * SEG // TILE
    layer_out, res_grad, d_t, lse, inner, dwo, late, dgain2, *early = pl.pallas_call(
        lambda *refs: middle_kernel(count, chunks, orders, *refs),
        grid=(2 * count + chunks * count,),
        in_specs=[
            rows_of(width, begin_at), lanes_of(width, begin_at), rows_of(width, begin_at),
            lanes_of(width, begin_at), lanes_of(1, begin_at), lanes_of(1, begin_at),
            full(tall), full(wide), full(square), full((1, width)),
            pl.BlockSpec((width, SEG), lambda i: (0, chunk_at(i))),
            pl.BlockSpec((SEG, width), lambda i: (chunk_at(i), 0)),
            full((count, SEG, width)),
        ],
        out_specs=[
            rows_of(width, end_at), rows_of(width, end_at), lanes_of(width, end_at),
            pl.BlockSpec((pairs, 2, SEG), lambda i: (0, 0, begin_at(i))),
            pl.BlockSpec((pairs, 2, SEG), lambda i: (0, 0, end_at(i))),
            full(square), full((chunks - EARLY, blocks, TILE, width)), full((16, width)),
        ]
        + [anywhere] * EARLY,
        out_shape=[
            struct((rows, width), BF16), struct((rows, width), F32), struct((width, rows), BF16),
            struct((pairs, 2, rows), F32), struct((pairs, 2, rows), F32), struct(square, BF16),
            struct((chunks - EARLY, blocks, TILE, width), BF16), struct((16, width), BF16),
        ]
        + [struct((blocks, TILE, width), BF16)] * EARLY,
        scratch_shapes=[
            pltpu.VMEM((SEG, SEG), F32), pltpu.VMEM((count, width, SEG), BF16),
            pltpu.VMEM((count, SEG, width), F32), pltpu.VMEM((count, SEG, width), BF16),
            pltpu.VMEM((count, width, SEG), BF16), pltpu.VMEM((count, width, SEG), BF16),
            pltpu.VMEM((count, SEG, width), F32), pltpu.VMEM((count, SEG, width), F32),
            pltpu.VMEM(square, F32), pltpu.VMEM((width, SEG), F32), pltpu.VMEM((width, SEG), F32),
            pltpu.VMEM((1, width), F32),
        ]
        + reduction_scratch([blocks] * EARLY, orders, width)
        + [pltpu.SemaphoreType.DMA((EARLY,))],
        compiler_params=params(0),
        name="middle",
    )(
        tokens, q_t, k, v_t, doc, pad, slot_k, slot_v_t, out_weight, gain2, up_weight, down_weight,
        out_cotangent.reshape(count, SEG, width),
    )

    vm = pl.BlockSpec(memory_space=pltpu.VMEM)
    (
        new_memory, g, g_t, wlse, winner, self_q_t, self_k_t, self_v_t, direct, dwgate, dwwrite, dbias,
    ) = pl.pallas_call(
        update_kernel,
        in_specs=[pl.BlockSpec(memory_space=pltpu.SMEM)] + [vm] * 9,
        out_specs=[vm] * 12,
        out_shape=[
            struct((slots_here, width), F32), struct(tall, BF16), struct(wide, BF16), struct(tall, F32),
            struct(tall, F32), struct(wide, F32), struct(wide, F32), struct(wide, F32), struct(tall, F32),
            struct(square, BF16), struct(square, BF16), struct((16, width), BF16),
        ],
        scratch_shapes=[pltpu.VMEM(tall, F32)],
        compiler_params=PLAIN,
        name="update",
    )(
        place.astype(jnp.int32).reshape(1, 1), all_stats, mem, mem_cot, slot_q, slot_k, slot_v,
        gate_weight, gate_bias[None, :], write_weight,
    )

    ready = [late[n] for n in range(chunks - EARLY)] + [
        jnp.concatenate([tiles(dwo), tiles(dwgate), tiles(dwwrite)], 0)
    ]
    sizes = [r.shape[0] for r in ready]
    wide_pair = 2 * DH
    pair_at = lambda s: jnp.minimum(s // count, pairs - 1)
    seg_at = lambda s: s % count
    final_at = lambda s: jnp.maximum(s - pairs * count, 0)
    pair_rows = pl.BlockSpec((SEG, wide_pair), lambda s: (seg_at(s), pair_at(s)))
    pair_lanes = pl.BlockSpec((wide_pair, SEG), lambda s: (pair_at(s), seg_at(s)))
    pair_stat = pl.BlockSpec((1, 2, SEG), lambda s: (pair_at(s), 0, seg_at(s)))
    pair_tall = pl.BlockSpec((slots, wide_pair), lambda s: (0, pair_at(s)))
    pair_wide = pl.BlockSpec((wide_pair, slots), lambda s: (pair_at(s), 0))
    input_grad, dwq, dwk, dwv, dwsq, gains, memory_grad, *sums = pl.pallas_call(
        lambda *refs: last_kernel(count, orders, sizes, *refs),
        grid=(pairs * count + count,),
        in_specs=[
            rows_of(width, final_at), full((1, width)), rows_of(width, seg_at),
            pair_lanes, pair_rows, pair_lanes, pair_rows, pair_lanes, pair_lanes, pair_stat, pair_stat,
            lanes_of(1, seg_at), lanes_of(1, seg_at), rows_of(width, final_at),
            pair_tall, pair_wide, pair_tall, pair_tall, pair_wide, pair_tall, pair_wide,
            pair_tall, pair_tall, pair_wide, pair_wide, pair_wide, full(tall), full(tall),
            full((1, width)), full(square), full(square), full(square), full(square),
            full((16, width)),
        ]
        + [anywhere] * len(ready),
        out_specs=[
            rows_of(width, final_at), full(square), full(square), full(square), full(square),
            full((32, width)), full((slots_here, width)),
        ]
        + [anywhere] * len(ready),
        out_shape=[
            struct((rows, width), F32), struct(square, BF16), struct(square, BF16), struct(square, BF16),
            struct(square, BF16), struct((32, width), F32), struct((slots_here, width), F32),
        ]
        + [struct(r.shape, BF16) for r in ready],
        scratch_shapes=[
            pltpu.VMEM((SEG, SEG), F32), pltpu.VMEM((count, pairs, 3 * wide_pair, SEG), BF16),
            pltpu.VMEM((3 * wide_pair, width), F32), pltpu.VMEM((width, 3 * width), BF16),
            pltpu.VMEM((wide_pair, slots), F32), pltpu.VMEM((wide_pair, slots), F32),
            pltpu.VMEM((wide_pair, slots), F32), pltpu.VMEM((pairs, wide_pair, slots), BF16),
            pltpu.VMEM((pairs, wide_pair, slots), BF16), pltpu.VMEM((pairs, wide_pair, slots), BF16),
            pltpu.VMEM(tall, BF16), pltpu.VMEM((1, width), F32),
            pltpu.VMEM((group, slots_here, width), F32), pltpu.VMEM((group, slots_here, width), F32),
            pltpu.SemaphoreType.DMA((2, group)), pltpu.SemaphoreType.DMA((len(ready),)),
            pltpu.SemaphoreType.DMA((len(ready),)),
        ]
        + reduction_scratch(sizes + [4 * wide_pair // TILE] * pairs + [2], orders, width),
        compiler_params=params(1),
        name="last",
    )(
        tokens, gain1, normed, q_t, k, k_t, v, v_t, d_t, lse, inner, doc, pad, res_grad,
        slot_k, slot_k_t, slot_v, slot_q, slot_q_t, g, g_t, wlse, winner,
        self_q_t, self_k_t, self_v_t, direct, mem, gain3,
        query_weight, key_weight, value_weight, slot_query_weight,
        jnp.concatenate([dgain2[:8], dbias[:8]], 0), *ready,
    )
    half = SEG // TILE
    ffn = list(early) + list(sums[: chunks - EARLY])
    dwup = jnp.concatenate([f[:half].reshape(width, SEG) for f in ffn], 1)
    dwdown = jnp.concatenate([f[half:].reshape(SEG, width) for f in ffn], 0)
    dwo, dwgate, dwwrite = (
        sums[-1][n * width // TILE : (n + 1) * width // TILE].reshape(width, width) for n in range(3)
    )

    return (
        layer_out,
        new_memory[None],
        input_grad,
        memory_grad[None],
        gains[0],
        dwq.astype(F32),
        dwk.astype(F32),
        dwv.astype(F32),
        dwo.astype(F32),
        gains[16],
        dwup.astype(F32),
        dwdown.astype(F32),
        gains[8],
        dwsq.astype(F32),
        dwgate.astype(F32),
        gains[24],
        dwwrite.astype(F32),
    )


def solution(mesh):
    token = P(("dp", "slot"), None)
    slot = P("dp", "slot", None)
    in_specs = (
        (token, slot, P(("dp", "slot"))) + (P(),) * 14 + (token, slot)
    )
    out_specs = (token, slot, token, slot) + (P(),) * 13
    return jax.shard_map(body, mesh=mesh, in_specs=in_specs, out_specs=out_specs, check_vma=False)
```

```python
import jax
import jax.numpy as jnp
from jax import lax
from jax.experimental import pallas as pl
from jax.experimental.pallas import tpu as pltpu
from jax.sharding import PartitionSpec as P

H = 8
DH = 64
SEG = 512
HALF = 256
FILL = -1e30
EPS = 1e-05
SCALE = DH ** (-0.5)
F32 = jnp.float32
BF16 = jnp.bfloat16

TAIL = (
    0.11962928145668905,
    0.12075423000729175,
    0.09991172819365436,
    0.12856765411993218,
    -0.053695489964182386,
    0.20636694099934239,
    -0.15721125090545032,
    0.035676834162404004,
)


def nn(a, b, precision=None):
    return lax.dot_general(
        a, b, (((1,), (0,)), ((), ())), preferred_element_type=F32, precision=precision
    )


def nt(a, b):
    return lax.dot_general(a, b, (((1,), (1,)), ((), ())), preferred_element_type=F32)


def norm(value):
    center = value - jnp.mean(value, -1, keepdims=True)
    inverse = lax.rsqrt(jnp.mean(center * center, -1, keepdims=True) + EPS)
    return center * inverse, inverse


def norm_back(grad, unit, inverse, gain):
    inner = grad * gain
    value_grad = inverse * (
        inner
        - jnp.mean(inner, -1, keepdims=True)
        - unit * jnp.mean(inner * unit, -1, keepdims=True)
    )
    return value_grad, jnp.sum(grad * unit, 0, keepdims=True)


def gelu_pair(x):
    t = 1.0 / (1.0 + 0.3 * jnp.abs(x))
    poly = TAIL[7]
    for c in TAIL[6::-1]:
        poly = poly * t + c
    bell = jnp.exp(-0.5 * (x * x))
    tail = bell * (poly * t)
    cdf = jnp.where(x >= 0, 1.0 - tail, tail)
    return x * cdf, cdf + x * (bell * 0.3989422804014327)


def segment_bias(doc_row, pad_row):
    code = jnp.where(pad_row > 0, doc_row, -1.0)
    key_code = jnp.transpose(jnp.broadcast_to(code, (SEG, SEG)))
    rows = lax.broadcasted_iota(jnp.int32, (SEG, SEG), 0)
    columns = lax.broadcasted_iota(jnp.int32, (SEG, SEG), 1)
    seen = (rows <= columns) & (key_code == doc_row)
    return jnp.where(seen, 0.0, FILL)


def head_rows(pair, odd):
    zero = jnp.zeros((DH, pair.shape[1]), pair.dtype)
    if odd:
        return jnp.concatenate([zero, pair[DH:]], 0)
    return jnp.concatenate([pair[:DH], zero], 0)


def head_lanes(pair, odd):
    lane = lax.broadcasted_iota(jnp.int32, pair.shape, 1)
    keep = (lane >= DH) if odd else (lane < DH)
    return jnp.where(keep, pair, jnp.zeros_like(pair))


def two(p):
    return slice(p * 2 * DH, (p + 1) * 2 * DH)


def one(h):
    return slice(h * DH, (h + 1) * DH)


BLOCKS = ((0, HALF), (HALF, SEG))


TILE = 16
MESH = pl.DeviceIdType.MESH


def bit_orders(sizes):
    dp = [("dp", 1 << n) for n in range(sizes["dp"].bit_length() - 1)]
    slot = [("slot", 1 << n) for n in range(sizes["slot"].bit_length() - 1)]
    first, other = slot[:1], slot[1:]
    return first + other + dp, first + dp[:1] + other + dp[1:]


def plan(blocks, orders):
    half = blocks // 2
    steps, recv = [], 0
    for n, order in enumerate(orders):
        size, row = half, []
        for axis, stride in order:
            halves = size % 2 == 0
            sent = size // 2 if halves else size
            row.append((axis, stride, halves, sent, recv))
            recv += sent
            size = sent
        steps.append((n * half, row))
    return steps, recv


def here():
    return {"dp": lax.axis_index("dp"), "slot": lax.axis_index("slot")}


def across(index, axis, stride):
    bit = (index[axis] // stride) % 2
    peer = dict(index)
    peer[axis] = index[axis] + stride - 2 * bit * stride
    return bit, (peer["dp"], peer["slot"])


def ring(index, offset, group):
    return (index["dp"], (index["slot"] + offset) % group)


def greet(orders, index, group):
    barrier = pltpu.get_barrier_semaphore()
    peers = [ring(index, n, group) for n in range(1, group)] + [
        across(index, axis, stride)[1] for axis, stride in orders[0] if axis == "dp"
    ]
    for peer in peers:
        pl.semaphore_signal(barrier, inc=1, device_id=peer, device_id_type=MESH)
    pl.semaphore_wait(barrier, len(peers))


def gather(ref, sems, index, group):
    own = ref.at[index["slot"]]
    return [
        pltpu.make_async_remote_copy(
            own, own, sems.at[0, n], sems.at[1, n],
            device_id=ring(index, n, group), device_id_type=MESH,
        )
        for n in range(1, group)
    ]


def run_events(step, last, events):
    events = sorted(events, key=lambda event: event[0])
    for when in range(last + 1):
        todo = [e for e in events if e[0] == when or (when == last and e[0] > last)]
        if not todo:
            continue

        @pl.when(step == when)
        def _():
            for _, act, args in todo:
                act(*args)


class Reduction:
    def __init__(self, buf, recv, sems, free, base, orders, index):
        self.buf, self.recv, self.sems, self.free = buf, recv, sems, free
        self.base, self.index = base, index
        self.steps, _ = plan(buf.shape[0], orders)
        self.depth = len(orders[0])
        up = [
            (level, False)
            for level in reversed(range(self.depth))
            if any(row[level][2] for _, row in self.steps)
        ]
        self.moves = [(level, True) for level in range(self.depth)] + up
        self.stages = len(self.moves) + 1

    def copies(self, move):
        level, down = self.moves[move]
        found = []
        for n, (start, row) in enumerate(self.steps):
            for axis, stride, halves, sent, _ in row[: level if down else level + 1]:
                if halves:
                    start = start + across(self.index, axis, stride)[0] * sent
            axis, stride, halves, sent, at = row[level]
            bit, peer = across(self.index, axis, stride)
            slot = self.base + n * self.depth + level
            if down:
                keep = start + bit * sent if halves else start
                give = start + sent - bit * sent if halves else start
                target, ends = self.recv.at[pl.ds(at, sent)], 0
            elif halves:
                keep, give = None, start
                target, ends = self.buf.at[pl.ds(give, sent)], 2
            else:
                continue
            copy = pltpu.make_async_remote_copy(
                self.buf.at[pl.ds(give, sent)], target,
                self.sems.at[ends, slot], self.sems.at[ends + 1, slot],
                device_id=peer, device_id_type=MESH,
            )
            found.append((copy, halves, keep, sent, at, slot, peer))
        return found

    def tick(self, stage):
        if stage > 0:
            down = self.moves[stage - 1][1]
            for copy, halves, keep, sent, at, slot, peer in self.copies(stage - 1):
                copy.wait()
                if not down:
                    continue
                if halves:
                    pl.semaphore_signal(
                        self.free.at[slot], inc=1, device_id=peer, device_id_type=MESH
                    )
                mine = self.buf[pl.ds(keep, sent)].astype(F32)
                self.buf[pl.ds(keep, sent)] = (
                    mine + self.recv[pl.ds(at, sent)].astype(F32)
                ).astype(BF16)
        if stage < len(self.moves):
            down = self.moves[stage][1]
            for copy, halves, keep, sent, at, slot, peer in self.copies(stage):
                if not down:
                    pl.semaphore_wait(self.free.at[slot], 1)
                copy.start()


def reduction_scratch(sizes, orders, width):
    depth = len(orders[0])
    return (
        [pltpu.VMEM((s, TILE, width), BF16) for s in sizes]
        + [pltpu.VMEM((plan(s, orders)[1], TILE, width), BF16) for s in sizes]
        + [
            pltpu.SemaphoreType.DMA((4, len(sizes) * 2 * depth)),
            pltpu.SemaphoreType.REGULAR((len(sizes) * 2 * depth,)),
        ]
    )


def reductions(refs, count, orders, index):
    bufs, recvs, (sems, free) = refs[:count], refs[count : 2 * count], refs[2 * count :]
    return [
        Reduction(bufs[n], recvs[n], sems, free, n * 2 * len(orders[0]), orders, index)
        for n in range(count)
    ]


def tiles(value):
    return value.reshape(value.shape[0] // TILE, TILE, value.shape[1])


EARLY = 2


def front_kernel(
    count, chunks, group, orders,
    x_in, mem_in, wq_in, wk_in, wv_in, wsq_in, wo_in, wup_in, wdown_in, cot_in,
    doc, pad, gain1, gain2, gain3,
    out, res_out, low_out, q_out, k_out, kt_out, v_out, vt_out, d_out, late, *rest,
):
    sums, rest = rest[:EARLY], rest[EARLY:]
    (lse, inner, slot_k, slot_kt, slot_v, slot_q, slot_qt, mem, stats, dwo_out, dgain) = rest[:11]
    (
        x, cot, low, q_t, k, k_t, v, v_t, o_t, second, second_t, cot_t, ffn, grad,
        wq, wk, wv, wsq, wo, wup, wdown, slot_vt, bias, dwo, dwup, dwdown_t, out_low, late_buf,
        loads, stores, gathers, late_sems,
    ) = rest[11:43]
    index = here()
    work = reductions(rest[43:], EARLY, orders, index)
    pairs = H // 2

    def load(n):
        pairs_of = (
            [(x_in.at[i], x.at[i]) for i in range(count)]
            + [(wq_in, wq), (wk_in, wk), (wv_in, wv), (wsq_in, wsq), (wo_in, wo)]
            + [(cot_in.at[i], cot.at[i]) for i in range(count)]
            + [
                (wup_in.at[:, c * SEG : (c + 1) * SEG], wup.at[c]) for c in range(chunks)
            ]
            + [(wdown_in.at[c], wdown.at[c]) for c in range(chunks)]
            + [(mem_in, mem.at[index["slot"]])]
        )
        return pltpu.make_async_copy(*pairs_of[n], loads.at[n])

    weights_at = count
    cot_at = count + 5
    up_at = 2 * count + 5
    down_at = up_at + chunks
    mem_at = down_at + chunks
    order = (
        [mem_at, 0, weights_at, weights_at + 1, weights_at + 2]
        + list(range(1, count))
        + [weights_at + 3, weights_at + 4]
        + list(range(cot_at, mem_at))
    )
    for n in order:
        load(n).start()
    greet(orders, index, group)
    load(mem_at).wait()
    for copy in gather(mem, gathers.at[0], index, group):
        copy.start()
    dwo[...] = jnp.zeros_like(dwo)
    dwup[...] = jnp.zeros_like(dwup)
    dwdown_t[...] = jnp.zeros_like(dwdown_t)
    dgain[...] = jnp.zeros_like(dgain)
    for n in range(weights_at, weights_at + 3):
        load(n).wait()

    kept = ((low, low_out), (q_t, q_out), (k, k_out), (k_t, kt_out), (v, v_out), (v_t, vt_out))

    def keep(n, i):
        source, target = kept[n]
        return pltpu.make_async_copy(source.at[i], target.at[i], stores.at[n, i])

    @pl.loop(0, count)
    def _(i):
        pltpu.make_async_copy(x_in.at[i], x.at[i], loads.at[i]).wait()
        unit, _ = norm(x[i].astype(F32))
        row = (unit * gain1[...]).astype(BF16)
        low[i] = row
        q_t[i] = jnp.transpose((nn(row, wq[...]) * SCALE).astype(BF16)).reshape(q_t.shape[1:])
        key = nn(row, wk[...]).astype(BF16)
        k_t[i] = jnp.transpose(key).reshape(k_t.shape[1:])
        value = nn(row, wv[...]).astype(BF16)
        v_t[i] = jnp.transpose(value).reshape(v_t.shape[1:])
        for p in range(pairs):
            k[i, p] = key[:, two(p)]
            v[i, p] = value[:, two(p)]
        for n in range(len(kept)):
            keep(n, i).start()

    for copy in gather(mem, gathers.at[0], index, group):
        copy.wait()
    load(weights_at + 3).wait()
    load(weights_at + 4).wait()
    slots = group * mem.shape[2]
    unit, _ = norm(mem[:, 0].reshape(slots, mem.shape[3]).astype(F32))
    row = (unit * gain3[...]).astype(BF16)
    sk = nn(row, wk[...]).astype(BF16)
    sv = nn(row, wv[...]).astype(BF16)
    sq = (nn(row, wsq[...]) * SCALE).astype(BF16)
    lane = lax.broadcasted_iota(jnp.int32, (slots, 2 * DH), 1) < DH
    for p in range(pairs):
        slot_k[p], slot_v[p], slot_q[p] = sk[:, two(p)], sv[:, two(p)], sq[:, two(p)]
        slot_kt[p] = jnp.transpose(sk[:, two(p)])
        slot_vt[p] = jnp.transpose(sv[:, two(p)])
        slot_qt[p] = jnp.transpose(sq[:, two(p)])
        parts = []
        for odd in range(2):
            mine = head_lanes(sq[:, two(p)], odd)
            cs = [
                nn(mine, k_t[i, p]) + jnp.where(pad[:, i * SEG : (i + 1) * SEG] > 0, 0.0, FILL)
                for i in range(count)
            ]
            top = jnp.max(cs[0], 1, keepdims=True)
            for c in cs[1:]:
                top = jnp.maximum(top, jnp.max(c, 1, keepdims=True))
            total, acc = 0.0, 0.0
            for i, c in enumerate(cs):
                w = jnp.exp(c - top)
                total = total + jnp.sum(w, 1, keepdims=True)
                acc = acc + nn(w.astype(BF16), v[i, p])
            parts.append((acc, top, total))
        for n in range(3):
            stats[index["slot"], n, :, two(p)] = jnp.where(lane, parts[0][n], parts[1][n])
    for copy in gather(stats, gathers.at[1], index, group):
        copy.start()

    @pl.loop(0, count)
    def _(i):
        cols = pl.ds(pl.multiple_of(i * SEG, SEG), SEG)
        bias[...] = segment_bias(doc[:, cols], pad[:, cols])
        for h in range(H):
            p, odd = h // 2, h % 2
            own = one(odd)
            qm = head_rows(q_t[i, p], odd)
            for lo, hi in BLOCKS:
                qb = qm[:, lo:hi]
                s = nn(k[i, p, :hi, :], qb) + bias[:hi, lo:hi]
                sm = nn(slot_k[p], qb)
                top = jnp.maximum(jnp.max(s, 0, keepdims=True), jnp.max(sm, 0, keepdims=True))
                e = jnp.exp(s - top)
                em = jnp.exp(sm - top)
                total = jnp.sum(e, 0, keepdims=True) + jnp.sum(em, 0, keepdims=True)
                o = nn(v_t[i, p, own, :hi], e.astype(BF16)) + nn(slot_vt[p, own, :], em.astype(BF16))
                o_t[i, one(h), lo:hi] = (o / total).astype(BF16)
                lse[i, p, odd : odd + 1, lo:hi] = top + jnp.log(total)
        res = x[i].astype(F32) + nn(jnp.transpose(o_t[i]), wo[...])
        ffn[i] = res
        grad[i] = jnp.zeros_like(res)
        unit, _ = norm(res)
        row = (unit * gain2[...]).astype(BF16)
        second[i] = row
        second_t[i] = jnp.transpose(row)
        pltpu.make_async_copy(cot_in.at[i], cot.at[i], loads.at[cot_at + i]).wait()
        cot_t[i] = jnp.transpose(cot[i])

    last = chunks * count + count - 1

    def summed(n, stage):
        work[n].tick(stage)
        if stage == work[n].stages - 1:
            pltpu.make_async_copy(work[n].buf, sums[n], late_sems.at[n]).start()

    events = [
        ((n + 1) * count - 1 + stage, summed, (n, stage))
        for n in range(EARLY)
        for stage in range(work[n].stages)
    ]

    @pl.loop(0, chunks * count)
    def _(step):
        c = step // count
        i = step % count

        @pl.when(i == 0)
        def _():
            for n in range(chunks):

                @pl.when(c == n)
                def _():
                    load(up_at + n).wait()
                    load(down_at + n).wait()

        act, slope = gelu_pair(nn(second[i], wup[c]))
        act = act.astype(BF16)
        ffn[i] += nn(act, wdown[c])
        up_grad = (nt(cot[i], wdown[c]) * slope).astype(BF16)
        dwdown_t[...] += nn(cot_t[i], act)
        dwup[...] += nn(second_t[i], up_grad)
        grad[i] += nt(up_grad, wup[c])

        half = SEG // TILE
        for n in range(chunks):

            @pl.when((i == count - 1) & (c == n))
            def _():
                target = work[n].buf if n < EARLY else late_buf.at[n - EARLY]
                target[:half] = tiles(dwup[...].astype(BF16))
                target[half:] = tiles(jnp.transpose(dwdown_t[...].astype(BF16)))
                dwup[...] = jnp.zeros_like(dwup)
                dwdown_t[...] = jnp.zeros_like(dwdown_t)
                if n >= EARLY:
                    pltpu.make_async_copy(target, late.at[n - EARLY], late_sems.at[n]).start()

        run_events(step, last, [e for e in events if e[0] < chunks * count])

    def finish(n, i):
        source, target = ((out_low, out), (grad, res_out), (o_t, d_out))[n]
        return pltpu.make_async_copy(source.at[i], target.at[i], stores.at[len(kept) + n, i])

    @pl.loop(0, count)
    def _(i):
        res = x[i].astype(F32) + nn(jnp.transpose(o_t[i]), wo[...])
        unit, inverse = norm(res)
        out_low[i] = ffn[i].astype(BF16)
        back, gain_part = norm_back(grad[i], unit, inverse, gain2[...])
        dgain[...] += gain_part
        back = back + cot[i].astype(F32)
        grad[i] = back
        row = back.astype(BF16)
        dwo[...] += nn(o_t[i], row)
        d = nt(wo[...], row).astype(BF16)
        prod = d.astype(F32) * o_t[i].astype(F32)
        for h in range(H):
            inner[i, h // 2, h % 2 : h % 2 + 1, :] = jnp.sum(prod[one(h), :], 0, keepdims=True)
        o_t[i] = d
        for n in range(3):
            finish(n, i).start()
        run_events(i + chunks * count, last, [e for e in events if e[0] >= chunks * count])

    dwo_out[...] = dwo[...].astype(BF16)
    for copy in gather(stats, gathers.at[1], index, group):
        copy.wait()
    for i in range(count):
        for n in range(len(kept)):
            keep(n, i).wait()
        for n in range(3):
            finish(n, i).wait()
    for n in range(EARLY):
        pltpu.make_async_copy(work[n].buf, sums[n], late_sems.at[n]).wait()
    for n in range(EARLY, chunks):
        pltpu.make_async_copy(late_buf.at[n - EARLY], late.at[n - EARLY], late_sems.at[n]).wait()


def update(
    index, stats, mem, slot_q, slot_k, slot_v, wgate, bgate, wwrite,
    new_memory, g_out, g_t, lse, inner_out, sq_acc, sk_acc, sv_acc, direct_out,
    dwgate, dwwrite, dbias, fresh,
):
    group, _, rows, width = mem.shape
    slots = group * rows
    pairs = H // 2
    same = (
        lax.broadcasted_iota(jnp.int32, (width, width), 0) // DH
        == lax.broadcasted_iota(jnp.int32, (width, width), 1) // DH
    ).astype(F32)

    def head_sum(value):
        return nn(value, same, lax.Precision.HIGHEST)

    start = index["slot"] * rows
    row = lax.broadcasted_iota(jnp.int32, (slots, width), 0)
    own = (row >= start) & (row < start + rows)
    sq, sk, sv = (
        jnp.concatenate([r[p] for p in range(pairs)], 1).astype(F32) for r in (slot_q, slot_k, slot_v)
    )
    state = mem[:, 0].reshape(slots, width).astype(F32)
    memory_out = mem[:, 1].reshape(slots, width).astype(F32)
    own_score = head_sum(sq * sk)
    top = own_score
    for n in range(group):
        top = jnp.maximum(top, stats[n, 1])
    power = jnp.exp(own_score - top)
    total = power
    weighted = power.astype(BF16).astype(F32) * sv
    for n in range(group):
        factor = jnp.exp(stats[n, 1] - top)
        total = total + factor * stats[n, 2]
        weighted = weighted + factor * stats[n, 0]
    value = weighted / total
    low = value.astype(BF16)
    gate = jax.nn.sigmoid(nn(low, wgate[...]) + bgate[...])
    written = nn(low, wwrite[...])
    fresh[...] = ((1.0 - gate) * state + gate * written).reshape(fresh.shape)
    new_memory[...] = fresh[index["slot"]]
    gate_grad = memory_out * (written - state) * gate * (1.0 - gate)
    gate_low = gate_grad.astype(BF16)
    written_low = (memory_out * gate).astype(BF16)
    zero = jnp.zeros((slots, width), F32)
    direct_out[...] = jnp.where(own, memory_out * (1.0 - gate), zero)
    mine = jnp.where(own, gate_grad, zero)
    dbias[...] = jnp.sum(mine, 0, keepdims=True)
    low_t = jnp.transpose(low)
    dwgate[...] = tiles(nn(low_t, mine.astype(BF16)).astype(BF16))
    dwwrite[...] = tiles(nn(low_t, jnp.where(own, memory_out * gate, zero).astype(BF16)).astype(BF16))
    g_low = (nt(gate_low, wgate[...]) + nt(written_low, wwrite[...])).astype(BF16)
    g = g_low.astype(F32)
    inner = head_sum(g * value)
    spread = top + jnp.log(total)
    delta = (power / total * (head_sum(g * sv) - inner)).astype(BF16).astype(F32)
    self_q = jnp.where(own, delta * sk, zero)
    self_k = jnp.where(own, delta * sq, zero)
    self_v = jnp.where(own, power.astype(BF16).astype(F32) / total * g, zero)
    for p in range(pairs):
        g_out[p] = g_low[:, two(p)]
        g_t[p] = jnp.transpose(g_low[:, two(p)])
        inner_out[p] = inner[:, two(p)]
        lse[p] = spread[:, two(p)]
        sq_acc[p] = jnp.transpose(self_q[:, two(p)])
        sk_acc[p] = jnp.transpose(self_k[:, two(p)])
        sv_acc[p] = jnp.transpose(self_v[:, two(p)])


def back_kernel(
    count, group, orders, sizes,
    x_in, low_in, q_in, k_in, kt_in, v_in, vt_in, d_in, res_in,
    wq_in, wk_in, wv_in, wsq_in, wgate_in, wwrite_in, late, dwo_in,
    lse, inner, doc, pad, gain1, mgain, slot_k, slot_kt, slot_v, slot_q, slot_qt, mem, stats, bgate,
    dgain2, *rest,
):
    early = len(sizes)
    input_grad = rest[0]
    sums = rest[1 : 1 + early]
    (
        dwq_out, dwk_out, dwv_out, dwsq_out, gains_out, memory_grad, new_memory,
        x, low, q_t, k, k_t, v, v_t, d_t, res, wq, wk, wv, wsq, wgate, wwrite,
        bias, grads, acc, w_all, sq_acc, sk_acc, sv_acc, g, g_t, wlse, winner, direct, fresh,
        slot_low, dgain, dgain3, dbias, part, part_in, part_sems, block_loads, loads, stores,
    ) = rest[1 + early : 46 + early]
    pairs = H // 2
    index = here()
    work = reductions(rest[46 + early :], early + pairs + 1, orders, index)
    wide = 2 * DH
    third = wo_blocks = wq.shape[0] // TILE

    blocks = (
        (q_in, q_t), (k_in, k), (kt_in, k_t), (v_in, v), (vt_in, v_t), (d_in, d_t), (low_in, low),
        (x_in, x), (res_in, res),
    )
    used = 7

    def block(n, i):
        return pltpu.make_async_copy(blocks[n][0].at[i], blocks[n][1].at[i], block_loads.at[n, i])

    whole = (
        [(wgate_in, wgate), (wwrite_in, wwrite), (wq_in, wq), (wk_in, wk), (wv_in, wv), (wsq_in, wsq)]
        + [(late.at[n], work[n].buf) for n in range(early - 1)]
        + [(dwo_in, work[early - 1].buf.at[:wo_blocks])]
    )

    def load(n):
        return pltpu.make_async_copy(*whole[n], loads.at[n])

    for n in (0, 1):
        load(n).start()
    for n in range(used):
        block(n, 0).start()
    for n in range(2, len(whole)):
        load(n).start()
    for i in range(1, count):
        for n in range(used):
            block(n, i).start()
    for i in range(count):
        for n in range(used, len(blocks)):
            block(n, i).start()
    greet(orders, index, group)
    load(0).wait()
    load(1).wait()
    update(
        index, stats, mem, slot_q, slot_k, slot_v, wgate, bgate, wwrite,
        new_memory, g, g_t, wlse, winner, sq_acc, sk_acc, sv_acc, direct,
        work[early - 1].buf.at[third : 2 * third], work[early - 1].buf.at[2 * third :], dbias, fresh,
    )
    for n in range(2, 6):
        load(n).wait()
    for n in range(pairs):
        for m, w in enumerate((wq, wk, wv)):
            at = (3 * n + m) * wide
            w_all[:, at : at + wide] = w[:, two(n)]
    slots = group * mem.shape[2]
    unit3, inverse3 = norm(mem[:, 0].reshape(slots, mem.shape[3]).astype(F32))
    slot_low[...] = (unit3 * mgain[...]).astype(BF16)
    dgain[...] = jnp.zeros_like(dgain)
    acc[...] = jnp.zeros_like(acc)

    strides = [1 << n for n in reversed(range(group.bit_length() - 1))]

    def scatter(level):
        stride = strides[level]
        start, at = 0, 0
        for s in strides[:level]:
            start = start + across(index, "slot", s)[0] * s
            at += s
        bit, peer = across(index, "slot", stride)
        copy = pltpu.make_async_remote_copy(
            part.at[pl.ds(start + stride - bit * stride, stride)], part_in.at[pl.ds(at, stride)],
            part_sems.at[0, level], part_sems.at[1, level], device_id=peer, device_id_type=MESH,
        )
        return copy, start + bit * stride, at, stride

    def slot_grads(stage):
        if stage == 0:
            unit, inverse = norm(mem[:, 0].reshape(slots, mem.shape[3]).astype(F32))
            grad_t = 0.0
            for p in range(pairs):
                grad_t = (
                    grad_t
                    + nn(wk[:, two(p)], sk_acc[p].astype(BF16))
                    + nn(wv[:, two(p)], sv_acc[p].astype(BF16))
                    + nn(wsq[:, two(p)], (sq_acc[p] * SCALE).astype(BF16))
                )
            back, gain_part = norm_back(jnp.transpose(grad_t), unit, inverse, mgain[...])
            part[...] = (back + direct[...]).reshape(part.shape)
            dgain3[...] = gain_part
        else:
            copy, keep, at, size = scatter(stage - 1)
            copy.wait()
            part[pl.ds(keep, size)] += part_in[pl.ds(at, size)]
        if stage < len(strides):
            scatter(stage)[0].start()
        else:
            memory_grad[...] = part[index["slot"]]

    def gains(stage):
        item = work[early + pairs]
        if stage == 0:
            rows = [jnp.broadcast_to(r[...], (8, dgain.shape[1])) for r in (dgain, dgain3, dgain2, dbias)]
            item.buf[...] = tiles(jnp.concatenate(rows, 0).astype(BF16))
        item.tick(stage)
        if stage == item.stages - 1:
            gains_out[...] = item.buf[...].reshape(gains_out.shape).astype(F32)

    def summed(n, stage):
        item = work[n]
        if n < early and stage == 0:
            load(6 + n).wait()
        item.tick(stage)
        if stage < item.stages - 1:
            return
        if n < early:
            pltpu.make_async_copy(item.buf, sums[n], stores.at[n]).start()
            return
        per = wide // TILE
        for m, out in enumerate((dwq_out, dwk_out, dwv_out, dwsq_out)):
            rows = item.buf[m * per : (m + 1) * per].reshape(wide, out.shape[0])
            out[:, two(n - early)] = jnp.transpose(rows)

    busy = pairs * count
    last = busy + count - 1
    events = []
    for n in range(early):
        events += [(n // 2 + stage, summed, (n, stage)) for stage in range(work[n].stages)]
    for n in range(pairs):
        events += [
            ((n + 1) * count - 1 + stage, summed, (early + n, stage))
            for stage in range(work[early + n].stages)
        ]
    events += [(busy + stage, slot_grads, (stage,)) for stage in range(len(strides) + 1)]
    events += [(last + stage, gains, (stage,)) for stage in range(work[early + pairs].stages)]

    @pl.loop(0, busy)
    def _(step):
        p = step // count
        i = step % count

        @pl.when(p == 0)
        def _():
            for n in range(used):
                block(n, i).wait()
            cols = pl.ds(pl.multiple_of(i * SEG, SEG), SEG)
            bias[i] = segment_bias(doc[:, cols], pad[:, cols])

        cols = pl.ds(pl.multiple_of(i * SEG, SEG), SEG)
        pad_bias = jnp.where(pad[:, cols] > 0, 0.0, FILL)
        for odd in range(2):
            own = one(odd)
            qm = head_rows(q_t[i, p], odd)
            dm = head_rows(d_t[i, p], odd)
            c = nn(head_lanes(slot_q[p], odd), k_t[i, p]) + pad_bias
            share = jnp.exp(c - wlse[p, :, odd * DH : odd * DH + 1])
            dotted = nn(head_lanes(g[p], odd), v_t[i, p])
            change = (share * (dotted - winner[p, :, odd * DH : odd * DH + 1])).astype(BF16)
            dk = nn(slot_qt[p, own, :], change)
            dv = nn(g_t[p, own, :], share.astype(BF16))
            sq_acc[p, own, :] += nt(k_t[i, p, own, :], change)
            for lo, hi in BLOCKS:
                qb = qm[:, lo:hi]
                db = dm[:, lo:hi]
                qh = q_t[i, p, own, lo:hi]
                dh = d_t[i, p, own, lo:hi]
                l = lse[i, p, odd : odd + 1, lo:hi]
                t = inner[i, p, odd : odd + 1, lo:hi]
                e = jnp.exp(nn(k[i, p, :hi, :], qb) + bias[i, :hi, lo:hi] - l)
                em = jnp.exp(nn(slot_k[p], qb) - l)
                ds = (e * (nn(v[i, p, :hi, :], db) - t)).astype(BF16)
                dsm = (em * (nn(slot_v[p], db) - t)).astype(BF16)
                dq = (nn(k_t[i, p, own, :hi], ds) + nn(slot_kt[p, own, :], dsm)) * SCALE
                grads[i, p, own, lo:hi] = dq.astype(BF16)
                dvp = nt(dh, e.astype(BF16))
                dkp = nt(qh, ds)
                if hi < SEG:
                    dvp = jnp.concatenate([dvp, jnp.zeros((DH, SEG - hi), F32)], 1)
                    dkp = jnp.concatenate([dkp, jnp.zeros((DH, SEG - hi), F32)], 1)
                dv = dv + dvp
                dk = dk + dkp
                sv_acc[p, own, :] += nt(dh, em.astype(BF16))
                sk_acc[p, own, :] += nt(qh, dsm)
            grads[i, p, wide + odd * DH : wide + (odd + 1) * DH, :] = dk.astype(BF16)
            grads[i, p, 2 * wide + odd * DH : 2 * wide + (odd + 1) * DH, :] = dv.astype(BF16)
        acc[...] += nn(grads[i, p], low[i])

        @pl.when(i == count - 1)
        def _():
            rows = jnp.concatenate(
                [
                    acc[:wide],
                    acc[wide : 2 * wide] + nn(sk_acc[p].astype(BF16), slot_low[...]),
                    acc[2 * wide :] + nn(sv_acc[p].astype(BF16), slot_low[...]),
                    nn((sq_acc[p] * SCALE).astype(BF16), slot_low[...]),
                ],
                0,
            )
            acc[...] = jnp.zeros_like(acc)
            rows = tiles(rows.astype(BF16))
            for n in range(pairs):

                @pl.when(p == n)
                def _():
                    work[early + n].buf[...] = rows

        run_events(step, last, [e for e in events if e[0] < busy])

    @pl.loop(0, count)
    def _(i):
        block(used, i).wait()
        block(used + 1, i).wait()
        unit, inverse = norm(x[i].astype(F32))
        grad_t = nn(w_all[...], grads[i].reshape(3 * pairs * wide, SEG))
        back, gain_part = norm_back(jnp.transpose(grad_t), unit, inverse, gain1[...])
        dgain[...] += gain_part
        res[i] += back
        pltpu.make_async_copy(res.at[i], input_grad.at[i], block_loads.at[0, i]).start()
        run_events(i + busy, last, [e for e in events if e[0] >= busy])

    for i in range(count):
        pltpu.make_async_copy(res.at[i], input_grad.at[i], block_loads.at[0, i]).wait()
    for n in range(early):
        pltpu.make_async_copy(work[n].buf, sums[n], stores.at[n]).wait()


def struct(shape, dtype):
    return jax.ShapeDtypeStruct(shape, dtype)


def params(collective_id):
    return pltpu.CompilerParams(
        vmem_limit_bytes=63 << 20, collective_id=collective_id, has_side_effects=True
    )


def body(
    tokens,
    memory,
    pad_mask,
    doc_lengths,
    first_gain,
    query_weight,
    key_weight,
    value_weight,
    out_weight,
    second_gain,
    up_weight,
    down_weight,
    memory_gain,
    slot_query_weight,
    gate_weight,
    gate_bias,
    write_weight,
    out_cotangent,
    memory_cotangent,
):
    rows, width = tokens.shape
    hidden = up_weight.shape[1]
    count = rows // SEG
    chunks = hidden // SEG
    pairs = H // 2
    two_heads = 2 * DH
    slots_here = memory.shape[1]
    group = lax.axis_size("slot")
    slots = slots_here * group
    begin = (lax.axis_index("dp") * group + lax.axis_index("slot")) * rows
    places = begin + jnp.arange(rows, dtype=jnp.int32)
    ends = jnp.cumsum(doc_lengths)
    document = jnp.sum((places[:, None] >= ends[None, :]).astype(jnp.int32), 1)
    doc = document.astype(F32)[None, :]
    pad = pad_mask.astype(F32)[None, :]
    gain1, gain2, gain3 = (g[None, :] for g in (first_gain, second_gain, memory_gain))
    orders = bit_orders({"dp": lax.axis_size("dp"), "slot": group})

    anywhere = pl.BlockSpec(memory_space=pl.ANY)
    vm = pl.BlockSpec(memory_space=pltpu.VMEM)
    tokens = tokens.reshape(count, SEG, width)
    segments = (count, SEG, width)
    by_rows = (count, pairs, SEG, two_heads)
    by_lanes = (count, pairs, two_heads, SEG)
    square = (width, width)
    blocks = 2 * SEG // TILE
    half = SEG // TILE
    slot_tall, slot_wide = (pairs, slots, two_heads), (pairs, two_heads, slots)
    per_head = (count, pairs, 2, SEG)
    outs = pl.pallas_call(
        lambda *refs: front_kernel(count, chunks, group, orders, *refs),
        in_specs=[anywhere] * 10 + [vm] * 5,
        out_specs=[anywhere] * (10 + EARLY) + [vm] * 11,
        out_shape=[
            struct(segments, BF16), struct(segments, F32), struct(segments, BF16),
            struct(by_lanes, BF16), struct(by_rows, BF16), struct(by_lanes, BF16),
            struct(by_rows, BF16), struct(by_lanes, BF16), struct((count, width, SEG), BF16),
            struct((chunks - EARLY, blocks, TILE, width), BF16),
        ]
        + [struct((blocks, TILE, width), BF16)] * EARLY
        + [
            struct(per_head, F32), struct(per_head, F32), struct(slot_tall, BF16),
            struct(slot_wide, BF16), struct(slot_tall, BF16), struct(slot_tall, BF16),
            struct(slot_wide, BF16), struct((group, 2, slots_here, width), BF16),
            struct((group, 3, slots, width), F32), struct(square, BF16), struct((1, width), F32),
        ],
        scratch_shapes=[
            pltpu.VMEM(segments, BF16), pltpu.VMEM(segments, BF16), pltpu.VMEM(segments, BF16),
            pltpu.VMEM(by_lanes, BF16), pltpu.VMEM(by_rows, BF16), pltpu.VMEM(by_lanes, BF16),
            pltpu.VMEM(by_rows, BF16), pltpu.VMEM(by_lanes, BF16),
            pltpu.VMEM((count, width, SEG), BF16), pltpu.VMEM(segments, BF16),
            pltpu.VMEM((count, width, SEG), BF16), pltpu.VMEM((count, width, SEG), BF16),
            pltpu.VMEM(segments, F32), pltpu.VMEM(segments, F32),
            pltpu.VMEM(square, BF16), pltpu.VMEM(square, BF16), pltpu.VMEM(square, BF16),
            pltpu.VMEM(square, BF16), pltpu.VMEM(square, BF16),
            pltpu.VMEM((chunks, width, SEG), BF16), pltpu.VMEM((chunks, SEG, width), BF16),
            pltpu.VMEM(slot_wide, BF16), pltpu.VMEM((SEG, SEG), F32), pltpu.VMEM(square, F32),
            pltpu.VMEM((width, SEG), F32), pltpu.VMEM((width, SEG), F32),
            pltpu.VMEM(segments, BF16), pltpu.VMEM((chunks - EARLY, blocks, TILE, width), BF16),
            pltpu.SemaphoreType.DMA((2 * count + 6 + 2 * chunks,)),
            pltpu.SemaphoreType.DMA((9, count)),
            pltpu.SemaphoreType.DMA((2, 2, group)),
            pltpu.SemaphoreType.DMA((chunks,)),
        ]
        + reduction_scratch([blocks] * EARLY, orders, width),
        compiler_params=params(0),
        name="front",
    )(
        tokens, jnp.stack([memory[0], memory_cotangent[0]]), query_weight, key_weight, value_weight,
        slot_query_weight, out_weight, up_weight, down_weight.reshape(chunks, SEG, width),
        out_cotangent.reshape(segments), doc, pad, gain1, gain2, gain3,
    )
    layer_out, res_grad, low, q_t, k, k_t, v, v_t, d_t, late = outs[:10]
    early = list(outs[10 : 10 + EARLY])
    (
        lse, inner, slot_k, slot_kt, slot_v, slot_q, slot_qt, mem, stats, dwo, dgain2,
    ) = outs[10 + EARLY :]

    sizes = [blocks] * (chunks - EARLY) + [3 * half]
    n_sum = len(sizes)
    outs = pl.pallas_call(
        lambda *refs: back_kernel(count, group, orders, sizes, *refs),
        in_specs=[anywhere] * 17 + [vm] * 15,
        out_specs=[anywhere] * (1 + n_sum) + [vm] * 7,
        out_shape=[struct(segments, F32)]
        + [struct((n, TILE, width), BF16) for n in sizes]
        + [struct(square, BF16)] * 4
        + [
            struct((32, width), F32), struct((slots_here, width), F32), struct((slots_here, width), F32),
        ],
        scratch_shapes=[
            pltpu.VMEM(segments, BF16), pltpu.VMEM(segments, BF16), pltpu.VMEM(by_lanes, BF16),
            pltpu.VMEM(by_rows, BF16), pltpu.VMEM(by_lanes, BF16), pltpu.VMEM(by_rows, BF16),
            pltpu.VMEM(by_lanes, BF16), pltpu.VMEM(by_lanes, BF16), pltpu.VMEM(segments, F32),
            pltpu.VMEM(square, BF16), pltpu.VMEM(square, BF16), pltpu.VMEM(square, BF16),
            pltpu.VMEM(square, BF16), pltpu.VMEM(square, BF16), pltpu.VMEM(square, BF16),
            pltpu.VMEM((count, SEG, SEG), F32), pltpu.VMEM((count, pairs, 3 * two_heads, SEG), BF16),
            pltpu.VMEM((3 * two_heads, width), F32), pltpu.VMEM((width, 3 * width), BF16),
            pltpu.VMEM(slot_wide, F32), pltpu.VMEM(slot_wide, F32), pltpu.VMEM(slot_wide, F32),
            pltpu.VMEM(slot_tall, BF16), pltpu.VMEM(slot_wide, BF16), pltpu.VMEM(slot_tall, F32),
            pltpu.VMEM(slot_tall, F32), pltpu.VMEM((slots, width), F32),
            pltpu.VMEM((group, slots_here, width), F32), pltpu.VMEM((slots, width), BF16),
            pltpu.VMEM((1, width), F32), pltpu.VMEM((1, width), F32), pltpu.VMEM((1, width), F32),
            pltpu.VMEM((group, slots_here, width), F32), pltpu.VMEM((group, slots_here, width), F32),
            pltpu.SemaphoreType.DMA((2, group)), pltpu.SemaphoreType.DMA((9, count)),
            pltpu.SemaphoreType.DMA((6 + n_sum,)), pltpu.SemaphoreType.DMA((n_sum,)),
        ]
        + reduction_scratch(sizes + [4 * two_heads // TILE] * pairs + [2], orders, width),
        compiler_params=params(1),
        name="back",
    )(
        tokens, low, q_t, k, k_t, v, v_t, d_t.reshape(by_lanes), res_grad,
        query_weight, key_weight, value_weight, slot_query_weight, gate_weight, write_weight,
        late, tiles(dwo),
        lse, inner, doc, pad, gain1, gain3, slot_k, slot_kt, slot_v, slot_q, slot_qt, mem, stats,
        gate_bias[None, :], dgain2,
    )
    input_grad = outs[0].reshape(rows, width)
    sums = outs[1 : 1 + n_sum]
    dwq, dwk, dwv, dwsq, gains, memory_grad, new_memory = outs[1 + n_sum :]
    ffn = early + list(sums[:-1])
    dwup = jnp.concatenate([f[:half].reshape(width, SEG) for f in ffn], 1)
    dwdown = jnp.concatenate([f[half:].reshape(SEG, width) for f in ffn], 0)
    dwo, dwgate, dwwrite = (
        sums[-1][n * half : (n + 1) * half].reshape(width, width) for n in range(3)
    )

    return (
        layer_out.reshape(rows, width),
        new_memory[None],
        input_grad,
        memory_grad[None],
        gains[0],
        dwq.astype(F32),
        dwk.astype(F32),
        dwv.astype(F32),
        dwo.astype(F32),
        gains[16],
        dwup.astype(F32),
        dwdown.astype(F32),
        gains[8],
        dwsq.astype(F32),
        dwgate.astype(F32),
        gains[24],
        dwwrite.astype(F32),
    )


def solution(mesh):
    token = P(("dp", "slot"), None)
    slot = P("dp", "slot", None)
    in_specs = (
        (token, slot, P(("dp", "slot"))) + (P(),) * 14 + (token, slot)
    )
    out_specs = (token, slot, token, slot) + (P(),) * 13
    return jax.shard_map(body, mesh=mesh, in_specs=in_specs, out_specs=out_specs, check_vma=False)
```

```python
import jax
import jax.numpy as jnp
from jax import lax
from jax.experimental import pallas as pl
from jax.experimental.pallas import tpu as pltpu
from jax.sharding import PartitionSpec as P

H = 8
DH = 64
SEG = 512
HALF = 256
FILL = -1e30
EPS = 1e-05
SCALE = DH ** (-0.5)
F32 = jnp.float32
BF16 = jnp.bfloat16

TAIL = (
    0.11962928145668905,
    0.12075423000729175,
    0.09991172819365436,
    0.12856765411993218,
    -0.053695489964182386,
    0.20636694099934239,
    -0.15721125090545032,
    0.035676834162404004,
)


def nn(a, b, precision=None):
    return lax.dot_general(
        a, b, (((1,), (0,)), ((), ())), preferred_element_type=F32, precision=precision
    )


def nt(a, b):
    return lax.dot_general(a, b, (((1,), (1,)), ((), ())), preferred_element_type=F32)


def norm(value):
    center = value - jnp.mean(value, -1, keepdims=True)
    inverse = lax.rsqrt(jnp.mean(center * center, -1, keepdims=True) + EPS)
    return center * inverse, inverse


def norm_back(grad, unit, inverse, gain):
    inner = grad * gain
    value_grad = inverse * (
        inner
        - jnp.mean(inner, -1, keepdims=True)
        - unit * jnp.mean(inner * unit, -1, keepdims=True)
    )
    return value_grad, jnp.sum(grad * unit, 0, keepdims=True)


def gelu_pair(x):
    t = 1.0 / (1.0 + 0.3 * jnp.abs(x))
    poly = TAIL[7]
    for c in TAIL[6::-1]:
        poly = poly * t + c
    bell = jnp.exp(-0.5 * (x * x))
    tail = bell * (poly * t)
    cdf = jnp.where(x >= 0, 1.0 - tail, tail)
    return x * cdf, cdf + x * (bell * 0.3989422804014327)


def segment_bias(doc_row, pad_row):
    code = jnp.where(pad_row > 0, doc_row, -1.0)
    key_code = jnp.transpose(jnp.broadcast_to(code, (SEG, SEG)))
    rows = lax.broadcasted_iota(jnp.int32, (SEG, SEG), 0)
    columns = lax.broadcasted_iota(jnp.int32, (SEG, SEG), 1)
    seen = (rows <= columns) & (key_code == doc_row)
    return jnp.where(seen, 0.0, FILL)


def documents(lengths, index, group, rows):
    place = lax.broadcasted_iota(jnp.int32, (1, rows), 1)
    place = place + (index["dp"] * group + index["slot"]) * rows
    end, doc = 0, jnp.zeros((1, rows), F32)
    for n in range(lengths.shape[0]):
        end = end + lengths[n]
        doc = doc + jnp.where(place >= end, 1.0, 0.0)
    return doc


def head_rows(pair, odd):
    zero = jnp.zeros((DH, pair.shape[1]), pair.dtype)
    if odd:
        return jnp.concatenate([zero, pair[DH:]], 0)
    return jnp.concatenate([pair[:DH], zero], 0)


def head_lanes(pair, odd):
    lane = lax.broadcasted_iota(jnp.int32, pair.shape, 1)
    keep = (lane >= DH) if odd else (lane < DH)
    return jnp.where(keep, pair, jnp.zeros_like(pair))


def two(p):
    return slice(p * 2 * DH, (p + 1) * 2 * DH)


def one(h):
    return slice(h * DH, (h + 1) * DH)


BLOCKS = ((0, HALF), (HALF, SEG))


TILE = 16
MESH = pl.DeviceIdType.MESH


def bit_orders(sizes):
    dp = [("dp", 1 << n) for n in range(sizes["dp"].bit_length() - 1)]
    slot = [("slot", 1 << n) for n in range(sizes["slot"].bit_length() - 1)]
    first, other = slot[:1], slot[1:]
    return first + other + dp, first + dp[:1] + other + dp[1:]


def plan(blocks, orders):
    half = blocks // 2
    steps, recv = [], 0
    for n, order in enumerate(orders):
        size, row = half, []
        for axis, stride in order:
            halves = size % 2 == 0
            sent = size // 2 if halves else size
            row.append((axis, stride, halves, sent, recv))
            recv += sent
            size = sent
        steps.append((n * half, row))
    return steps, recv


def here():
    return {"dp": lax.axis_index("dp"), "slot": lax.axis_index("slot")}


def across(index, axis, stride):
    bit = (index[axis] // stride) % 2
    peer = dict(index)
    peer[axis] = index[axis] + stride - 2 * bit * stride
    return bit, (peer["dp"], peer["slot"])


def ring(index, offset, group):
    return (index["dp"], (index["slot"] + offset) % group)


def greet(orders, index, group):
    barrier = pltpu.get_barrier_semaphore()
    peers = [ring(index, n, group) for n in range(1, group)] + [
        across(index, axis, stride)[1] for axis, stride in orders[0] if axis == "dp"
    ]
    for peer in peers:
        pl.semaphore_signal(barrier, inc=1, device_id=peer, device_id_type=MESH)
    pl.semaphore_wait(barrier, len(peers))


def gather(ref, sems, index, group):
    own = ref.at[index["slot"]]
    return [
        pltpu.make_async_remote_copy(
            own, own, sems.at[0, n], sems.at[1, n],
            device_id=ring(index, n, group), device_id_type=MESH,
        )
        for n in range(1, group)
    ]


def run_events(step, last, events):
    events = sorted(events, key=lambda event: event[0])
    for when in range(last + 1):
        todo = [e for e in events if e[0] == when or (when == last and e[0] > last)]
        if not todo:
            continue

        @pl.when(step == when)
        def _():
            for _, act, args in todo:
                act(*args)


class Reduction:
    def __init__(self, buf, recv, sems, free, base, orders, index):
        self.buf, self.recv, self.sems, self.free = buf, recv, sems, free
        self.base, self.index = base, index
        self.steps, _ = plan(buf.shape[0], orders)
        self.depth = len(orders[0])
        up = [
            (level, False)
            for level in reversed(range(self.depth))
            if any(row[level][2] for _, row in self.steps)
        ]
        self.moves = [(level, True) for level in range(self.depth)] + up
        self.stages = len(self.moves) + 1

    def copies(self, move):
        level, down = self.moves[move]
        found = []
        for n, (start, row) in enumerate(self.steps):
            for axis, stride, halves, sent, _ in row[: level if down else level + 1]:
                if halves:
                    start = start + across(self.index, axis, stride)[0] * sent
            axis, stride, halves, sent, at = row[level]
            bit, peer = across(self.index, axis, stride)
            slot = self.base + n * self.depth + level
            if down:
                keep = start + bit * sent if halves else start
                give = start + sent - bit * sent if halves else start
                target, ends = self.recv.at[pl.ds(at, sent)], 0
            elif halves:
                keep, give = None, start
                target, ends = self.buf.at[pl.ds(give, sent)], 2
            else:
                continue
            copy = pltpu.make_async_remote_copy(
                self.buf.at[pl.ds(give, sent)], target,
                self.sems.at[ends, slot], self.sems.at[ends + 1, slot],
                device_id=peer, device_id_type=MESH,
            )
            found.append((copy, halves, keep, sent, at, slot, peer))
        return found

    def tick(self, stage):
        if stage > 0:
            down = self.moves[stage - 1][1]
            for copy, halves, keep, sent, at, slot, peer in self.copies(stage - 1):
                copy.wait()
                if not down:
                    continue
                if halves:
                    pl.semaphore_signal(
                        self.free.at[slot], inc=1, device_id=peer, device_id_type=MESH
                    )
                mine = self.buf[pl.ds(keep, sent)].astype(F32)
                self.buf[pl.ds(keep, sent)] = (
                    mine + self.recv[pl.ds(at, sent)].astype(F32)
                ).astype(BF16)
        if stage < len(self.moves):
            down = self.moves[stage][1]
            for copy, halves, keep, sent, at, slot, peer in self.copies(stage):
                if not down:
                    pl.semaphore_wait(self.free.at[slot], 1)
                copy.start()


def reduction_scratch(sizes, orders, width):
    depth = len(orders[0])
    return (
        [pltpu.VMEM((s, TILE, width), BF16) for s in sizes]
        + [pltpu.VMEM((plan(s, orders)[1], TILE, width), BF16) for s in sizes]
        + [
            pltpu.SemaphoreType.DMA((4, len(sizes) * 2 * depth)),
            pltpu.SemaphoreType.REGULAR((len(sizes) * 2 * depth,)),
        ]
    )


def reductions(refs, count, orders, index):
    bufs, recvs, (sems, free) = refs[:count], refs[count : 2 * count], refs[2 * count :]
    return [
        Reduction(bufs[n], recvs[n], sems, free, n * 2 * len(orders[0]), orders, index)
        for n in range(count)
    ]


def tiles(value):
    return value.reshape(value.shape[0] // TILE, TILE, value.shape[1])


EARLY = 2


def front_kernel(
    count, chunks, group, orders,
    x_in, mem_in, mem_cot_in, wq_in, wk_in, wv_in, wsq_in, wo_in, wup_in, wdown_in, cot_in,
    lengths, pad, gain1, gain2, gain3,
    out, res_out, low_out, q_out, k_out, kt_out, v_out, vt_out, d_out, late, *rest,
):
    sums, rest = rest[:EARLY], rest[EARLY:]
    (lse, inner, slot_k, slot_kt, slot_v, slot_q, slot_qt, mem, stats, dwo_out, dgain) = rest[:11]
    (
        x, cot, low, q_t, k, k_t, v, v_t, o_t, second, second_t, cot_t, ffn, grad,
        wq, wk, wv, wsq, wo, wup, wdown, slot_vt, bias, dwo, dwup, dwdown_t, out_low, late_buf, doc,
        loads, stores, gathers, late_sems,
    ) = rest[11:44]
    index = here()
    work = reductions(rest[44:], EARLY, orders, index)
    pairs = H // 2

    def load(n):
        pairs_of = (
            [(x_in.at[i], x.at[i]) for i in range(count)]
            + [(wq_in, wq), (wk_in, wk), (wv_in, wv), (wsq_in, wsq), (wo_in, wo)]
            + [(cot_in.at[i], cot.at[i]) for i in range(count)]
            + [
                (wup_in.at[:, c * SEG : (c + 1) * SEG], wup.at[c]) for c in range(chunks)
            ]
            + [(wdown_in.at[c], wdown.at[c]) for c in range(chunks)]
            + [(mem_in, mem.at[index["slot"], 0]), (mem_cot_in, mem.at[index["slot"], 1])]
        )
        return pltpu.make_async_copy(*pairs_of[n], loads.at[n])

    weights_at = count
    cot_at = count + 5
    up_at = 2 * count + 5
    down_at = up_at + chunks
    mem_at = down_at + chunks
    order = (
        [mem_at, mem_at + 1, 0, weights_at, weights_at + 1, weights_at + 2]
        + list(range(1, count))
        + [weights_at + 3, weights_at + 4]
        + list(range(cot_at, mem_at))
    )
    for n in order:
        load(n).start()
    greet(orders, index, group)
    load(mem_at).wait()
    load(mem_at + 1).wait()
    for copy in gather(mem, gathers.at[0], index, group):
        copy.start()
    doc[...] = documents(lengths, index, group, doc.shape[1])
    dwo[...] = jnp.zeros_like(dwo)
    dwup[...] = jnp.zeros_like(dwup)
    dwdown_t[...] = jnp.zeros_like(dwdown_t)
    dgain[...] = jnp.zeros_like(dgain)
    for n in range(weights_at, weights_at + 3):
        load(n).wait()

    kept = ((low, low_out), (q_t, q_out), (k, k_out), (k_t, kt_out), (v, v_out), (v_t, vt_out))

    def keep(n, i):
        source, target = kept[n]
        return pltpu.make_async_copy(source.at[i], target.at[i], stores.at[n, i])

    @pl.loop(0, count)
    def _(i):
        pltpu.make_async_copy(x_in.at[i], x.at[i], loads.at[i]).wait()
        unit, _ = norm(x[i].astype(F32))
        row = (unit * gain1[...]).astype(BF16)
        low[i] = row
        q_t[i] = jnp.transpose((nn(row, wq[...]) * SCALE).astype(BF16)).reshape(q_t.shape[1:])
        key = nn(row, wk[...]).astype(BF16)
        k_t[i] = jnp.transpose(key).reshape(k_t.shape[1:])
        value = nn(row, wv[...]).astype(BF16)
        v_t[i] = jnp.transpose(value).reshape(v_t.shape[1:])
        for p in range(pairs):
            k[i, p] = key[:, two(p)]
            v[i, p] = value[:, two(p)]
        for n in range(len(kept)):
            keep(n, i).start()

    for copy in gather(mem, gathers.at[0], index, group):
        copy.wait()
    load(weights_at + 3).wait()
    load(weights_at + 4).wait()
    slots = group * mem.shape[2]
    unit, _ = norm(mem[:, 0].reshape(slots, mem.shape[3]).astype(F32))
    row = (unit * gain3[...]).astype(BF16)
    sk = nn(row, wk[...]).astype(BF16)
    sv = nn(row, wv[...]).astype(BF16)
    sq = (nn(row, wsq[...]) * SCALE).astype(BF16)
    lane = lax.broadcasted_iota(jnp.int32, (slots, 2 * DH), 1) < DH
    for p in range(pairs):
        slot_k[p], slot_v[p], slot_q[p] = sk[:, two(p)], sv[:, two(p)], sq[:, two(p)]
        slot_kt[p] = jnp.transpose(sk[:, two(p)])
        slot_vt[p] = jnp.transpose(sv[:, two(p)])
        slot_qt[p] = jnp.transpose(sq[:, two(p)])
        parts = []
        for odd in range(2):
            mine = head_lanes(sq[:, two(p)], odd)
            cs = [
                nn(mine, k_t[i, p]) + jnp.where(pad[:, i * SEG : (i + 1) * SEG] > 0, 0.0, FILL)
                for i in range(count)
            ]
            top = jnp.max(cs[0], 1, keepdims=True)
            for c in cs[1:]:
                top = jnp.maximum(top, jnp.max(c, 1, keepdims=True))
            total, acc = 0.0, 0.0
            for i, c in enumerate(cs):
                w = jnp.exp(c - top)
                total = total + jnp.sum(w, 1, keepdims=True)
                acc = acc + nn(w.astype(BF16), v[i, p])
            parts.append((acc, top, total))
        for n in range(3):
            stats[index["slot"], n, :, two(p)] = jnp.where(lane, parts[0][n], parts[1][n])
    for copy in gather(stats, gathers.at[1], index, group):
        copy.start()

    @pl.loop(0, count)
    def _(i):
        cols = pl.ds(pl.multiple_of(i * SEG, SEG), SEG)
        bias[...] = segment_bias(doc[:, cols], pad[:, cols])
        for h in range(H):
            p, odd = h // 2, h % 2
            own = one(odd)
            qm = head_rows(q_t[i, p], odd)
            for lo, hi in BLOCKS:
                qb = qm[:, lo:hi]
                s = nn(k[i, p, :hi, :], qb) + bias[:hi, lo:hi]
                sm = nn(slot_k[p], qb)
                top = jnp.maximum(jnp.max(s, 0, keepdims=True), jnp.max(sm, 0, keepdims=True))
                e = jnp.exp(s - top)
                em = jnp.exp(sm - top)
                total = jnp.sum(e, 0, keepdims=True) + jnp.sum(em, 0, keepdims=True)
                o = nn(v_t[i, p, own, :hi], e.astype(BF16)) + nn(slot_vt[p, own, :], em.astype(BF16))
                o_t[i, one(h), lo:hi] = (o / total).astype(BF16)
                lse[i, p, odd : odd + 1, lo:hi] = top + jnp.log(total)
        res = x[i].astype(F32) + nn(jnp.transpose(o_t[i]), wo[...])
        ffn[i] = res
        grad[i] = jnp.zeros_like(res)
        unit, _ = norm(res)
        row = (unit * gain2[...]).astype(BF16)
        second[i] = row
        second_t[i] = jnp.transpose(row)
        pltpu.make_async_copy(cot_in.at[i], cot.at[i], loads.at[cot_at + i]).wait()
        cot_t[i] = jnp.transpose(cot[i])

    last = chunks * count + count - 1

    def summed(n, stage):
        work[n].tick(stage)
        if stage == work[n].stages - 1:
            pltpu.make_async_copy(work[n].buf, sums[n], late_sems.at[n]).start()

    events = [
        ((n + 1) * count - 1 + stage, summed, (n, stage))
        for n in range(EARLY)
        for stage in range(work[n].stages)
    ]

    @pl.loop(0, chunks * count)
    def _(step):
        c = step // count
        i = step % count

        @pl.when(i == 0)
        def _():
            for n in range(chunks):

                @pl.when(c == n)
                def _():
                    load(up_at + n).wait()
                    load(down_at + n).wait()

        act, slope = gelu_pair(nn(second[i], wup[c]))
        act = act.astype(BF16)
        ffn[i] += nn(act, wdown[c])
        up_grad = (nt(cot[i], wdown[c]) * slope).astype(BF16)
        dwdown_t[...] += nn(cot_t[i], act)
        dwup[...] += nn(second_t[i], up_grad)
        grad[i] += nt(up_grad, wup[c])

        half = SEG // TILE
        for n in range(chunks):

            @pl.when((i == count - 1) & (c == n))
            def _():
                target = work[n].buf if n < EARLY else late_buf.at[n - EARLY]
                target[:half] = tiles(dwup[...].astype(BF16))
                target[half:] = tiles(jnp.transpose(dwdown_t[...].astype(BF16)))
                dwup[...] = jnp.zeros_like(dwup)
                dwdown_t[...] = jnp.zeros_like(dwdown_t)
                if n >= EARLY:
                    pltpu.make_async_copy(target, late.at[n - EARLY], late_sems.at[n]).start()

        run_events(step, last, [e for e in events if e[0] < chunks * count])

    def finish(n, i):
        source, target = ((out_low, out), (grad, res_out), (o_t, d_out))[n]
        return pltpu.make_async_copy(source.at[i], target.at[i], stores.at[len(kept) + n, i])

    @pl.loop(0, count)
    def _(i):
        res = x[i].astype(F32) + nn(jnp.transpose(o_t[i]), wo[...])
        unit, inverse = norm(res)
        out_low[i] = ffn[i].astype(BF16)
        back, gain_part = norm_back(grad[i], unit, inverse, gain2[...])
        dgain[...] += gain_part
        back = back + cot[i].astype(F32)
        grad[i] = back
        row = back.astype(BF16)
        dwo[...] += nn(o_t[i], row)
        d = nt(wo[...], row).astype(BF16)
        prod = d.astype(F32) * o_t[i].astype(F32)
        for h in range(H):
            inner[i, h // 2, h % 2 : h % 2 + 1, :] = jnp.sum(prod[one(h), :], 0, keepdims=True)
        o_t[i] = d
        for n in range(3):
            finish(n, i).start()
        run_events(i + chunks * count, last, [e for e in events if e[0] >= chunks * count])

    dwo_out[...] = dwo[...].astype(BF16)
    for copy in gather(stats, gathers.at[1], index, group):
        copy.wait()
    for i in range(count):
        for n in range(len(kept)):
            keep(n, i).wait()
        for n in range(3):
            finish(n, i).wait()
    for n in range(EARLY):
        pltpu.make_async_copy(work[n].buf, sums[n], late_sems.at[n]).wait()
    for n in range(EARLY, chunks):
        pltpu.make_async_copy(late_buf.at[n - EARLY], late.at[n - EARLY], late_sems.at[n]).wait()


def update(
    index, stats, mem, slot_q, slot_k, slot_v, wgate, bgate, wwrite,
    new_memory, g_out, g_t, lse, inner_out, sq_acc, sk_acc, sv_acc, direct_out,
    dwgate, dwwrite, dbias, fresh,
):
    group, _, rows, width = mem.shape
    slots = group * rows
    pairs = H // 2
    same = (
        lax.broadcasted_iota(jnp.int32, (width, width), 0) // DH
        == lax.broadcasted_iota(jnp.int32, (width, width), 1) // DH
    ).astype(F32)

    def head_sum(value):
        return nn(value, same, lax.Precision.HIGHEST)

    start = index["slot"] * rows
    row = lax.broadcasted_iota(jnp.int32, (slots, width), 0)
    own = (row >= start) & (row < start + rows)
    sq, sk, sv = (
        jnp.concatenate([r[p] for p in range(pairs)], 1).astype(F32) for r in (slot_q, slot_k, slot_v)
    )
    state = mem[:, 0].reshape(slots, width).astype(F32)
    memory_out = mem[:, 1].reshape(slots, width).astype(F32)
    own_score = head_sum(sq * sk)
    top = own_score
    for n in range(group):
        top = jnp.maximum(top, stats[n, 1])
    power = jnp.exp(own_score - top)
    total = power
    weighted = power.astype(BF16).astype(F32) * sv
    for n in range(group):
        factor = jnp.exp(stats[n, 1] - top)
        total = total + factor * stats[n, 2]
        weighted = weighted + factor * stats[n, 0]
    value = weighted / total
    low = value.astype(BF16)
    gate = jax.nn.sigmoid(nn(low, wgate[...]) + bgate[...])
    written = nn(low, wwrite[...])
    fresh[...] = ((1.0 - gate) * state + gate * written).reshape(fresh.shape)
    new_memory[...] = fresh[index["slot"]]
    gate_grad = memory_out * (written - state) * gate * (1.0 - gate)
    gate_low = gate_grad.astype(BF16)
    written_low = (memory_out * gate).astype(BF16)
    zero = jnp.zeros((slots, width), F32)
    direct_out[...] = jnp.where(own, memory_out * (1.0 - gate), zero)
    mine = jnp.where(own, gate_grad, zero)
    dbias[...] = jnp.sum(mine, 0, keepdims=True)
    low_t = jnp.transpose(low)
    dwgate[...] = tiles(nn(low_t, mine.astype(BF16)).astype(BF16))
    dwwrite[...] = tiles(nn(low_t, jnp.where(own, memory_out * gate, zero).astype(BF16)).astype(BF16))
    g_low = (nt(gate_low, wgate[...]) + nt(written_low, wwrite[...])).astype(BF16)
    g = g_low.astype(F32)
    inner = head_sum(g * value)
    spread = top + jnp.log(total)
    delta = (power / total * (head_sum(g * sv) - inner)).astype(BF16).astype(F32)
    self_q = jnp.where(own, delta * sk, zero)
    self_k = jnp.where(own, delta * sq, zero)
    self_v = jnp.where(own, power.astype(BF16).astype(F32) / total * g, zero)
    for p in range(pairs):
        g_out[p] = g_low[:, two(p)]
        g_t[p] = jnp.transpose(g_low[:, two(p)])
        inner_out[p] = inner[:, two(p)]
        lse[p] = spread[:, two(p)]
        sq_acc[p] = jnp.transpose(self_q[:, two(p)])
        sk_acc[p] = jnp.transpose(self_k[:, two(p)])
        sv_acc[p] = jnp.transpose(self_v[:, two(p)])


def back_kernel(
    count, group, orders, sizes,
    x_in, low_in, q_in, k_in, kt_in, v_in, vt_in, d_in, res_in,
    wq_in, wk_in, wv_in, wsq_in, wgate_in, wwrite_in, late, dwo_in,
    lse, inner, lengths, pad, gain1, mgain, slot_k, slot_kt, slot_v, slot_q, slot_qt, mem, stats, bgate,
    dgain2, *rest,
):
    early = len(sizes)
    input_grad = rest[0]
    sums = rest[1 : 1 + early]
    (
        dwq_out, dwk_out, dwv_out, dwsq_out, gains_out, memory_grad, new_memory,
        x, low, q_t, k, k_t, v, v_t, d_t, res, wq, wk, wv, wsq, wgate, wwrite,
        bias, grads, acc, w_all, sq_acc, sk_acc, sv_acc, g, g_t, wlse, winner, direct, fresh,
        slot_low, dgain, dgain3, dbias, part, part_in, doc, part_sems, block_loads, loads, stores,
    ) = rest[1 + early : 47 + early]
    pairs = H // 2
    index = here()
    work = reductions(rest[47 + early :], early + pairs + 1, orders, index)
    wide = 2 * DH
    third = wo_blocks = wq.shape[0] // TILE

    blocks = (
        (q_in, q_t), (k_in, k), (kt_in, k_t), (v_in, v), (vt_in, v_t), (d_in, d_t), (low_in, low),
        (x_in, x), (res_in, res),
    )
    used = 7

    def block(n, i):
        return pltpu.make_async_copy(blocks[n][0].at[i], blocks[n][1].at[i], block_loads.at[n, i])

    whole = (
        [(wgate_in, wgate), (wwrite_in, wwrite), (wq_in, wq), (wk_in, wk), (wv_in, wv), (wsq_in, wsq)]
        + [(late.at[n], work[n].buf) for n in range(early - 1)]
        + [(dwo_in, work[early - 1].buf.at[:wo_blocks])]
    )

    def load(n):
        return pltpu.make_async_copy(*whole[n], loads.at[n])

    for n in (0, 1):
        load(n).start()
    for n in range(used):
        block(n, 0).start()
    for n in range(2, len(whole)):
        load(n).start()
    for i in range(1, count):
        for n in range(used):
            block(n, i).start()
    for i in range(count):
        for n in range(used, len(blocks)):
            block(n, i).start()
    greet(orders, index, group)
    doc[...] = documents(lengths, index, group, doc.shape[1])
    load(0).wait()
    load(1).wait()
    update(
        index, stats, mem, slot_q, slot_k, slot_v, wgate, bgate, wwrite,
        new_memory, g, g_t, wlse, winner, sq_acc, sk_acc, sv_acc, direct,
        work[early - 1].buf.at[third : 2 * third], work[early - 1].buf.at[2 * third :], dbias, fresh,
    )
    for n in range(2, 6):
        load(n).wait()
    for n in range(pairs):
        for m, w in enumerate((wq, wk, wv)):
            at = (3 * n + m) * wide
            w_all[:, at : at + wide] = w[:, two(n)]
    slots = group * mem.shape[2]
    unit3, inverse3 = norm(mem[:, 0].reshape(slots, mem.shape[3]).astype(F32))
    slot_low[...] = (unit3 * mgain[...]).astype(BF16)
    dgain[...] = jnp.zeros_like(dgain)
    acc[...] = jnp.zeros_like(acc)

    strides = [1 << n for n in reversed(range(group.bit_length() - 1))]

    def scatter(level):
        stride = strides[level]
        start, at = 0, 0
        for s in strides[:level]:
            start = start + across(index, "slot", s)[0] * s
            at += s
        bit, peer = across(index, "slot", stride)
        copy = pltpu.make_async_remote_copy(
            part.at[pl.ds(start + stride - bit * stride, stride)], part_in.at[pl.ds(at, stride)],
            part_sems.at[0, level], part_sems.at[1, level], device_id=peer, device_id_type=MESH,
        )
        return copy, start + bit * stride, at, stride

    def slot_grads(stage):
        if stage == 0:
            unit, inverse = norm(mem[:, 0].reshape(slots, mem.shape[3]).astype(F32))
            grad_t = 0.0
            for p in range(pairs):
                grad_t = (
                    grad_t
                    + nn(wk[:, two(p)], sk_acc[p].astype(BF16))
                    + nn(wv[:, two(p)], sv_acc[p].astype(BF16))
                    + nn(wsq[:, two(p)], (sq_acc[p] * SCALE).astype(BF16))
                )
            back, gain_part = norm_back(jnp.transpose(grad_t), unit, inverse, mgain[...])
            part[...] = (back + direct[...]).reshape(part.shape)
            dgain3[...] = gain_part
        else:
            copy, keep, at, size = scatter(stage - 1)
            copy.wait()
            part[pl.ds(keep, size)] += part_in[pl.ds(at, size)]
        if stage < len(strides):
            scatter(stage)[0].start()
        else:
            memory_grad[...] = part[index["slot"]]

    def gains(stage):
        item = work[early + pairs]
        if stage == 0:
            rows = [jnp.broadcast_to(r[...], (8, dgain.shape[1])) for r in (dgain, dgain3, dgain2, dbias)]
            item.buf[...] = tiles(jnp.concatenate(rows, 0).astype(BF16))
        item.tick(stage)
        if stage == item.stages - 1:
            gains_out[...] = item.buf[...].reshape(gains_out.shape).astype(F32)

    def summed(n, stage):
        item = work[n]
        if n < early and stage == 0:
            load(6 + n).wait()
        item.tick(stage)
        if stage < item.stages - 1:
            return
        if n < early:
            pltpu.make_async_copy(item.buf, sums[n], stores.at[n]).start()
            return
        per = wide // TILE
        for m, out in enumerate((dwq_out, dwk_out, dwv_out, dwsq_out)):
            rows = item.buf[m * per : (m + 1) * per].reshape(wide, out.shape[0])
            out[:, two(n - early)] = jnp.transpose(rows)

    busy = pairs * count
    last = busy + count - 1
    events = []
    for n in range(early):
        events += [(n // 2 + stage, summed, (n, stage)) for stage in range(work[n].stages)]
    for n in range(pairs):
        events += [
            ((n + 1) * count - 1 + stage, summed, (early + n, stage))
            for stage in range(work[early + n].stages)
        ]
    events += [(busy + stage, slot_grads, (stage,)) for stage in range(len(strides) + 1)]
    events += [(last + stage, gains, (stage,)) for stage in range(work[early + pairs].stages)]

    @pl.loop(0, busy)
    def _(step):
        p = step // count
        i = step % count

        @pl.when(p == 0)
        def _():
            for n in range(used):
                block(n, i).wait()
            cols = pl.ds(pl.multiple_of(i * SEG, SEG), SEG)
            bias[i] = segment_bias(doc[:, cols], pad[:, cols])

        cols = pl.ds(pl.multiple_of(i * SEG, SEG), SEG)
        pad_bias = jnp.where(pad[:, cols] > 0, 0.0, FILL)
        for odd in range(2):
            own = one(odd)
            qm = head_rows(q_t[i, p], odd)
            dm = head_rows(d_t[i, p], odd)
            c = nn(head_lanes(slot_q[p], odd), k_t[i, p]) + pad_bias
            share = jnp.exp(c - wlse[p, :, odd * DH : odd * DH + 1])
            dotted = nn(head_lanes(g[p], odd), v_t[i, p])
            change = (share * (dotted - winner[p, :, odd * DH : odd * DH + 1])).astype(BF16)
            dk = nn(slot_qt[p, own, :], change)
            dv = nn(g_t[p, own, :], share.astype(BF16))
            sq_acc[p, own, :] += nt(k_t[i, p, own, :], change)
            for lo, hi in BLOCKS:
                qb = qm[:, lo:hi]
                db = dm[:, lo:hi]
                qh = q_t[i, p, own, lo:hi]
                dh = d_t[i, p, own, lo:hi]
                l = lse[i, p, odd : odd + 1, lo:hi]
                t = inner[i, p, odd : odd + 1, lo:hi]
                e = jnp.exp(nn(k[i, p, :hi, :], qb) + bias[i, :hi, lo:hi] - l)
                em = jnp.exp(nn(slot_k[p], qb) - l)
                ds = (e * (nn(v[i, p, :hi, :], db) - t)).astype(BF16)
                dsm = (em * (nn(slot_v[p], db) - t)).astype(BF16)
                dq = (nn(k_t[i, p, own, :hi], ds) + nn(slot_kt[p, own, :], dsm)) * SCALE
                grads[i, p, own, lo:hi] = dq.astype(BF16)
                dvp = nt(dh, e.astype(BF16))
                dkp = nt(qh, ds)
                if hi < SEG:
                    dvp = jnp.concatenate([dvp, jnp.zeros((DH, SEG - hi), F32)], 1)
                    dkp = jnp.concatenate([dkp, jnp.zeros((DH, SEG - hi), F32)], 1)
                dv = dv + dvp
                dk = dk + dkp
                sv_acc[p, own, :] += nt(dh, em.astype(BF16))
                sk_acc[p, own, :] += nt(qh, dsm)
            grads[i, p, wide + odd * DH : wide + (odd + 1) * DH, :] = dk.astype(BF16)
            grads[i, p, 2 * wide + odd * DH : 2 * wide + (odd + 1) * DH, :] = dv.astype(BF16)
        acc[...] += nn(grads[i, p], low[i])

        @pl.when(i == count - 1)
        def _():
            rows = jnp.concatenate(
                [
                    acc[:wide],
                    acc[wide : 2 * wide] + nn(sk_acc[p].astype(BF16), slot_low[...]),
                    acc[2 * wide :] + nn(sv_acc[p].astype(BF16), slot_low[...]),
                    nn((sq_acc[p] * SCALE).astype(BF16), slot_low[...]),
                ],
                0,
            )
            acc[...] = jnp.zeros_like(acc)
            rows = tiles(rows.astype(BF16))
            for n in range(pairs):

                @pl.when(p == n)
                def _():
                    work[early + n].buf[...] = rows

        run_events(step, last, [e for e in events if e[0] < busy])

    @pl.loop(0, count)
    def _(i):
        block(used, i).wait()
        block(used + 1, i).wait()
        unit, inverse = norm(x[i].astype(F32))
        grad_t = nn(w_all[...], grads[i].reshape(3 * pairs * wide, SEG))
        back, gain_part = norm_back(jnp.transpose(grad_t), unit, inverse, gain1[...])
        dgain[...] += gain_part
        res[i] += back
        pltpu.make_async_copy(res.at[i], input_grad.at[i], block_loads.at[0, i]).start()
        run_events(i + busy, last, [e for e in events if e[0] >= busy])

    for i in range(count):
        pltpu.make_async_copy(res.at[i], input_grad.at[i], block_loads.at[0, i]).wait()
    for n in range(early):
        pltpu.make_async_copy(work[n].buf, sums[n], stores.at[n]).wait()


def widen_kernel(chunks, half, *refs):
    ffn, rest = refs[:chunks], refs[chunks:]
    own, dwq, dwk, dwv, dwsq, layer_in, grad_in, new_in, mem_in, gains_in = rest[:10]
    (
        layer_out, new_out, grad_out, mem_out,
        dwq_out, dwk_out, dwv_out, dwo_out, dwsq_out, dwgate_out, dwwrite_out, dwup_out, dwdown_out,
    ) = rest[10:23]
    gain_outs = rest[23:27]
    layer, grad, slots, gains, low, wide = rest[27:33]
    rows, loads, stores = rest[33:37], rest[37], rest[38]
    count, seg = layer.shape[:2]

    jobs = [(dwq, dwq_out), (dwk, dwk_out), (dwv, dwv_out), (dwsq, dwsq_out)]
    for n, out in enumerate((dwo_out, dwgate_out, dwwrite_out)):
        jobs.append((own.at[n * half : (n + 1) * half], out))
    for c in range(chunks):
        jobs.append((ffn[c].at[:half], dwup_out.at[:, c * seg : (c + 1) * seg]))
        jobs.append((ffn[c].at[half:], dwdown_out.at[c * seg : (c + 1) * seg, :]))
    passed = [(gains_in, gains, None)]
    passed += [(new_in, slots.at[0], new_out), (mem_in, slots.at[1], mem_out)]
    for i in range(count):
        passed += [
            (grad_in.at[i], grad.at[i], grad_out.at[i]),
            (layer_in.at[i], layer.at[i], layer_out.at[i]),
        ]
    moves = [(source, low.at[n], wide.at[n], target) for n, (source, target) in enumerate(jobs)]
    todo = []
    for n in range(max(len(moves), len(passed))):
        todo += moves[n : n + 1] + passed[n : n + 1]
    copies = [pltpu.make_async_copy(t[0], t[1], loads.at[n]) for n, t in enumerate(todo)]
    for copy in copies:
        copy.start()
    sent = []

    def send(source, target):
        copy = pltpu.make_async_copy(source, target, stores.at[len(sent)])
        copy.start()
        sent.append(copy)

    for copy, t in zip(copies, todo):
        copy.wait()
        if len(t) == 4:
            _, narrow, full, target = t
            per = 4

            @pl.loop(0, half // per)
            def _(b):
                at = pl.ds(pl.multiple_of(b * per * TILE, per * TILE), per * TILE)
                full[at, :] = narrow[pl.ds(b * per, per)].reshape(per * TILE, full.shape[1]).astype(F32)

            send(full, target)
        elif t[2] is None:
            for n, at in enumerate((0, 16, 8, 24)):
                rows[n][...] = gains[at : at + 1, :]
                send(rows[n], gain_outs[n])
        else:
            send(t[1], t[2])
    for copy in sent:
        copy.wait()


def struct(shape, dtype):
    return jax.ShapeDtypeStruct(shape, dtype)


def params(collective_id):
    return pltpu.CompilerParams(
        vmem_limit_bytes=63 << 20, collective_id=collective_id, has_side_effects=True
    )


def body(
    tokens,
    memory,
    pad_mask,
    doc_lengths,
    first_gain,
    query_weight,
    key_weight,
    value_weight,
    out_weight,
    second_gain,
    up_weight,
    down_weight,
    memory_gain,
    slot_query_weight,
    gate_weight,
    gate_bias,
    write_weight,
    out_cotangent,
    memory_cotangent,
):
    rows, width = tokens.shape
    hidden = up_weight.shape[1]
    count = rows // SEG
    chunks = hidden // SEG
    pairs = H // 2
    two_heads = 2 * DH
    slots_here = memory.shape[1]
    group = lax.axis_size("slot")
    slots = slots_here * group
    pad = pad_mask[None, :]
    gain1, gain2, gain3 = (g[None, :] for g in (first_gain, second_gain, memory_gain))
    orders = bit_orders({"dp": lax.axis_size("dp"), "slot": group})

    anywhere = pl.BlockSpec(memory_space=pl.ANY)
    vm = pl.BlockSpec(memory_space=pltpu.VMEM)
    sm = pl.BlockSpec(memory_space=pltpu.SMEM)
    tokens = tokens.reshape(count, SEG, width)
    segments = (count, SEG, width)
    by_rows = (count, pairs, SEG, two_heads)
    by_lanes = (count, pairs, two_heads, SEG)
    square = (width, width)
    blocks = 2 * SEG // TILE
    half = SEG // TILE
    slot_tall, slot_wide = (pairs, slots, two_heads), (pairs, two_heads, slots)
    per_head = (count, pairs, 2, SEG)
    outs = pl.pallas_call(
        lambda *refs: front_kernel(count, chunks, group, orders, *refs),
        in_specs=[anywhere] * 11 + [sm] + [vm] * 4,
        out_specs=[anywhere] * (10 + EARLY) + [vm] * 11,
        out_shape=[
            struct(segments, BF16), struct(segments, F32), struct(segments, BF16),
            struct(by_lanes, BF16), struct(by_rows, BF16), struct(by_lanes, BF16),
            struct(by_rows, BF16), struct(by_lanes, BF16), struct((count, width, SEG), BF16),
            struct((chunks - EARLY, blocks, TILE, width), BF16),
        ]
        + [struct((blocks, TILE, width), BF16)] * EARLY
        + [
            struct(per_head, F32), struct(per_head, F32), struct(slot_tall, BF16),
            struct(slot_wide, BF16), struct(slot_tall, BF16), struct(slot_tall, BF16),
            struct(slot_wide, BF16), struct((group, 2, slots_here, width), BF16),
            struct((group, 3, slots, width), F32), struct(square, BF16), struct((1, width), F32),
        ],
        scratch_shapes=[
            pltpu.VMEM(segments, BF16), pltpu.VMEM(segments, BF16), pltpu.VMEM(segments, BF16),
            pltpu.VMEM(by_lanes, BF16), pltpu.VMEM(by_rows, BF16), pltpu.VMEM(by_lanes, BF16),
            pltpu.VMEM(by_rows, BF16), pltpu.VMEM(by_lanes, BF16),
            pltpu.VMEM((count, width, SEG), BF16), pltpu.VMEM(segments, BF16),
            pltpu.VMEM((count, width, SEG), BF16), pltpu.VMEM((count, width, SEG), BF16),
            pltpu.VMEM(segments, F32), pltpu.VMEM(segments, F32),
            pltpu.VMEM(square, BF16), pltpu.VMEM(square, BF16), pltpu.VMEM(square, BF16),
            pltpu.VMEM(square, BF16), pltpu.VMEM(square, BF16),
            pltpu.VMEM((chunks, width, SEG), BF16), pltpu.VMEM((chunks, SEG, width), BF16),
            pltpu.VMEM(slot_wide, BF16), pltpu.VMEM((SEG, SEG), F32), pltpu.VMEM(square, F32),
            pltpu.VMEM((width, SEG), F32), pltpu.VMEM((width, SEG), F32),
            pltpu.VMEM(segments, BF16), pltpu.VMEM((chunks - EARLY, blocks, TILE, width), BF16),
            pltpu.VMEM((1, rows), F32),
            pltpu.SemaphoreType.DMA((2 * count + 7 + 2 * chunks,)),
            pltpu.SemaphoreType.DMA((9, count)),
            pltpu.SemaphoreType.DMA((2, 2, group)),
            pltpu.SemaphoreType.DMA((chunks,)),
        ]
        + reduction_scratch([blocks] * EARLY, orders, width),
        compiler_params=params(0),
        name="front",
    )(
        tokens, memory[0], memory_cotangent[0], query_weight, key_weight, value_weight,
        slot_query_weight, out_weight, up_weight, down_weight.reshape(chunks, SEG, width),
        out_cotangent.reshape(segments), doc_lengths, pad, gain1, gain2, gain3,
    )
    layer_out, res_grad, low, q_t, k, k_t, v, v_t, d_t, late = outs[:10]
    early = list(outs[10 : 10 + EARLY])
    (
        lse, inner, slot_k, slot_kt, slot_v, slot_q, slot_qt, mem, stats, dwo, dgain2,
    ) = outs[10 + EARLY :]

    sizes = [blocks] * (chunks - EARLY) + [3 * half]
    n_sum = len(sizes)
    outs = pl.pallas_call(
        lambda *refs: back_kernel(count, group, orders, sizes, *refs),
        in_specs=[anywhere] * 17 + [vm] * 2 + [sm] + [vm] * 12,
        out_specs=[anywhere] * (1 + n_sum) + [vm] * 7,
        out_shape=[struct(segments, F32)]
        + [struct((n, TILE, width), BF16) for n in sizes]
        + [struct(square, BF16)] * 4
        + [
            struct((32, width), F32), struct((slots_here, width), F32), struct((slots_here, width), F32),
        ],
        scratch_shapes=[
            pltpu.VMEM(segments, BF16), pltpu.VMEM(segments, BF16), pltpu.VMEM(by_lanes, BF16),
            pltpu.VMEM(by_rows, BF16), pltpu.VMEM(by_lanes, BF16), pltpu.VMEM(by_rows, BF16),
            pltpu.VMEM(by_lanes, BF16), pltpu.VMEM(by_lanes, BF16), pltpu.VMEM(segments, F32),
            pltpu.VMEM(square, BF16), pltpu.VMEM(square, BF16), pltpu.VMEM(square, BF16),
            pltpu.VMEM(square, BF16), pltpu.VMEM(square, BF16), pltpu.VMEM(square, BF16),
            pltpu.VMEM((count, SEG, SEG), F32), pltpu.VMEM((count, pairs, 3 * two_heads, SEG), BF16),
            pltpu.VMEM((3 * two_heads, width), F32), pltpu.VMEM((width, 3 * width), BF16),
            pltpu.VMEM(slot_wide, F32), pltpu.VMEM(slot_wide, F32), pltpu.VMEM(slot_wide, F32),
            pltpu.VMEM(slot_tall, BF16), pltpu.VMEM(slot_wide, BF16), pltpu.VMEM(slot_tall, F32),
            pltpu.VMEM(slot_tall, F32), pltpu.VMEM((slots, width), F32),
            pltpu.VMEM((group, slots_here, width), F32), pltpu.VMEM((slots, width), BF16),
            pltpu.VMEM((1, width), F32), pltpu.VMEM((1, width), F32), pltpu.VMEM((1, width), F32),
            pltpu.VMEM((group, slots_here, width), F32), pltpu.VMEM((group, slots_here, width), F32),
            pltpu.VMEM((1, rows), F32),
            pltpu.SemaphoreType.DMA((2, group)), pltpu.SemaphoreType.DMA((9, count)),
            pltpu.SemaphoreType.DMA((6 + n_sum,)), pltpu.SemaphoreType.DMA((n_sum,)),
        ]
        + reduction_scratch(sizes + [4 * two_heads // TILE] * pairs + [2], orders, width),
        compiler_params=params(1),
        name="back",
    )(
        tokens, low, q_t, k, k_t, v, v_t, d_t.reshape(by_lanes), res_grad,
        query_weight, key_weight, value_weight, slot_query_weight, gate_weight, write_weight,
        late, tiles(dwo),
        lse, inner, doc_lengths, pad, gain1, gain3, slot_k, slot_kt, slot_v, slot_q, slot_qt, mem, stats,
        gate_bias[None, :], dgain2,
    )
    input_grad = outs[0]
    sums = list(outs[1 : 1 + n_sum])
    dwq, dwk, dwv, dwsq, gains, memory_grad, new_memory = outs[1 + n_sum :]
    ffn = early + sums[:-1]
    low_jobs = 7 + 2 * chunks
    outs = pl.pallas_call(
        lambda *refs: widen_kernel(chunks, half, *refs),
        in_specs=[anywhere] * (chunks + 10),
        out_specs=[anywhere] * 17,
        out_shape=[
            struct(segments, BF16), struct((slots_here, width), F32), struct(segments, F32),
            struct((slots_here, width), F32),
        ]
        + [struct(square, F32)] * 7
        + [struct((width, hidden), F32), struct((hidden, width), F32)]
        + [struct((1, width), F32)] * 4,
        scratch_shapes=[
            pltpu.VMEM(segments, BF16), pltpu.VMEM(segments, F32),
            pltpu.VMEM((2, slots_here, width), F32), pltpu.VMEM((32, width), F32),
            pltpu.VMEM((low_jobs, half, TILE, width), BF16), pltpu.VMEM((low_jobs, width, width), F32),
        ]
        + [pltpu.VMEM((1, width), F32)] * 4
        + [
            pltpu.SemaphoreType.DMA((2 * count + 3 + low_jobs,)),
            pltpu.SemaphoreType.DMA((2 * count + 6 + low_jobs,)),
        ],
        compiler_params=pltpu.CompilerParams(vmem_limit_bytes=63 << 20),
        name="widen",
    )(
        *ffn, sums[-1], tiles(dwq), tiles(dwk), tiles(dwv), tiles(dwsq),
        layer_out, input_grad, new_memory, memory_grad, gains,
    )
    layer_out, new_memory, input_grad, memory_grad = outs[:4]
    dwq, dwk, dwv, dwo, dwsq, dwgate, dwwrite, dwup, dwdown = outs[4:13]
    gain1, gain2, gain3, bias = (r[0] for r in outs[13:])
    return (
        layer_out.reshape(rows, width), new_memory[None], input_grad.reshape(rows, width),
        memory_grad[None], gain1, dwq, dwk, dwv, dwo, gain2, dwup, dwdown, gain3, dwsq, dwgate,
        bias, dwwrite,
    )


def solution(mesh):
    token = P(("dp", "slot"), None)
    slot = P("dp", "slot", None)
    in_specs = (
        (token, slot, P(("dp", "slot"))) + (P(),) * 14 + (token, slot)
    )
    out_specs = (token, slot, token, slot) + (P(),) * 13
    return jax.shard_map(body, mesh=mesh, in_specs=in_specs, out_specs=out_specs, check_vma=False)
```

```python
import jax
import jax.numpy as jnp
from jax import lax
from jax.experimental import pallas as pl
from jax.experimental.pallas import tpu as pltpu
from jax.sharding import PartitionSpec as P

H = 8
DH = 64
SEG = 512
HALF = 256
FILL = -1e30
EPS = 1e-05
SCALE = DH ** (-0.5)
F32 = jnp.float32
BF16 = jnp.bfloat16

TAIL = (
    0.11962928145668905,
    0.12075423000729175,
    0.09991172819365436,
    0.12856765411993218,
    -0.053695489964182386,
    0.20636694099934239,
    -0.15721125090545032,
    0.035676834162404004,
)


def nn(a, b, precision=None):
    return lax.dot_general(
        a, b, (((1,), (0,)), ((), ())), preferred_element_type=F32, precision=precision
    )


def nt(a, b):
    return lax.dot_general(a, b, (((1,), (1,)), ((), ())), preferred_element_type=F32)


def norm(value):
    center = value - jnp.mean(value, -1, keepdims=True)
    inverse = lax.rsqrt(jnp.mean(center * center, -1, keepdims=True) + EPS)
    return center * inverse, inverse


def norm_back(grad, unit, inverse, gain):
    inner = grad * gain
    value_grad = inverse * (
        inner
        - jnp.mean(inner, -1, keepdims=True)
        - unit * jnp.mean(inner * unit, -1, keepdims=True)
    )
    return value_grad, jnp.sum(grad * unit, 0, keepdims=True)


def gelu_pair(x):
    t = 1.0 / (1.0 + 0.3 * jnp.abs(x))
    poly = TAIL[7]
    for c in TAIL[6::-1]:
        poly = poly * t + c
    bell = jnp.exp(-0.5 * (x * x))
    tail = bell * (poly * t)
    cdf = jnp.where(x >= 0, 1.0 - tail, tail)
    return x * cdf, cdf + x * (bell * 0.3989422804014327)


def segment_bias(doc_row, pad_row):
    code = jnp.where(pad_row > 0, doc_row, -1.0)
    key_code = jnp.transpose(jnp.broadcast_to(code, (SEG, SEG)))
    rows = lax.broadcasted_iota(jnp.int32, (SEG, SEG), 0)
    columns = lax.broadcasted_iota(jnp.int32, (SEG, SEG), 1)
    seen = (rows <= columns) & (key_code == doc_row)
    return jnp.where(seen, 0.0, FILL)


def documents(lengths, index, group, rows):
    place = lax.broadcasted_iota(jnp.int32, (1, rows), 1)
    place = place + (index["dp"] * group + index["slot"]) * rows
    end, doc = 0, jnp.zeros((1, rows), F32)
    for n in range(lengths.shape[0]):
        end = end + lengths[n]
        doc = doc + jnp.where(place >= end, 1.0, 0.0)
    return doc


def head_rows(pair, odd):
    zero = jnp.zeros((DH, pair.shape[1]), pair.dtype)
    if odd:
        return jnp.concatenate([zero, pair[DH:]], 0)
    return jnp.concatenate([pair[:DH], zero], 0)


def head_lanes(pair, odd):
    lane = lax.broadcasted_iota(jnp.int32, pair.shape, 1)
    keep = (lane >= DH) if odd else (lane < DH)
    return jnp.where(keep, pair, jnp.zeros_like(pair))


def two(p):
    return slice(p * 2 * DH, (p + 1) * 2 * DH)


def one(h):
    return slice(h * DH, (h + 1) * DH)


BLOCKS = ((0, HALF), (HALF, SEG))


TILE = 16
MESH = pl.DeviceIdType.MESH


PARTS = 2
WHOLE = 2


def bit_orders(sizes):
    dp = [("dp", 1 << n) for n in range(sizes["dp"].bit_length() - 1)]
    slot = [("slot", 1 << n) for n in range(sizes["slot"].bit_length() - 1)]
    first, other = slot[:1], slot[1:]
    return first + other + dp, first + dp[:1] + other + dp[1:]


def plan(blocks, orders):
    parts = min(blocks, len(orders))
    steps, recv = [], 0
    for n, order in enumerate(orders[:parts]):
        size, row = blocks // parts, []
        for level, (axis, stride) in enumerate(order):
            halves = size % 2 == 0 and level < len(order) - WHOLE
            sent = size // 2 if halves else size
            row.append((axis, stride, halves, sent, recv))
            recv += sent
            size = sent
        steps.append((n * (blocks // parts), row))
    return steps, recv


def here():
    return {"dp": lax.axis_index("dp"), "slot": lax.axis_index("slot")}


def across(index, axis, stride):
    bit = (index[axis] // stride) % 2
    peer = dict(index)
    peer[axis] = index[axis] + stride - 2 * bit * stride
    return bit, (peer["dp"], peer["slot"])


def ring(index, offset, group):
    return (index["dp"], (index["slot"] + offset) % group)


def greet(orders, index, group):
    barrier = pltpu.get_barrier_semaphore()
    peers = [ring(index, n, group) for n in range(1, group)] + [
        across(index, axis, stride)[1] for axis, stride in orders[0] if axis == "dp"
    ]
    for peer in peers:
        pl.semaphore_signal(barrier, inc=1, device_id=peer, device_id_type=MESH)
    pl.semaphore_wait(barrier, len(peers))


def gather(ref, sems, index, group):
    own = ref.at[index["slot"]]
    return [
        pltpu.make_async_remote_copy(
            own, own, sems.at[0, n], sems.at[1, n],
            device_id=ring(index, n, group), device_id_type=MESH,
        )
        for n in range(1, group)
    ]


def run_events(step, last, events):
    events = sorted(events, key=lambda event: event[0])
    for when in range(last + 1):
        todo = [e for e in events if e[0] == when or (when == last and e[0] > last)]
        if not todo:
            continue

        @pl.when(step == when)
        def _():
            for _, act, args in todo:
                act(*args)


class Reduction:
    def __init__(self, buf, recv, sems, free, base, orders, index):
        self.buf, self.recv, self.sems, self.free = buf, recv, sems, free
        self.base, self.index = base, index
        self.steps, _ = plan(buf.shape[0], orders)
        self.depth = len(orders[0])
        up = [
            (level, False)
            for level in reversed(range(self.depth))
            if any(row[level][2] for _, row in self.steps)
        ]
        self.moves = [(level, True) for level in range(self.depth)] + up
        self.stages = len(self.moves) + 1

    def copies(self, move):
        level, down = self.moves[move]
        found = []
        for n, (start, row) in enumerate(self.steps):
            for axis, stride, halves, sent, _ in row[: level if down else level + 1]:
                if halves:
                    start = start + across(self.index, axis, stride)[0] * sent
            axis, stride, halves, sent, at = row[level]
            bit, peer = across(self.index, axis, stride)
            slot = self.base + n * self.depth + level
            if down:
                keep = start + bit * sent if halves else start
                give = start + sent - bit * sent if halves else start
                target, ends = self.recv.at[pl.ds(at, sent)], 0
            elif halves:
                keep, give = None, start
                target, ends = self.buf.at[pl.ds(give, sent)], 2
            else:
                continue
            copy = pltpu.make_async_remote_copy(
                self.buf.at[pl.ds(give, sent)], target,
                self.sems.at[ends, slot], self.sems.at[ends + 1, slot],
                device_id=peer, device_id_type=MESH,
            )
            found.append((copy, halves, keep, sent, at, slot, peer))
        return found

    def tick(self, stage):
        if stage > 0:
            down = self.moves[stage - 1][1]
            for copy, halves, keep, sent, at, slot, peer in self.copies(stage - 1):
                copy.wait()
                if not down:
                    continue
                if halves:
                    pl.semaphore_signal(
                        self.free.at[slot], inc=1, device_id=peer, device_id_type=MESH
                    )
                mine = self.buf[pl.ds(keep, sent)].astype(F32)
                self.buf[pl.ds(keep, sent)] = (
                    mine + self.recv[pl.ds(at, sent)].astype(F32)
                ).astype(BF16)
        if stage < len(self.moves):
            down = self.moves[stage][1]
            for copy, halves, keep, sent, at, slot, peer in self.copies(stage):
                if not down:
                    pl.semaphore_wait(self.free.at[slot], 1)
                copy.start()


def reduction_scratch(sizes, orders, width):
    depth = len(orders[0])
    return (
        [pltpu.VMEM((s, TILE, width), BF16) for s in sizes]
        + [pltpu.VMEM((plan(s, orders)[1], TILE, width), BF16) for s in sizes]
        + [
            pltpu.SemaphoreType.DMA((4, len(sizes) * PARTS * depth)),
            pltpu.SemaphoreType.REGULAR((len(sizes) * PARTS * depth,)),
        ]
    )


def reductions(refs, count, orders, index):
    bufs, recvs, (sems, free) = refs[:count], refs[count : 2 * count], refs[2 * count :]
    return [
        Reduction(bufs[n], recvs[n], sems, free, n * PARTS * len(orders[0]), orders, index)
        for n in range(count)
    ]


def tiles(value):
    return value.reshape(value.shape[0] // TILE, TILE, value.shape[1])


EARLY = 2


def front_kernel(
    count, chunks, group, orders,
    x_in, mem_in, mem_cot_in, wq_in, wk_in, wv_in, wsq_in, wo_in, wup_in, wdown_in, cot_in,
    lengths, pad, gain1, gain2, gain3,
    out, res_out, low_out, q_out, k_out, kt_out, v_out, vt_out, d_out, late, *rest,
):
    sums, rest = rest[:EARLY], rest[EARLY:]
    (lse, inner, slot_k, slot_kt, slot_v, slot_q, slot_qt, mem, stats, dwo_out, dgain) = rest[:11]
    (
        x, cot, low, q_t, k, k_t, v, v_t, o_t, second, second_t, cot_t, ffn, grad,
        wq, wk, wv, wsq, wo, wup, wdown, slot_vt, bias, dwo, dwup, dwdown_t, out_low, late_buf, doc,
        loads, stores, gathers, late_sems,
    ) = rest[11:44]
    index = here()
    work = reductions(rest[44:], EARLY, orders, index)
    pairs = H // 2

    def load(n):
        pairs_of = (
            [(x_in.at[i], x.at[i]) for i in range(count)]
            + [(wq_in, wq), (wk_in, wk), (wv_in, wv), (wsq_in, wsq), (wo_in, wo)]
            + [(cot_in.at[i], cot.at[i]) for i in range(count)]
            + [
                (wup_in.at[:, c * SEG : (c + 1) * SEG], wup.at[c]) for c in range(chunks)
            ]
            + [(wdown_in.at[c], wdown.at[c]) for c in range(chunks)]
            + [(mem_in, mem.at[index["slot"], 0]), (mem_cot_in, mem.at[index["slot"], 1])]
        )
        return pltpu.make_async_copy(*pairs_of[n], loads.at[n])

    weights_at = count
    cot_at = count + 5
    up_at = 2 * count + 5
    down_at = up_at + chunks
    mem_at = down_at + chunks
    order = (
        [mem_at, mem_at + 1, 0, weights_at, weights_at + 1, weights_at + 2]
        + list(range(1, count))
        + [weights_at + 3, weights_at + 4]
        + list(range(cot_at, mem_at))
    )
    for n in order:
        load(n).start()
    greet(orders, index, group)
    load(mem_at).wait()
    load(mem_at + 1).wait()
    for copy in gather(mem, gathers.at[0], index, group):
        copy.start()
    doc[...] = documents(lengths, index, group, doc.shape[1])
    dwo[...] = jnp.zeros_like(dwo)
    dwup[...] = jnp.zeros_like(dwup)
    dwdown_t[...] = jnp.zeros_like(dwdown_t)
    dgain[...] = jnp.zeros_like(dgain)
    for n in range(weights_at, weights_at + 3):
        load(n).wait()

    kept = ((low, low_out), (q_t, q_out), (k, k_out), (k_t, kt_out), (v, v_out), (v_t, vt_out))

    def keep(n, i):
        source, target = kept[n]
        return pltpu.make_async_copy(source.at[i], target.at[i], stores.at[n, i])

    @pl.loop(0, count)
    def _(i):
        pltpu.make_async_copy(x_in.at[i], x.at[i], loads.at[i]).wait()
        unit, _ = norm(x[i].astype(F32))
        row = (unit * gain1[...]).astype(BF16)
        low[i] = row
        q_t[i] = jnp.transpose((nn(row, wq[...]) * SCALE).astype(BF16)).reshape(q_t.shape[1:])
        key = nn(row, wk[...]).astype(BF16)
        k_t[i] = jnp.transpose(key).reshape(k_t.shape[1:])
        value = nn(row, wv[...]).astype(BF16)
        v_t[i] = jnp.transpose(value).reshape(v_t.shape[1:])
        for p in range(pairs):
            k[i, p] = key[:, two(p)]
            v[i, p] = value[:, two(p)]
        for n in range(len(kept)):
            keep(n, i).start()

    for copy in gather(mem, gathers.at[0], index, group):
        copy.wait()
    load(weights_at + 3).wait()
    load(weights_at + 4).wait()
    slots = group * mem.shape[2]
    unit, _ = norm(mem[:, 0].reshape(slots, mem.shape[3]).astype(F32))
    row = (unit * gain3[...]).astype(BF16)
    sk = nn(row, wk[...]).astype(BF16)
    sv = nn(row, wv[...]).astype(BF16)
    sq = (nn(row, wsq[...]) * SCALE).astype(BF16)
    lane = lax.broadcasted_iota(jnp.int32, (slots, 2 * DH), 1) < DH
    for p in range(pairs):
        slot_k[p], slot_v[p], slot_q[p] = sk[:, two(p)], sv[:, two(p)], sq[:, two(p)]
        slot_kt[p] = jnp.transpose(sk[:, two(p)])
        slot_vt[p] = jnp.transpose(sv[:, two(p)])
        slot_qt[p] = jnp.transpose(sq[:, two(p)])
        parts = []
        for odd in range(2):
            mine = head_lanes(sq[:, two(p)], odd)
            cs = [
                nn(mine, k_t[i, p]) + jnp.where(pad[:, i * SEG : (i + 1) * SEG] > 0, 0.0, FILL)
                for i in range(count)
            ]
            top = jnp.max(cs[0], 1, keepdims=True)
            for c in cs[1:]:
                top = jnp.maximum(top, jnp.max(c, 1, keepdims=True))
            total, acc = 0.0, 0.0
            for i, c in enumerate(cs):
                w = jnp.exp(c - top)
                total = total + jnp.sum(w, 1, keepdims=True)
                acc = acc + nn(w.astype(BF16), v[i, p])
            parts.append((acc, top, total))
        for n in range(3):
            stats[index["slot"], n, :, two(p)] = jnp.where(lane, parts[0][n], parts[1][n])
    for copy in gather(stats, gathers.at[1], index, group):
        copy.start()

    @pl.loop(0, count)
    def _(i):
        cols = pl.ds(pl.multiple_of(i * SEG, SEG), SEG)
        bias[...] = segment_bias(doc[:, cols], pad[:, cols])
        for h in range(H):
            p, odd = h // 2, h % 2
            own = one(odd)
            qm = head_rows(q_t[i, p], odd)
            for lo, hi in BLOCKS:
                qb = qm[:, lo:hi]
                s = nn(k[i, p, :hi, :], qb) + bias[:hi, lo:hi]
                sm = nn(slot_k[p], qb)
                top = jnp.maximum(jnp.max(s, 0, keepdims=True), jnp.max(sm, 0, keepdims=True))
                e = jnp.exp(s - top)
                em = jnp.exp(sm - top)
                total = jnp.sum(e, 0, keepdims=True) + jnp.sum(em, 0, keepdims=True)
                o = nn(v_t[i, p, own, :hi], e.astype(BF16)) + nn(slot_vt[p, own, :], em.astype(BF16))
                o_t[i, one(h), lo:hi] = (o / total).astype(BF16)
                lse[i, p, odd : odd + 1, lo:hi] = top + jnp.log(total)
        res = x[i].astype(F32) + nn(jnp.transpose(o_t[i]), wo[...])
        ffn[i] = res
        grad[i] = jnp.zeros_like(res)
        unit, _ = norm(res)
        row = (unit * gain2[...]).astype(BF16)
        second[i] = row
        second_t[i] = jnp.transpose(row)
        pltpu.make_async_copy(cot_in.at[i], cot.at[i], loads.at[cot_at + i]).wait()
        cot_t[i] = jnp.transpose(cot[i])

    last = chunks * count + count - 1

    def summed(n, stage):
        work[n].tick(stage)
        if stage == work[n].stages - 1:
            pltpu.make_async_copy(work[n].buf, sums[n], late_sems.at[n]).start()

    events = [
        ((n + 1) * count - 1 + ((4 - n) * stage) // 2, summed, (n, stage))
        for n in range(EARLY)
        for stage in range(work[n].stages)
    ]

    @pl.loop(0, chunks * count)
    def _(step):
        c = step // count
        i = step % count

        @pl.when(i == 0)
        def _():
            for n in range(chunks):

                @pl.when(c == n)
                def _():
                    load(up_at + n).wait()
                    load(down_at + n).wait()

        act, slope = gelu_pair(nn(second[i], wup[c]))
        act = act.astype(BF16)
        ffn[i] += nn(act, wdown[c])
        up_grad = (nt(cot[i], wdown[c]) * slope).astype(BF16)
        dwdown_t[...] += nn(cot_t[i], act)
        dwup[...] += nn(second_t[i], up_grad)
        grad[i] += nt(up_grad, wup[c])

        half = SEG // TILE
        for n in range(chunks):

            @pl.when((i == count - 1) & (c == n))
            def _():
                target = work[n].buf if n < EARLY else late_buf.at[n - EARLY]
                target[:half] = tiles(dwup[...].astype(BF16))
                target[half:] = tiles(jnp.transpose(dwdown_t[...].astype(BF16)))
                dwup[...] = jnp.zeros_like(dwup)
                dwdown_t[...] = jnp.zeros_like(dwdown_t)
                if n >= EARLY:
                    pltpu.make_async_copy(target, late.at[n - EARLY], late_sems.at[n]).start()

        run_events(step, last, [e for e in events if e[0] < chunks * count])

    def finish(n, i):
        source, target = ((out_low, out), (grad, res_out), (o_t, d_out))[n]
        return pltpu.make_async_copy(source.at[i], target.at[i], stores.at[len(kept) + n, i])

    @pl.loop(0, count)
    def _(i):
        res = x[i].astype(F32) + nn(jnp.transpose(o_t[i]), wo[...])
        unit, inverse = norm(res)
        out_low[i] = ffn[i].astype(BF16)
        back, gain_part = norm_back(grad[i], unit, inverse, gain2[...])
        dgain[...] += gain_part
        back = back + cot[i].astype(F32)
        grad[i] = back
        row = back.astype(BF16)
        dwo[...] += nn(o_t[i], row)
        d = nt(wo[...], row).astype(BF16)
        prod = d.astype(F32) * o_t[i].astype(F32)
        for h in range(H):
            inner[i, h // 2, h % 2 : h % 2 + 1, :] = jnp.sum(prod[one(h), :], 0, keepdims=True)
        o_t[i] = d
        for n in range(3):
            finish(n, i).start()
        run_events(i + chunks * count, last, [e for e in events if e[0] >= chunks * count])

    dwo_out[...] = dwo[...].astype(BF16)
    for copy in gather(stats, gathers.at[1], index, group):
        copy.wait()
    for i in range(count):
        for n in range(len(kept)):
            keep(n, i).wait()
        for n in range(3):
            finish(n, i).wait()
    for n in range(EARLY):
        pltpu.make_async_copy(work[n].buf, sums[n], late_sems.at[n]).wait()
    for n in range(EARLY, chunks):
        pltpu.make_async_copy(late_buf.at[n - EARLY], late.at[n - EARLY], late_sems.at[n]).wait()


def update(
    index, stats, mem, slot_q, slot_k, slot_v, wgate, bgate, wwrite,
    new_memory, g_out, g_t, lse, inner_out, sq_acc, sk_acc, sv_acc, direct_out,
    dwgate, dwwrite, dbias, fresh,
):
    group, _, rows, width = mem.shape
    slots = group * rows
    pairs = H // 2
    same = (
        lax.broadcasted_iota(jnp.int32, (width, width), 0) // DH
        == lax.broadcasted_iota(jnp.int32, (width, width), 1) // DH
    ).astype(F32)

    def head_sum(value):
        return nn(value, same, lax.Precision.HIGHEST)

    start = index["slot"] * rows
    row = lax.broadcasted_iota(jnp.int32, (slots, width), 0)
    own = (row >= start) & (row < start + rows)
    sq, sk, sv = (
        jnp.concatenate([r[p] for p in range(pairs)], 1).astype(F32) for r in (slot_q, slot_k, slot_v)
    )
    state = mem[:, 0].reshape(slots, width).astype(F32)
    memory_out = mem[:, 1].reshape(slots, width).astype(F32)
    own_score = head_sum(sq * sk)
    top = own_score
    for n in range(group):
        top = jnp.maximum(top, stats[n, 1])
    power = jnp.exp(own_score - top)
    total = power
    weighted = power.astype(BF16).astype(F32) * sv
    for n in range(group):
        factor = jnp.exp(stats[n, 1] - top)
        total = total + factor * stats[n, 2]
        weighted = weighted + factor * stats[n, 0]
    value = weighted / total
    low = value.astype(BF16)
    gate = jax.nn.sigmoid(nn(low, wgate[...]) + bgate[...])
    written = nn(low, wwrite[...])
    fresh[...] = ((1.0 - gate) * state + gate * written).reshape(fresh.shape)
    new_memory[...] = fresh[index["slot"]]
    gate_grad = memory_out * (written - state) * gate * (1.0 - gate)
    gate_low = gate_grad.astype(BF16)
    written_low = (memory_out * gate).astype(BF16)
    zero = jnp.zeros((slots, width), F32)
    direct_out[...] = jnp.where(own, memory_out * (1.0 - gate), zero)
    mine = jnp.where(own, gate_grad, zero)
    dbias[...] = jnp.sum(mine, 0, keepdims=True)
    low_t = jnp.transpose(low)
    dwgate[...] = tiles(nn(low_t, mine.astype(BF16)).astype(BF16))
    dwwrite[...] = tiles(nn(low_t, jnp.where(own, memory_out * gate, zero).astype(BF16)).astype(BF16))
    g_low = (nt(gate_low, wgate[...]) + nt(written_low, wwrite[...])).astype(BF16)
    g = g_low.astype(F32)
    inner = head_sum(g * value)
    spread = top + jnp.log(total)
    delta = (power / total * (head_sum(g * sv) - inner)).astype(BF16).astype(F32)
    self_q = jnp.where(own, delta * sk, zero)
    self_k = jnp.where(own, delta * sq, zero)
    self_v = jnp.where(own, power.astype(BF16).astype(F32) / total * g, zero)
    for p in range(pairs):
        g_out[p] = g_low[:, two(p)]
        g_t[p] = jnp.transpose(g_low[:, two(p)])
        inner_out[p] = inner[:, two(p)]
        lse[p] = spread[:, two(p)]
        sq_acc[p] = jnp.transpose(self_q[:, two(p)])
        sk_acc[p] = jnp.transpose(self_k[:, two(p)])
        sv_acc[p] = jnp.transpose(self_v[:, two(p)])


def back_kernel(
    count, group, orders, sizes,
    x_in, low_in, q_in, k_in, kt_in, v_in, vt_in, d_in, res_in,
    wq_in, wk_in, wv_in, wsq_in, wgate_in, wwrite_in, late, dwo_in,
    lse, inner, lengths, pad, gain1, mgain, slot_k, slot_kt, slot_v, slot_q, slot_qt, mem, stats, bgate,
    dgain2, *rest,
):
    early = len(sizes)
    input_grad = rest[0]
    sums = rest[1 : 1 + early]
    (
        dwq_out, dwk_out, dwv_out, dwsq_out, gains_out, memory_grad, new_memory,
        x, low, q_t, k, k_t, v, v_t, d_t, res, wq, wk, wv, wsq, wgate, wwrite,
        bias, grads, acc, w_all, sq_acc, sk_acc, sv_acc, g, g_t, wlse, winner, direct, fresh,
        slot_low, dgain, dgain3, dbias, part, part_in, doc, part_sems, block_loads, loads, stores,
    ) = rest[1 + early : 47 + early]
    pairs = H // 2
    index = here()
    work = reductions(rest[47 + early :], early + pairs + 1, orders, index)
    wide = 2 * DH
    third = wo_blocks = wq.shape[0] // TILE

    blocks = (
        (q_in, q_t), (k_in, k), (kt_in, k_t), (v_in, v), (vt_in, v_t), (d_in, d_t), (low_in, low),
        (x_in, x), (res_in, res),
    )
    used = 7

    def block(n, i):
        return pltpu.make_async_copy(blocks[n][0].at[i], blocks[n][1].at[i], block_loads.at[n, i])

    whole = (
        [(wgate_in, wgate), (wwrite_in, wwrite), (wq_in, wq), (wk_in, wk), (wv_in, wv), (wsq_in, wsq)]
        + [(late.at[n], work[n].buf) for n in range(early - 1)]
        + [(dwo_in, work[early - 1].buf.at[:wo_blocks])]
    )

    def load(n):
        return pltpu.make_async_copy(*whole[n], loads.at[n])

    for n in (*range(6, 5 + early), 0, 1):
        load(n).start()
    for n in range(used):
        block(n, 0).start()
    for n in (*range(2, 6), 5 + early):
        load(n).start()
    for i in range(1, count):
        for n in range(used):
            block(n, i).start()
    for i in range(count):
        for n in range(used, len(blocks)):
            block(n, i).start()
    greet(orders, index, group)
    for n in range(early - 1):
        load(6 + n).wait()
        work[n].tick(0)
    doc[...] = documents(lengths, index, group, doc.shape[1])
    load(0).wait()
    load(1).wait()
    update(
        index, stats, mem, slot_q, slot_k, slot_v, wgate, bgate, wwrite,
        new_memory, g, g_t, wlse, winner, sq_acc, sk_acc, sv_acc, direct,
        work[early - 1].buf.at[third : 2 * third], work[early - 1].buf.at[2 * third :], dbias, fresh,
    )
    for n in range(early - 1):
        work[n].tick(1)
    for n in range(2, 6):
        load(n).wait()
    for n in range(pairs):
        for m, w in enumerate((wq, wk, wv)):
            at = (3 * n + m) * wide
            w_all[:, at : at + wide] = w[:, two(n)]
    slots = group * mem.shape[2]
    unit3, inverse3 = norm(mem[:, 0].reshape(slots, mem.shape[3]).astype(F32))
    slot_low[...] = (unit3 * mgain[...]).astype(BF16)
    dgain[...] = jnp.zeros_like(dgain)
    acc[...] = jnp.zeros_like(acc)

    strides = [1 << n for n in reversed(range(group.bit_length() - 1))]

    def scatter(level):
        stride = strides[level]
        start, at = 0, 0
        for s in strides[:level]:
            start = start + across(index, "slot", s)[0] * s
            at += s
        bit, peer = across(index, "slot", stride)
        copy = pltpu.make_async_remote_copy(
            part.at[pl.ds(start + stride - bit * stride, stride)], part_in.at[pl.ds(at, stride)],
            part_sems.at[0, level], part_sems.at[1, level], device_id=peer, device_id_type=MESH,
        )
        return copy, start + bit * stride, at, stride

    def slot_grads(stage):
        if stage == 0:
            unit, inverse = norm(mem[:, 0].reshape(slots, mem.shape[3]).astype(F32))
            grad_t = 0.0
            for p in range(pairs):
                grad_t = (
                    grad_t
                    + nn(wk[:, two(p)], sk_acc[p].astype(BF16))
                    + nn(wv[:, two(p)], sv_acc[p].astype(BF16))
                    + nn(wsq[:, two(p)], (sq_acc[p] * SCALE).astype(BF16))
                )
            back, gain_part = norm_back(jnp.transpose(grad_t), unit, inverse, mgain[...])
            part[...] = (back + direct[...]).reshape(part.shape)
            dgain3[...] = gain_part
        else:
            copy, keep, at, size = scatter(stage - 1)
            copy.wait()
            part[pl.ds(keep, size)] += part_in[pl.ds(at, size)]
        if stage < len(strides):
            scatter(stage)[0].start()
        else:
            memory_grad[...] = part[index["slot"]]

    def gains(stage):
        item = work[early + pairs]
        if stage == 0:
            rows = [jnp.broadcast_to(r[...], (8, dgain.shape[1])) for r in (dgain, dgain3, dgain2, dbias)]
            item.buf[...] = tiles(jnp.concatenate(rows, 0).astype(BF16))
        item.tick(stage)
        if stage == item.stages - 1:
            gains_out[...] = item.buf[...].reshape(gains_out.shape).astype(F32)

    def summed(n, stage):
        item = work[n]
        if n == early - 1 and stage == 0:
            load(6 + n).wait()
        item.tick(stage)
        if stage < item.stages - 1:
            return
        if n < early:
            pltpu.make_async_copy(item.buf, sums[n], stores.at[n]).start()
            return
        per = wide // TILE
        for m, out in enumerate((dwq_out, dwk_out, dwv_out, dwsq_out)):
            rows = item.buf[m * per : (m + 1) * per].reshape(wide, out.shape[0])
            out[:, two(n - early)] = jnp.transpose(rows)

    busy = pairs * count
    last = busy + count - 1
    events = []
    for n in range(early - 1):
        events += [
            (1 + n + 3 * (stage - 2) // 2, summed, (n, stage)) for stage in range(2, work[n].stages)
        ]
    events += [
        (1 + 3 * stage // 2, summed, (early - 1, stage)) for stage in range(work[early - 1].stages)
    ]
    for n in range(pairs):
        events += [
            ((n + 1) * count - 1 + (stage if n else 3 * stage // 2), summed, (early + n, stage))
            for stage in range(work[early + n].stages)
        ]
    events += [(busy + stage, slot_grads, (stage,)) for stage in range(len(strides) + 1)]
    events += [(busy + stage, gains, (stage,)) for stage in range(work[early + pairs].stages)]

    @pl.loop(0, busy)
    def _(step):
        p = step // count
        i = step % count

        @pl.when(p == 0)
        def _():
            for n in range(used):
                block(n, i).wait()
            cols = pl.ds(pl.multiple_of(i * SEG, SEG), SEG)
            bias[i] = segment_bias(doc[:, cols], pad[:, cols])

        cols = pl.ds(pl.multiple_of(i * SEG, SEG), SEG)
        pad_bias = jnp.where(pad[:, cols] > 0, 0.0, FILL)
        for odd in range(2):
            own = one(odd)
            qm = head_rows(q_t[i, p], odd)
            dm = head_rows(d_t[i, p], odd)
            c = nn(head_lanes(slot_q[p], odd), k_t[i, p]) + pad_bias
            share = jnp.exp(c - wlse[p, :, odd * DH : odd * DH + 1])
            dotted = nn(head_lanes(g[p], odd), v_t[i, p])
            change = (share * (dotted - winner[p, :, odd * DH : odd * DH + 1])).astype(BF16)
            dk = nn(slot_qt[p, own, :], change)
            dv = nn(g_t[p, own, :], share.astype(BF16))
            sq_acc[p, own, :] += nt(k_t[i, p, own, :], change)
            for lo, hi in BLOCKS:
                qb = qm[:, lo:hi]
                db = dm[:, lo:hi]
                qh = q_t[i, p, own, lo:hi]
                dh = d_t[i, p, own, lo:hi]
                l = lse[i, p, odd : odd + 1, lo:hi]
                t = inner[i, p, odd : odd + 1, lo:hi]
                e = jnp.exp(nn(k[i, p, :hi, :], qb) + bias[i, :hi, lo:hi] - l)
                em = jnp.exp(nn(slot_k[p], qb) - l)
                ds = (e * (nn(v[i, p, :hi, :], db) - t)).astype(BF16)
                dsm = (em * (nn(slot_v[p], db) - t)).astype(BF16)
                dq = (nn(k_t[i, p, own, :hi], ds) + nn(slot_kt[p, own, :], dsm)) * SCALE
                grads[i, p, own, lo:hi] = dq.astype(BF16)
                dvp = nt(dh, e.astype(BF16))
                dkp = nt(qh, ds)
                if hi < SEG:
                    dvp = jnp.concatenate([dvp, jnp.zeros((DH, SEG - hi), F32)], 1)
                    dkp = jnp.concatenate([dkp, jnp.zeros((DH, SEG - hi), F32)], 1)
                dv = dv + dvp
                dk = dk + dkp
                sv_acc[p, own, :] += nt(dh, em.astype(BF16))
                sk_acc[p, own, :] += nt(qh, dsm)
            grads[i, p, wide + odd * DH : wide + (odd + 1) * DH, :] = dk.astype(BF16)
            grads[i, p, 2 * wide + odd * DH : 2 * wide + (odd + 1) * DH, :] = dv.astype(BF16)
        acc[...] += nn(grads[i, p], low[i])

        @pl.when(i == count - 1)
        def _():
            rows = jnp.concatenate(
                [
                    acc[:wide],
                    acc[wide : 2 * wide] + nn(sk_acc[p].astype(BF16), slot_low[...]),
                    acc[2 * wide :] + nn(sv_acc[p].astype(BF16), slot_low[...]),
                    nn((sq_acc[p] * SCALE).astype(BF16), slot_low[...]),
                ],
                0,
            )
            rows = tiles(rows.astype(BF16))
            token = acc[...]
            acc[...] = jnp.zeros_like(acc)
            for n in range(pairs):

                @pl.when(p == n)
                def _():
                    w = jnp.transpose(w_all[:, n * 3 * wide : (n + 1) * 3 * wide]).astype(F32)
                    dgain[...] += jnp.sum(token * w, 0, keepdims=True) / gain1[...]
                    work[early + n].buf[...] = rows

        run_events(step, last, [e for e in events if e[0] < busy])

    @pl.loop(0, count)
    def _(i):
        block(used, i).wait()
        block(used + 1, i).wait()
        unit, inverse = norm(x[i].astype(F32))
        grad_t = nn(w_all[...], grads[i].reshape(3 * pairs * wide, SEG))
        back, _ = norm_back(jnp.transpose(grad_t), unit, inverse, gain1[...])
        res[i] += back
        pltpu.make_async_copy(res.at[i], input_grad.at[i], block_loads.at[0, i]).start()
        run_events(i + busy, last, [e for e in events if e[0] >= busy])

    for i in range(count):
        pltpu.make_async_copy(res.at[i], input_grad.at[i], block_loads.at[0, i]).wait()
    for n in range(early):
        pltpu.make_async_copy(work[n].buf, sums[n], stores.at[n]).wait()


def widen_kernel(chunks, half, *refs):
    ffn, rest = refs[:chunks], refs[chunks:]
    own, dwq, dwk, dwv, dwsq, layer_in, grad_in, new_in, mem_in, gains_in = rest[:10]
    (
        layer_out, new_out, grad_out, mem_out,
        dwq_out, dwk_out, dwv_out, dwo_out, dwsq_out, dwgate_out, dwwrite_out, dwup_out, dwdown_out,
    ) = rest[10:23]
    gain_outs = rest[23:27]
    layer, grad, slots, gains, low, wide = rest[27:33]
    rows, loads, stores = rest[33:37], rest[37], rest[38]
    count, seg = layer.shape[:2]

    jobs = [(dwq, dwq_out), (dwk, dwk_out), (dwv, dwv_out), (dwsq, dwsq_out)]
    for n, out in enumerate((dwo_out, dwgate_out, dwwrite_out)):
        jobs.append((own.at[n * half : (n + 1) * half], out))
    for c in range(chunks):
        jobs.append((ffn[c].at[:half], dwup_out.at[:, c * seg : (c + 1) * seg]))
        jobs.append((ffn[c].at[half:], dwdown_out.at[c * seg : (c + 1) * seg, :]))
    passed = [(gains_in, gains, None)]
    passed += [(new_in, slots.at[0], new_out), (mem_in, slots.at[1], mem_out)]
    for i in range(count):
        passed += [
            (grad_in.at[i], grad.at[i], grad_out.at[i]),
            (layer_in.at[i], layer.at[i], layer_out.at[i]),
        ]
    moves = [(source, low.at[n], wide.at[n], target) for n, (source, target) in enumerate(jobs)]
    todo = []
    for n in range(max(len(moves), len(passed))):
        todo += moves[n : n + 1] + passed[n : n + 1]
    copies = [pltpu.make_async_copy(t[0], t[1], loads.at[n]) for n, t in enumerate(todo)]
    for copy in copies:
        copy.start()
    sent = []

    def send(source, target):
        copy = pltpu.make_async_copy(source, target, stores.at[len(sent)])
        copy.start()
        sent.append(copy)

    for copy, t in zip(copies, todo):
        copy.wait()
        if len(t) == 4:
            _, narrow, full, target = t
            per = 4

            @pl.loop(0, half // per)
            def _(b):
                at = pl.ds(pl.multiple_of(b * per * TILE, per * TILE), per * TILE)
                full[at, :] = narrow[pl.ds(b * per, per)].reshape(per * TILE, full.shape[1]).astype(F32)

            send(full, target)
        elif t[2] is None:
            for n, at in enumerate((0, 16, 8, 24)):
                rows[n][...] = gains[at : at + 1, :]
                send(rows[n], gain_outs[n])
        else:
            send(t[1], t[2])
    for copy in sent:
        copy.wait()


def struct(shape, dtype):
    return jax.ShapeDtypeStruct(shape, dtype)


def params(collective_id):
    return pltpu.CompilerParams(
        vmem_limit_bytes=63 << 20, collective_id=collective_id, has_side_effects=True
    )


def body(
    tokens,
    memory,
    pad_mask,
    doc_lengths,
    first_gain,
    query_weight,
    key_weight,
    value_weight,
    out_weight,
    second_gain,
    up_weight,
    down_weight,
    memory_gain,
    slot_query_weight,
    gate_weight,
    gate_bias,
    write_weight,
    out_cotangent,
    memory_cotangent,
):
    rows, width = tokens.shape
    hidden = up_weight.shape[1]
    count = rows // SEG
    chunks = hidden // SEG
    pairs = H // 2
    two_heads = 2 * DH
    slots_here = memory.shape[1]
    group = lax.axis_size("slot")
    slots = slots_here * group
    pad = pad_mask[None, :]
    gain1, gain2, gain3 = (g[None, :] for g in (first_gain, second_gain, memory_gain))
    orders = bit_orders({"dp": lax.axis_size("dp"), "slot": group})

    anywhere = pl.BlockSpec(memory_space=pl.ANY)
    vm = pl.BlockSpec(memory_space=pltpu.VMEM)
    sm = pl.BlockSpec(memory_space=pltpu.SMEM)
    tokens = tokens.reshape(count, SEG, width)
    segments = (count, SEG, width)
    by_rows = (count, pairs, SEG, two_heads)
    by_lanes = (count, pairs, two_heads, SEG)
    square = (width, width)
    blocks = 2 * SEG // TILE
    half = SEG // TILE
    slot_tall, slot_wide = (pairs, slots, two_heads), (pairs, two_heads, slots)
    per_head = (count, pairs, 2, SEG)
    outs = pl.pallas_call(
        lambda *refs: front_kernel(count, chunks, group, orders, *refs),
        in_specs=[anywhere] * 11 + [sm] + [vm] * 4,
        out_specs=[anywhere] * (10 + EARLY) + [vm] * 11,
        out_shape=[
            struct(segments, BF16), struct(segments, F32), struct(segments, BF16),
            struct(by_lanes, BF16), struct(by_rows, BF16), struct(by_lanes, BF16),
            struct(by_rows, BF16), struct(by_lanes, BF16), struct((count, width, SEG), BF16),
            struct((chunks - EARLY, blocks, TILE, width), BF16),
        ]
        + [struct((blocks, TILE, width), BF16)] * EARLY
        + [
            struct(per_head, F32), struct(per_head, F32), struct(slot_tall, BF16),
            struct(slot_wide, BF16), struct(slot_tall, BF16), struct(slot_tall, BF16),
            struct(slot_wide, BF16), struct((group, 2, slots_here, width), BF16),
            struct((group, 3, slots, width), F32), struct(square, BF16), struct((1, width), F32),
        ],
        scratch_shapes=[
            pltpu.VMEM(segments, BF16), pltpu.VMEM(segments, BF16), pltpu.VMEM(segments, BF16),
            pltpu.VMEM(by_lanes, BF16), pltpu.VMEM(by_rows, BF16), pltpu.VMEM(by_lanes, BF16),
            pltpu.VMEM(by_rows, BF16), pltpu.VMEM(by_lanes, BF16),
            pltpu.VMEM((count, width, SEG), BF16), pltpu.VMEM(segments, BF16),
            pltpu.VMEM((count, width, SEG), BF16), pltpu.VMEM((count, width, SEG), BF16),
            pltpu.VMEM(segments, F32), pltpu.VMEM(segments, F32),
            pltpu.VMEM(square, BF16), pltpu.VMEM(square, BF16), pltpu.VMEM(square, BF16),
            pltpu.VMEM(square, BF16), pltpu.VMEM(square, BF16),
            pltpu.VMEM((chunks, width, SEG), BF16), pltpu.VMEM((chunks, SEG, width), BF16),
            pltpu.VMEM(slot_wide, BF16), pltpu.VMEM((SEG, SEG), F32), pltpu.VMEM(square, F32),
            pltpu.VMEM((width, SEG), F32), pltpu.VMEM((width, SEG), F32),
            pltpu.VMEM(segments, BF16), pltpu.VMEM((chunks - EARLY, blocks, TILE, width), BF16),
            pltpu.VMEM((1, rows), F32),
            pltpu.SemaphoreType.DMA((2 * count + 7 + 2 * chunks,)),
            pltpu.SemaphoreType.DMA((9, count)),
            pltpu.SemaphoreType.DMA((2, 2, group)),
            pltpu.SemaphoreType.DMA((chunks,)),
        ]
        + reduction_scratch([blocks] * EARLY, orders, width),
        compiler_params=params(0),
        name="front",
    )(
        tokens, memory[0], memory_cotangent[0], query_weight, key_weight, value_weight,
        slot_query_weight, out_weight, up_weight, down_weight.reshape(chunks, SEG, width),
        out_cotangent.reshape(segments), doc_lengths, pad, gain1, gain2, gain3,
    )
    layer_out, res_grad, low, q_t, k, k_t, v, v_t, d_t, late = outs[:10]
    early = list(outs[10 : 10 + EARLY])
    (
        lse, inner, slot_k, slot_kt, slot_v, slot_q, slot_qt, mem, stats, dwo, dgain2,
    ) = outs[10 + EARLY :]

    sizes = [blocks] * (chunks - EARLY) + [3 * half]
    n_sum = len(sizes)
    outs = pl.pallas_call(
        lambda *refs: back_kernel(count, group, orders, sizes, *refs),
        in_specs=[anywhere] * 17 + [vm] * 2 + [sm] + [vm] * 12,
        out_specs=[anywhere] * (1 + n_sum) + [vm] * 7,
        out_shape=[struct(segments, F32)]
        + [struct((n, TILE, width), BF16) for n in sizes]
        + [struct(square, BF16)] * 4
        + [
            struct((32, width), F32), struct((slots_here, width), F32), struct((slots_here, width), F32),
        ],
        scratch_shapes=[
            pltpu.VMEM(segments, BF16), pltpu.VMEM(segments, BF16), pltpu.VMEM(by_lanes, BF16),
            pltpu.VMEM(by_rows, BF16), pltpu.VMEM(by_lanes, BF16), pltpu.VMEM(by_rows, BF16),
            pltpu.VMEM(by_lanes, BF16), pltpu.VMEM(by_lanes, BF16), pltpu.VMEM(segments, F32),
            pltpu.VMEM(square, BF16), pltpu.VMEM(square, BF16), pltpu.VMEM(square, BF16),
            pltpu.VMEM(square, BF16), pltpu.VMEM(square, BF16), pltpu.VMEM(square, BF16),
            pltpu.VMEM((count, SEG, SEG), F32), pltpu.VMEM((count, pairs, 3 * two_heads, SEG), BF16),
            pltpu.VMEM((3 * two_heads, width), F32), pltpu.VMEM((width, 3 * width), BF16),
            pltpu.VMEM(slot_wide, F32), pltpu.VMEM(slot_wide, F32), pltpu.VMEM(slot_wide, F32),
            pltpu.VMEM(slot_tall, BF16), pltpu.VMEM(slot_wide, BF16), pltpu.VMEM(slot_tall, F32),
            pltpu.VMEM(slot_tall, F32), pltpu.VMEM((slots, width), F32),
            pltpu.VMEM((group, slots_here, width), F32), pltpu.VMEM((slots, width), BF16),
            pltpu.VMEM((1, width), F32), pltpu.VMEM((1, width), F32), pltpu.VMEM((1, width), F32),
            pltpu.VMEM((group, slots_here, width), F32), pltpu.VMEM((group, slots_here, width), F32),
            pltpu.VMEM((1, rows), F32),
            pltpu.SemaphoreType.DMA((2, group)), pltpu.SemaphoreType.DMA((9, count)),
            pltpu.SemaphoreType.DMA((6 + n_sum,)), pltpu.SemaphoreType.DMA((n_sum,)),
        ]
        + reduction_scratch(sizes + [4 * two_heads // TILE] * pairs + [2], orders, width),
        compiler_params=params(1),
        name="back",
    )(
        tokens, low, q_t, k, k_t, v, v_t, d_t.reshape(by_lanes), res_grad,
        query_weight, key_weight, value_weight, slot_query_weight, gate_weight, write_weight,
        late, tiles(dwo),
        lse, inner, doc_lengths, pad, gain1, gain3, slot_k, slot_kt, slot_v, slot_q, slot_qt, mem, stats,
        gate_bias[None, :], dgain2,
    )
    input_grad = outs[0]
    sums = list(outs[1 : 1 + n_sum])
    dwq, dwk, dwv, dwsq, gains, memory_grad, new_memory = outs[1 + n_sum :]
    ffn = early + sums[:-1]
    low_jobs = 7 + 2 * chunks
    outs = pl.pallas_call(
        lambda *refs: widen_kernel(chunks, half, *refs),
        in_specs=[anywhere] * (chunks + 10),
        out_specs=[anywhere] * 17,
        out_shape=[
            struct(segments, BF16), struct((slots_here, width), F32), struct(segments, F32),
            struct((slots_here, width), F32),
        ]
        + [struct(square, F32)] * 7
        + [struct((width, hidden), F32), struct((hidden, width), F32)]
        + [struct((1, width), F32)] * 4,
        scratch_shapes=[
            pltpu.VMEM(segments, BF16), pltpu.VMEM(segments, F32),
            pltpu.VMEM((2, slots_here, width), F32), pltpu.VMEM((32, width), F32),
            pltpu.VMEM((low_jobs, half, TILE, width), BF16), pltpu.VMEM((low_jobs, width, width), F32),
        ]
        + [pltpu.VMEM((1, width), F32)] * 4
        + [
            pltpu.SemaphoreType.DMA((2 * count + 3 + low_jobs,)),
            pltpu.SemaphoreType.DMA((2 * count + 6 + low_jobs,)),
        ],
        compiler_params=pltpu.CompilerParams(vmem_limit_bytes=63 << 20),
        name="widen",
    )(
        *ffn, sums[-1], tiles(dwq), tiles(dwk), tiles(dwv), tiles(dwsq),
        layer_out, input_grad, new_memory, memory_grad, gains,
    )
    layer_out, new_memory, input_grad, memory_grad = outs[:4]
    dwq, dwk, dwv, dwo, dwsq, dwgate, dwwrite, dwup, dwdown = outs[4:13]
    gain1, gain2, gain3, bias = (r[0] for r in outs[13:])
    return (
        layer_out.reshape(rows, width), new_memory[None], input_grad.reshape(rows, width),
        memory_grad[None], gain1, dwq, dwk, dwv, dwo, gain2, dwup, dwdown, gain3, dwsq, dwgate,
        bias, dwwrite,
    )


def solution(mesh):
    token = P(("dp", "slot"), None)
    slot = P("dp", "slot", None)
    in_specs = (
        (token, slot, P(("dp", "slot"))) + (P(),) * 14 + (token, slot)
    )
    out_specs = (token, slot, token, slot) + (P(),) * 13
    return jax.shard_map(body, mesh=mesh, in_specs=in_specs, out_specs=out_specs, check_vma=False)
```

```python
import jax
import jax.numpy as jnp
from jax import lax
from jax.experimental import pallas as pl
from jax.experimental.pallas import tpu as pltpu
from jax.sharding import PartitionSpec as P

H = 8
DH = 64
SEG = 512
HALF = 256
FILL = -1e30
EPS = 1e-05
SCALE = DH ** (-0.5)
F32 = jnp.float32
BF16 = jnp.bfloat16

TAIL = (
    0.11962928145668905,
    0.12075423000729175,
    0.09991172819365436,
    0.12856765411993218,
    -0.053695489964182386,
    0.20636694099934239,
    -0.15721125090545032,
    0.035676834162404004,
)


def nn(a, b, precision=None):
    return lax.dot_general(
        a, b, (((1,), (0,)), ((), ())), preferred_element_type=F32, precision=precision
    )


def nt(a, b):
    return lax.dot_general(a, b, (((1,), (1,)), ((), ())), preferred_element_type=F32)


def norm(value):
    center = value - jnp.mean(value, -1, keepdims=True)
    inverse = lax.rsqrt(jnp.mean(center * center, -1, keepdims=True) + EPS)
    return center * inverse, inverse


def norm_back(grad, unit, inverse, gain):
    inner = grad * gain
    value_grad = inverse * (
        inner
        - jnp.mean(inner, -1, keepdims=True)
        - unit * jnp.mean(inner * unit, -1, keepdims=True)
    )
    return value_grad, jnp.sum(grad * unit, 0, keepdims=True)


def gelu_pair(x):
    t = 1.0 / (1.0 + 0.3 * jnp.abs(x))
    poly = TAIL[7]
    for c in TAIL[6::-1]:
        poly = poly * t + c
    bell = jnp.exp(-0.5 * (x * x))
    tail = bell * (poly * t)
    cdf = jnp.where(x >= 0, 1.0 - tail, tail)
    return x * cdf, cdf + x * (bell * 0.3989422804014327)


def segment_bias(doc_row, pad_row):
    code = jnp.where(pad_row > 0, doc_row, -1.0)
    key_code = jnp.transpose(jnp.broadcast_to(code, (SEG, SEG)))
    rows = lax.broadcasted_iota(jnp.int32, (SEG, SEG), 0)
    columns = lax.broadcasted_iota(jnp.int32, (SEG, SEG), 1)
    seen = (rows <= columns) & (key_code == doc_row)
    return jnp.where(seen, 0.0, FILL)


def documents(lengths, index, group, rows):
    place = lax.broadcasted_iota(jnp.int32, (1, rows), 1)
    place = place + (index["dp"] * group + index["slot"]) * rows
    end, doc = 0, jnp.zeros((1, rows), F32)
    for n in range(lengths.shape[0]):
        end = end + lengths[n]
        doc = doc + jnp.where(place >= end, 1.0, 0.0)
    return doc


def head_rows(pair, odd):
    zero = jnp.zeros((DH, pair.shape[1]), pair.dtype)
    if odd:
        return jnp.concatenate([zero, pair[DH:]], 0)
    return jnp.concatenate([pair[:DH], zero], 0)


def head_lanes(pair, odd):
    lane = lax.broadcasted_iota(jnp.int32, pair.shape, 1)
    keep = (lane >= DH) if odd else (lane < DH)
    return jnp.where(keep, pair, jnp.zeros_like(pair))


def two(p):
    return slice(p * 2 * DH, (p + 1) * 2 * DH)


def one(h):
    return slice(h * DH, (h + 1) * DH)


BLOCKS = ((0, HALF), (HALF, SEG))


TILE = 16
MESH = pl.DeviceIdType.MESH


PARTS = 2
WHOLE = 2


def bit_orders(sizes):
    dp = [("dp", 1 << n) for n in range(sizes["dp"].bit_length() - 1)]
    slot = [("slot", 1 << n) for n in range(sizes["slot"].bit_length() - 1)]
    first, other = slot[:1], slot[1:]
    return first + other + dp, first + dp[:1] + other + dp[1:]


def plan(blocks, orders):
    parts = min(blocks, len(orders))
    steps, recv = [], 0
    for n, order in enumerate(orders[:parts]):
        size, row = blocks // parts, []
        for level, (axis, stride) in enumerate(order):
            halves = size % 2 == 0 and level < len(order) - WHOLE
            sent = size // 2 if halves else size
            row.append((axis, stride, halves, sent, recv))
            recv += sent
            size = sent
        steps.append((n * (blocks // parts), row))
    return steps, recv


def here():
    return {"dp": lax.axis_index("dp"), "slot": lax.axis_index("slot")}


def across(index, axis, stride):
    bit = (index[axis] // stride) % 2
    peer = dict(index)
    peer[axis] = index[axis] + stride - 2 * bit * stride
    return bit, (peer["dp"], peer["slot"])


def ring(index, offset, group):
    return (index["dp"], (index["slot"] + offset) % group)


def greet(orders, index, group):
    barrier = pltpu.get_barrier_semaphore()
    peers = [ring(index, n, group) for n in range(1, group)] + [
        across(index, axis, stride)[1] for axis, stride in orders[0] if axis == "dp"
    ]
    for peer in peers:
        pl.semaphore_signal(barrier, inc=1, device_id=peer, device_id_type=MESH)
    pl.semaphore_wait(barrier, len(peers))


def gather(ref, sems, index, group):
    own = ref.at[index["slot"]]
    return [
        pltpu.make_async_remote_copy(
            own, own, sems.at[0, n], sems.at[1, n],
            device_id=ring(index, n, group), device_id_type=MESH,
        )
        for n in range(1, group)
    ]


def run_events(step, last, events):
    events = sorted(events, key=lambda event: event[0])
    for when in range(last + 1):
        todo = [e for e in events if e[0] == when or (when == last and e[0] > last)]
        if not todo:
            continue

        @pl.when(step == when)
        def _():
            for _, act, args in todo:
                act(*args)


class Reduction:
    def __init__(self, buf, recv, sems, free, base, orders, index):
        self.buf, self.recv, self.sems, self.free = buf, recv, sems, free
        self.base, self.index = base, index
        self.steps, _ = plan(buf.shape[0], orders)
        self.depth = len(orders[0])
        up = [
            (level, False)
            for level in reversed(range(self.depth))
            if any(row[level][2] for _, row in self.steps)
        ]
        self.moves = [(level, True) for level in range(self.depth)] + up
        self.stages = len(self.moves) + 1

    def copies(self, move):
        level, down = self.moves[move]
        found = []
        for n, (start, row) in enumerate(self.steps):
            for axis, stride, halves, sent, _ in row[: level if down else level + 1]:
                if halves:
                    start = start + across(self.index, axis, stride)[0] * sent
            axis, stride, halves, sent, at = row[level]
            bit, peer = across(self.index, axis, stride)
            slot = self.base + n * self.depth + level
            if down:
                keep = start + bit * sent if halves else start
                give = start + sent - bit * sent if halves else start
                target, ends = self.recv.at[pl.ds(at, sent)], 0
            elif halves:
                keep, give = None, start
                target, ends = self.buf.at[pl.ds(give, sent)], 2
            else:
                continue
            copy = pltpu.make_async_remote_copy(
                self.buf.at[pl.ds(give, sent)], target,
                self.sems.at[ends, slot], self.sems.at[ends + 1, slot],
                device_id=peer, device_id_type=MESH,
            )
            found.append((copy, halves, keep, sent, at, slot, peer))
        return found

    def tick(self, stage):
        if stage > 0:
            down = self.moves[stage - 1][1]
            for copy, halves, keep, sent, at, slot, peer in self.copies(stage - 1):
                copy.wait()
                if not down:
                    continue
                if halves:
                    pl.semaphore_signal(
                        self.free.at[slot], inc=1, device_id=peer, device_id_type=MESH
                    )
                mine = self.buf[pl.ds(keep, sent)].astype(F32)
                self.buf[pl.ds(keep, sent)] = (
                    mine + self.recv[pl.ds(at, sent)].astype(F32)
                ).astype(BF16)
        if stage < len(self.moves):
            down = self.moves[stage][1]
            for copy, halves, keep, sent, at, slot, peer in self.copies(stage):
                if not down:
                    pl.semaphore_wait(self.free.at[slot], 1)
                copy.start()


def reduction_scratch(sizes, orders, width):
    depth = len(orders[0])
    return (
        [pltpu.VMEM((s, TILE, width), BF16) for s in sizes]
        + [pltpu.VMEM((plan(s, orders)[1], TILE, width), BF16) for s in sizes]
        + [
            pltpu.SemaphoreType.DMA((4, len(sizes) * PARTS * depth)),
            pltpu.SemaphoreType.REGULAR((len(sizes) * PARTS * depth,)),
        ]
    )


def reductions(refs, count, orders, index):
    bufs, recvs, (sems, free) = refs[:count], refs[count : 2 * count], refs[2 * count :]
    return [
        Reduction(bufs[n], recvs[n], sems, free, n * PARTS * len(orders[0]), orders, index)
        for n in range(count)
    ]


def tiles(value):
    return value.reshape(value.shape[0] // TILE, TILE, value.shape[1])


EARLY = 2


def front_kernel(
    count, chunks, group, orders,
    x_in, mem_in, mem_cot_in, wq_in, wk_in, wv_in, wsq_in, wo_in, wup_in, wdown_in, cot_in,
    lengths, pad, gain1, gain2, gain3,
    out, res_out, low_out, q_out, k_out, kt_out, v_out, vt_out, d_out, late, *rest,
):
    sums, rest = rest[:EARLY], rest[EARLY:]
    (lse, inner, slot_k, slot_kt, slot_v, slot_q, slot_qt, mem, stats, dwo_out, dgain) = rest[:11]
    (
        x, cot, low, q_t, k, k_t, v, v_t, o_t, second, second_t, cot_t, ffn, grad,
        wq, wk, wv, wsq, wo, wup, wdown, slot_vt, bias, dwo, dwup, dwdown_t, out_low, late_buf, doc,
        loads, stores, gathers, late_sems,
    ) = rest[11:44]
    index = here()
    work = reductions(rest[44:], EARLY, orders, index)
    pairs = H // 2

    def load(n):
        pairs_of = (
            [(x_in.at[i], x.at[i]) for i in range(count)]
            + [(wq_in, wq), (wk_in, wk), (wv_in, wv), (wsq_in, wsq), (wo_in, wo)]
            + [(cot_in.at[i], cot.at[i]) for i in range(count)]
            + [
                (wup_in.at[:, c * SEG : (c + 1) * SEG], wup.at[c]) for c in range(chunks)
            ]
            + [(wdown_in.at[c], wdown.at[c]) for c in range(chunks)]
            + [(mem_in, mem.at[index["slot"], 0]), (mem_cot_in, mem.at[index["slot"], 1])]
        )
        return pltpu.make_async_copy(*pairs_of[n], loads.at[n])

    weights_at = count
    cot_at = count + 5
    up_at = 2 * count + 5
    down_at = up_at + chunks
    mem_at = down_at + chunks
    order = (
        [mem_at, mem_at + 1, 0, weights_at, weights_at + 1, weights_at + 2]
        + list(range(1, count))
        + [weights_at + 3, weights_at + 4]
        + list(range(cot_at, mem_at))
    )
    for n in order:
        load(n).start()
    greet(orders, index, group)
    load(mem_at).wait()
    load(mem_at + 1).wait()
    for copy in gather(mem, gathers.at[0], index, group):
        copy.start()
    doc[...] = documents(lengths, index, group, doc.shape[1])
    dwo[...] = jnp.zeros_like(dwo)
    dwup[...] = jnp.zeros_like(dwup)
    dwdown_t[...] = jnp.zeros_like(dwdown_t)
    dgain[...] = jnp.zeros_like(dgain)
    for n in range(weights_at, weights_at + 3):
        load(n).wait()

    kept = ((low, low_out), (q_t, q_out), (k, k_out), (k_t, kt_out), (v, v_out), (v_t, vt_out))

    def keep(n, i):
        source, target = kept[n]
        return pltpu.make_async_copy(source.at[i], target.at[i], stores.at[n, i])

    @pl.loop(0, count)
    def _(i):
        pltpu.make_async_copy(x_in.at[i], x.at[i], loads.at[i]).wait()
        unit, _ = norm(x[i].astype(F32))
        row = (unit * gain1[...]).astype(BF16)
        low[i] = row
        q_t[i] = jnp.transpose((nn(row, wq[...]) * SCALE).astype(BF16)).reshape(q_t.shape[1:])
        key = nn(row, wk[...]).astype(BF16)
        k_t[i] = jnp.transpose(key).reshape(k_t.shape[1:])
        value = nn(row, wv[...]).astype(BF16)
        v_t[i] = jnp.transpose(value).reshape(v_t.shape[1:])
        for p in range(pairs):
            k[i, p] = key[:, two(p)]
            v[i, p] = value[:, two(p)]
        for n in range(len(kept)):
            keep(n, i).start()

    for copy in gather(mem, gathers.at[0], index, group):
        copy.wait()
    load(weights_at + 3).wait()
    load(weights_at + 4).wait()
    slots = group * mem.shape[2]
    unit, _ = norm(mem[:, 0].reshape(slots, mem.shape[3]).astype(F32))
    row = (unit * gain3[...]).astype(BF16)
    sk = nn(row, wk[...]).astype(BF16)
    sv = nn(row, wv[...]).astype(BF16)
    sq = (nn(row, wsq[...]) * SCALE).astype(BF16)
    lane = lax.broadcasted_iota(jnp.int32, (slots, 2 * DH), 1) < DH
    for p in range(pairs):
        slot_k[p], slot_v[p], slot_q[p] = sk[:, two(p)], sv[:, two(p)], sq[:, two(p)]
        slot_kt[p] = jnp.transpose(sk[:, two(p)])
        slot_vt[p] = jnp.transpose(sv[:, two(p)])
        slot_qt[p] = jnp.transpose(sq[:, two(p)])
        parts = []
        for odd in range(2):
            mine = head_lanes(sq[:, two(p)], odd)
            cs = [
                nn(mine, k_t[i, p]) + jnp.where(pad[:, i * SEG : (i + 1) * SEG] > 0, 0.0, FILL)
                for i in range(count)
            ]
            top = jnp.max(cs[0], 1, keepdims=True)
            for c in cs[1:]:
                top = jnp.maximum(top, jnp.max(c, 1, keepdims=True))
            total, acc = 0.0, 0.0
            for i, c in enumerate(cs):
                w = jnp.exp(c - top)
                total = total + jnp.sum(w, 1, keepdims=True)
                acc = acc + nn(w.astype(BF16), v[i, p])
            parts.append((acc, top, total))
        for n in range(3):
            stats[index["slot"], n, :, two(p)] = jnp.where(lane, parts[0][n], parts[1][n])
    for copy in gather(stats, gathers.at[1], index, group):
        copy.start()

    @pl.loop(0, count)
    def _(i):
        cols = pl.ds(pl.multiple_of(i * SEG, SEG), SEG)
        bias[...] = segment_bias(doc[:, cols], pad[:, cols])
        for h in range(H):
            p, odd = h // 2, h % 2
            own = one(odd)
            qm = head_rows(q_t[i, p], odd)
            for lo, hi in BLOCKS:
                qb = qm[:, lo:hi]
                s = nn(k[i, p, :hi, :], qb) + bias[:hi, lo:hi]
                sm = nn(slot_k[p], qb)
                top = jnp.maximum(jnp.max(s, 0, keepdims=True), jnp.max(sm, 0, keepdims=True))
                e = jnp.exp(s - top)
                em = jnp.exp(sm - top)
                total = jnp.sum(e, 0, keepdims=True) + jnp.sum(em, 0, keepdims=True)
                o = nn(v_t[i, p, own, :hi], e.astype(BF16)) + nn(slot_vt[p, own, :], em.astype(BF16))
                o_t[i, one(h), lo:hi] = (o / total).astype(BF16)
                lse[i, p, odd : odd + 1, lo:hi] = top + jnp.log(total)
        res = x[i].astype(F32) + nn(jnp.transpose(o_t[i]), wo[...])
        ffn[i] = res
        grad[i] = jnp.zeros_like(res)
        unit, _ = norm(res)
        row = (unit * gain2[...]).astype(BF16)
        second[i] = row
        second_t[i] = jnp.transpose(row)
        pltpu.make_async_copy(cot_in.at[i], cot.at[i], loads.at[cot_at + i]).wait()
        cot_t[i] = jnp.transpose(cot[i])

    last = chunks * count + count - 1

    def summed(n, stage):
        work[n].tick(stage)
        if stage == work[n].stages - 1:
            pltpu.make_async_copy(work[n].buf, sums[n], late_sems.at[n]).start()

    events = [
        ((n + 1) * count - 1 + ((4 - n) * stage) // 2, summed, (n, stage))
        for n in range(EARLY)
        for stage in range(work[n].stages)
    ]

    @pl.loop(0, chunks * count)
    def _(step):
        c = step // count
        i = step % count

        @pl.when(i == 0)
        def _():
            for n in range(chunks):

                @pl.when(c == n)
                def _():
                    load(up_at + n).wait()
                    load(down_at + n).wait()

        act, slope = gelu_pair(nn(second[i], wup[c]))
        act = act.astype(BF16)
        ffn[i] += nn(act, wdown[c])
        up_grad = (nt(cot[i], wdown[c]) * slope).astype(BF16)
        dwdown_t[...] += nn(cot_t[i], act)
        dwup[...] += nn(second_t[i], up_grad)
        grad[i] += nt(up_grad, wup[c])

        half = SEG // TILE
        for n in range(chunks):

            @pl.when((i == count - 1) & (c == n))
            def _():
                target = work[n].buf if n < EARLY else late_buf.at[n - EARLY]
                target[:half] = tiles(dwup[...].astype(BF16))
                target[half:] = tiles(jnp.transpose(dwdown_t[...].astype(BF16)))
                dwup[...] = jnp.zeros_like(dwup)
                dwdown_t[...] = jnp.zeros_like(dwdown_t)
                if n >= EARLY:
                    pltpu.make_async_copy(target, late.at[n - EARLY], late_sems.at[n]).start()

        run_events(step, last, [e for e in events if e[0] < chunks * count])

    def finish(n, i):
        source, target = ((out_low, out), (grad, res_out), (o_t, d_out))[n]
        return pltpu.make_async_copy(source.at[i], target.at[i], stores.at[len(kept) + n, i])

    @pl.loop(0, count)
    def _(i):
        res = x[i].astype(F32) + nn(jnp.transpose(o_t[i]), wo[...])
        unit, inverse = norm(res)
        out_low[i] = ffn[i].astype(BF16)
        back, gain_part = norm_back(grad[i], unit, inverse, gain2[...])
        dgain[...] += gain_part
        back = back + cot[i].astype(F32)
        grad[i] = back
        row = back.astype(BF16)
        dwo[...] += nn(o_t[i], row)
        d = nt(wo[...], row).astype(BF16)
        prod = d.astype(F32) * o_t[i].astype(F32)
        for h in range(H):
            inner[i, h // 2, h % 2 : h % 2 + 1, :] = jnp.sum(prod[one(h), :], 0, keepdims=True)
        o_t[i] = d
        for n in range(3):
            finish(n, i).start()
        run_events(i + chunks * count, last, [e for e in events if e[0] >= chunks * count])

    dwo_out[...] = dwo[...].astype(BF16)
    for copy in gather(stats, gathers.at[1], index, group):
        copy.wait()
    for i in range(count):
        for n in range(len(kept)):
            keep(n, i).wait()
        for n in range(3):
            finish(n, i).wait()
    for n in range(EARLY):
        pltpu.make_async_copy(work[n].buf, sums[n], late_sems.at[n]).wait()
    for n in range(EARLY, chunks):
        pltpu.make_async_copy(late_buf.at[n - EARLY], late.at[n - EARLY], late_sems.at[n]).wait()


def update(
    index, stats, mem, slot_q, slot_k, slot_v, wgate, bgate, wwrite,
    new_memory, g_out, g_t, lse, inner_out, sq_acc, sk_acc, sv_acc, direct_out,
    dwgate, dwwrite, dbias, fresh,
):
    group, _, rows, width = mem.shape
    slots = group * rows
    pairs = H // 2
    same = (
        lax.broadcasted_iota(jnp.int32, (width, width), 0) // DH
        == lax.broadcasted_iota(jnp.int32, (width, width), 1) // DH
    ).astype(F32)

    def head_sum(value):
        return nn(value, same, lax.Precision.HIGHEST)

    start = index["slot"] * rows
    row = lax.broadcasted_iota(jnp.int32, (slots, width), 0)
    own = (row >= start) & (row < start + rows)
    sq, sk, sv = (
        jnp.concatenate([r[p] for p in range(pairs)], 1).astype(F32) for r in (slot_q, slot_k, slot_v)
    )
    state = mem[:, 0].reshape(slots, width).astype(F32)
    memory_out = mem[:, 1].reshape(slots, width).astype(F32)
    own_score = head_sum(sq * sk)
    top = own_score
    for n in range(group):
        top = jnp.maximum(top, stats[n, 1])
    power = jnp.exp(own_score - top)
    total = power
    weighted = power.astype(BF16).astype(F32) * sv
    for n in range(group):
        factor = jnp.exp(stats[n, 1] - top)
        total = total + factor * stats[n, 2]
        weighted = weighted + factor * stats[n, 0]
    value = weighted / total
    low = value.astype(BF16)
    gate = jax.nn.sigmoid(nn(low, wgate[...]) + bgate[...])
    written = nn(low, wwrite[...])
    fresh[...] = ((1.0 - gate) * state + gate * written).reshape(fresh.shape)
    new_memory[...] = fresh[index["slot"]]
    gate_grad = memory_out * (written - state) * gate * (1.0 - gate)
    gate_low = gate_grad.astype(BF16)
    written_low = (memory_out * gate).astype(BF16)
    zero = jnp.zeros((slots, width), F32)
    direct_out[...] = jnp.where(own, memory_out * (1.0 - gate), zero)
    mine = jnp.where(own, gate_grad, zero)
    dbias[...] = jnp.sum(mine, 0, keepdims=True)
    low_t = jnp.transpose(low)
    dwgate[...] = tiles(nn(low_t, mine.astype(BF16)).astype(BF16))
    dwwrite[...] = tiles(nn(low_t, jnp.where(own, memory_out * gate, zero).astype(BF16)).astype(BF16))
    g_low = (nt(gate_low, wgate[...]) + nt(written_low, wwrite[...])).astype(BF16)
    g = g_low.astype(F32)
    inner = head_sum(g * value)
    spread = top + jnp.log(total)
    delta = (power / total * (head_sum(g * sv) - inner)).astype(BF16).astype(F32)
    self_q = jnp.where(own, delta * sk, zero)
    self_k = jnp.where(own, delta * sq, zero)
    self_v = jnp.where(own, power.astype(BF16).astype(F32) / total * g, zero)
    for p in range(pairs):
        g_out[p] = g_low[:, two(p)]
        g_t[p] = jnp.transpose(g_low[:, two(p)])
        inner_out[p] = inner[:, two(p)]
        lse[p] = spread[:, two(p)]
        sq_acc[p] = jnp.transpose(self_q[:, two(p)])
        sk_acc[p] = jnp.transpose(self_k[:, two(p)])
        sv_acc[p] = jnp.transpose(self_v[:, two(p)])


def back_kernel(
    count, group, orders, sizes,
    x_in, low_in, q_in, k_in, kt_in, v_in, vt_in, d_in, res_in,
    wq_in, wk_in, wv_in, wsq_in, wgate_in, wwrite_in, late, dwo_in,
    lse, inner, lengths, pad, gain1, mgain, slot_k, slot_kt, slot_v, slot_q, slot_qt, mem, stats, bgate,
    dgain2, *rest,
):
    early = len(sizes)
    input_grad = rest[0]
    sums = rest[1 : 1 + early]
    (
        dwq_out, dwk_out, dwv_out, dwsq_out, gains_out, memory_grad, new_memory,
        x, low, q_t, k, k_t, v, v_t, d_t, res, wq, wk, wv, wsq, wgate, wwrite,
        bias, grads, acc, w_all, sq_acc, sk_acc, sv_acc, g, g_t, wlse, winner, direct, fresh,
        slot_low, dgain, dgain3, dbias, part, part_in, doc, part_sems, block_loads, loads, stores,
    ) = rest[1 + early : 47 + early]
    pairs = H // 2
    index = here()
    work = reductions(rest[47 + early :], early + pairs + 1, orders, index)
    wide = 2 * DH
    third = wo_blocks = wq.shape[0] // TILE

    blocks = (
        (q_in, q_t), (k_in, k), (kt_in, k_t), (v_in, v), (vt_in, v_t), (d_in, d_t), (low_in, low),
        (x_in, x), (res_in, res),
    )
    used = 7

    def block(n, i):
        return pltpu.make_async_copy(blocks[n][0].at[i], blocks[n][1].at[i], block_loads.at[n, i])

    whole = (
        [(wgate_in, wgate), (wwrite_in, wwrite), (wq_in, wq), (wk_in, wk), (wv_in, wv), (wsq_in, wsq)]
        + [(late.at[n], work[n].buf) for n in range(early - 1)]
        + [(dwo_in, work[early - 1].buf.at[:wo_blocks])]
    )

    def load(n):
        return pltpu.make_async_copy(*whole[n], loads.at[n])

    for n in (*range(6, 5 + early), 0, 1):
        load(n).start()
    for n in range(used):
        block(n, 0).start()
    for n in (*range(2, 6), 5 + early):
        load(n).start()
    for i in range(1, count):
        for n in range(used):
            block(n, i).start()
    for i in range(count):
        for n in range(used, len(blocks)):
            block(n, i).start()
    greet(orders, index, group)
    for n in range(early - 1):
        load(6 + n).wait()
        work[n].tick(0)
    doc[...] = documents(lengths, index, group, doc.shape[1])
    load(0).wait()
    load(1).wait()
    update(
        index, stats, mem, slot_q, slot_k, slot_v, wgate, bgate, wwrite,
        new_memory, g, g_t, wlse, winner, sq_acc, sk_acc, sv_acc, direct,
        work[early - 1].buf.at[third : 2 * third], work[early - 1].buf.at[2 * third :], dbias, fresh,
    )
    for n in range(early - 1):
        work[n].tick(1)
    for n in range(2, 6):
        load(n).wait()
    for n in range(pairs):
        for m, w in enumerate((wq, wk, wv)):
            at = (3 * n + m) * wide
            w_all[:, at : at + wide] = w[:, two(n)]
    slots = group * mem.shape[2]
    unit3, inverse3 = norm(mem[:, 0].reshape(slots, mem.shape[3]).astype(F32))
    slot_low[...] = (unit3 * mgain[...]).astype(BF16)
    dgain[...] = jnp.zeros_like(dgain)
    acc[...] = jnp.zeros_like(acc)

    strides = [1 << n for n in reversed(range(group.bit_length() - 1))]

    def scatter(level):
        stride = strides[level]
        start, at = 0, 0
        for s in strides[:level]:
            start = start + across(index, "slot", s)[0] * s
            at += s
        bit, peer = across(index, "slot", stride)
        copy = pltpu.make_async_remote_copy(
            part.at[pl.ds(start + stride - bit * stride, stride)], part_in.at[pl.ds(at, stride)],
            part_sems.at[0, level], part_sems.at[1, level], device_id=peer, device_id_type=MESH,
        )
        return copy, start + bit * stride, at, stride

    def slot_grads(stage):
        if stage == 0:
            unit, inverse = norm(mem[:, 0].reshape(slots, mem.shape[3]).astype(F32))
            grad_t = 0.0
            for p in range(pairs):
                grad_t = (
                    grad_t
                    + nn(wk[:, two(p)], sk_acc[p].astype(BF16))
                    + nn(wv[:, two(p)], sv_acc[p].astype(BF16))
                    + nn(wsq[:, two(p)], (sq_acc[p] * SCALE).astype(BF16))
                )
            back, gain_part = norm_back(jnp.transpose(grad_t), unit, inverse, mgain[...])
            part[...] = (back + direct[...]).reshape(part.shape)
            dgain3[...] = gain_part
        else:
            copy, keep, at, size = scatter(stage - 1)
            copy.wait()
            part[pl.ds(keep, size)] += part_in[pl.ds(at, size)]
        if stage < len(strides):
            scatter(stage)[0].start()
        else:
            memory_grad[...] = part[index["slot"]]

    def gains(stage):
        item = work[early + pairs]
        if stage == 0:
            rows = [jnp.broadcast_to(r[...], (8, dgain.shape[1])) for r in (dgain, dgain3, dgain2, dbias)]
            item.buf[...] = tiles(jnp.concatenate(rows, 0).astype(BF16))
        item.tick(stage)
        if stage == item.stages - 1:
            gains_out[...] = item.buf[...].reshape(gains_out.shape).astype(F32)

    def summed(n, stage):
        item = work[n]
        if n == early - 1 and stage == 0:
            load(6 + n).wait()
        item.tick(stage)
        if stage < item.stages - 1:
            return
        if n < early:
            pltpu.make_async_copy(item.buf, sums[n], stores.at[n]).start()
            return
        per = wide // TILE
        for m, out in enumerate((dwq_out, dwk_out, dwv_out, dwsq_out)):
            rows = item.buf[m * per : (m + 1) * per].reshape(wide, out.shape[0])
            out[:, two(n - early)] = jnp.transpose(rows)

    busy = pairs * count
    last = busy + count - 1
    events = []
    for n in range(early - 1):
        events += [
            (1 + n + 5 * (stage - 2) // 2, summed, (n, stage)) for stage in range(2, work[n].stages)
        ]
    events += [
        (2 + 2 * stage, summed, (early - 1, stage)) for stage in range(work[early - 1].stages)
    ]
    for n in range(pairs):
        events += [
            ((n + 1) * count - 1 + (stage if n > 1 else (4 - n) * stage // 2), summed, (early + n, stage))
            for stage in range(work[early + n].stages)
        ]
    events += [(busy + stage, slot_grads, (stage,)) for stage in range(len(strides) + 1)]
    events += [(busy + stage, gains, (stage,)) for stage in range(work[early + pairs].stages)]

    @pl.loop(0, busy)
    def _(step):
        p = step // count
        i = step % count

        @pl.when(p == 0)
        def _():
            for n in range(used):
                block(n, i).wait()
            cols = pl.ds(pl.multiple_of(i * SEG, SEG), SEG)
            bias[i] = segment_bias(doc[:, cols], pad[:, cols])

        cols = pl.ds(pl.multiple_of(i * SEG, SEG), SEG)
        pad_bias = jnp.where(pad[:, cols] > 0, 0.0, FILL)
        for odd in range(2):
            own = one(odd)
            qm = head_rows(q_t[i, p], odd)
            dm = head_rows(d_t[i, p], odd)
            c = nn(head_lanes(slot_q[p], odd), k_t[i, p]) + pad_bias
            share = jnp.exp(c - wlse[p, :, odd * DH : odd * DH + 1])
            dotted = nn(head_lanes(g[p], odd), v_t[i, p])
            change = (share * (dotted - winner[p, :, odd * DH : odd * DH + 1])).astype(BF16)
            dk = nn(slot_qt[p, own, :], change)
            dv = nn(g_t[p, own, :], share.astype(BF16))
            sq_acc[p, own, :] += nt(k_t[i, p, own, :], change)
            for lo, hi in BLOCKS:
                qb = qm[:, lo:hi]
                db = dm[:, lo:hi]
                qh = q_t[i, p, own, lo:hi]
                dh = d_t[i, p, own, lo:hi]
                l = lse[i, p, odd : odd + 1, lo:hi]
                t = inner[i, p, odd : odd + 1, lo:hi]
                e = jnp.exp(nn(k[i, p, :hi, :], qb) + bias[i, :hi, lo:hi] - l)
                em = jnp.exp(nn(slot_k[p], qb) - l)
                ds = (e * (nn(v[i, p, :hi, :], db) - t)).astype(BF16)
                dsm = (em * (nn(slot_v[p], db) - t)).astype(BF16)
                dq = (nn(k_t[i, p, own, :hi], ds) + nn(slot_kt[p, own, :], dsm)) * SCALE
                grads[i, p, own, lo:hi] = dq.astype(BF16)
                dvp = nt(dh, e.astype(BF16))
                dkp = nt(qh, ds)
                if hi < SEG:
                    dvp = jnp.concatenate([dvp, jnp.zeros((DH, SEG - hi), F32)], 1)
                    dkp = jnp.concatenate([dkp, jnp.zeros((DH, SEG - hi), F32)], 1)
                dv = dv + dvp
                dk = dk + dkp
                sv_acc[p, own, :] += nt(dh, em.astype(BF16))
                sk_acc[p, own, :] += nt(qh, dsm)
            grads[i, p, wide + odd * DH : wide + (odd + 1) * DH, :] = dk.astype(BF16)
            grads[i, p, 2 * wide + odd * DH : 2 * wide + (odd + 1) * DH, :] = dv.astype(BF16)
        acc[...] += nn(grads[i, p], low[i])

        @pl.when(i == count - 1)
        def _():
            rows = jnp.concatenate(
                [
                    acc[:wide],
                    acc[wide : 2 * wide] + nn(sk_acc[p].astype(BF16), slot_low[...]),
                    acc[2 * wide :] + nn(sv_acc[p].astype(BF16), slot_low[...]),
                    nn((sq_acc[p] * SCALE).astype(BF16), slot_low[...]),
                ],
                0,
            )
            rows = tiles(rows.astype(BF16))
            token = acc[...]
            acc[...] = jnp.zeros_like(acc)
            for n in range(pairs):

                @pl.when(p == n)
                def _():
                    w = jnp.transpose(w_all[:, n * 3 * wide : (n + 1) * 3 * wide]).astype(F32)
                    dgain[...] += jnp.sum(token * w, 0, keepdims=True) / gain1[...]
                    work[early + n].buf[...] = rows

        run_events(step, last, [e for e in events if e[0] < busy])

    @pl.loop(0, count)
    def _(i):
        block(used, i).wait()
        block(used + 1, i).wait()
        unit, inverse = norm(x[i].astype(F32))
        grad_t = nn(w_all[...], grads[i].reshape(3 * pairs * wide, SEG))
        back, _ = norm_back(jnp.transpose(grad_t), unit, inverse, gain1[...])
        res[i] += back
        pltpu.make_async_copy(res.at[i], input_grad.at[i], block_loads.at[0, i]).start()
        run_events(i + busy, last, [e for e in events if e[0] >= busy])

    for i in range(count):
        pltpu.make_async_copy(res.at[i], input_grad.at[i], block_loads.at[0, i]).wait()
    for n in range(early):
        pltpu.make_async_copy(work[n].buf, sums[n], stores.at[n]).wait()


def widen_kernel(chunks, half, *refs):
    ffn, rest = refs[:chunks], refs[chunks:]
    own, dwq, dwk, dwv, dwsq, layer_in, grad_in, new_in, mem_in, gains_in = rest[:10]
    (
        layer_out, new_out, grad_out, mem_out,
        dwq_out, dwk_out, dwv_out, dwo_out, dwsq_out, dwgate_out, dwwrite_out, dwup_out, dwdown_out,
    ) = rest[10:23]
    gain_outs = rest[23:27]
    layer, grad, slots, gains, low, wide = rest[27:33]
    rows, loads, stores = rest[33:37], rest[37], rest[38]
    count, seg = layer.shape[:2]

    jobs = [(dwq, dwq_out), (dwk, dwk_out), (dwv, dwv_out), (dwsq, dwsq_out)]
    for n, out in enumerate((dwo_out, dwgate_out, dwwrite_out)):
        jobs.append((own.at[n * half : (n + 1) * half], out))
    for c in range(chunks):
        jobs.append((ffn[c].at[:half], dwup_out.at[:, c * seg : (c + 1) * seg]))
        jobs.append((ffn[c].at[half:], dwdown_out.at[c * seg : (c + 1) * seg, :]))
    passed = [(gains_in, gains, None)]
    passed += [(new_in, slots.at[0], new_out), (mem_in, slots.at[1], mem_out)]
    for i in range(count):
        passed += [
            (grad_in.at[i], grad.at[i], grad_out.at[i]),
            (layer_in.at[i], layer.at[i], layer_out.at[i]),
        ]
    moves = [(source, low.at[n], wide.at[n], target) for n, (source, target) in enumerate(jobs)]
    todo = []
    for n in range(max(len(moves), len(passed))):
        todo += moves[n : n + 1] + passed[n : n + 1]
    copies = [pltpu.make_async_copy(t[0], t[1], loads.at[n]) for n, t in enumerate(todo)]
    for copy in copies:
        copy.start()
    sent = []

    def send(source, target):
        copy = pltpu.make_async_copy(source, target, stores.at[len(sent)])
        copy.start()
        sent.append(copy)

    for copy, t in zip(copies, todo):
        copy.wait()
        if len(t) == 4:
            _, narrow, full, target = t
            per = 4

            @pl.loop(0, half // per)
            def _(b):
                at = pl.ds(pl.multiple_of(b * per * TILE, per * TILE), per * TILE)
                full[at, :] = narrow[pl.ds(b * per, per)].reshape(per * TILE, full.shape[1]).astype(F32)

            send(full, target)
        elif t[2] is None:
            for n, at in enumerate((0, 16, 8, 24)):
                rows[n][...] = gains[at : at + 1, :]
                send(rows[n], gain_outs[n])
        else:
            send(t[1], t[2])
    for copy in sent:
        copy.wait()


def struct(shape, dtype):
    return jax.ShapeDtypeStruct(shape, dtype)


def params(collective_id):
    return pltpu.CompilerParams(
        vmem_limit_bytes=63 << 20, collective_id=collective_id, has_side_effects=True
    )


def body(
    tokens,
    memory,
    pad_mask,
    doc_lengths,
    first_gain,
    query_weight,
    key_weight,
    value_weight,
    out_weight,
    second_gain,
    up_weight,
    down_weight,
    memory_gain,
    slot_query_weight,
    gate_weight,
    gate_bias,
    write_weight,
    out_cotangent,
    memory_cotangent,
):
    rows, width = tokens.shape
    hidden = up_weight.shape[1]
    count = rows // SEG
    chunks = hidden // SEG
    pairs = H // 2
    two_heads = 2 * DH
    slots_here = memory.shape[1]
    group = lax.axis_size("slot")
    slots = slots_here * group
    pad = pad_mask[None, :]
    gain1, gain2, gain3 = (g[None, :] for g in (first_gain, second_gain, memory_gain))
    orders = bit_orders({"dp": lax.axis_size("dp"), "slot": group})

    anywhere = pl.BlockSpec(memory_space=pl.ANY)
    vm = pl.BlockSpec(memory_space=pltpu.VMEM)
    sm = pl.BlockSpec(memory_space=pltpu.SMEM)
    tokens = tokens.reshape(count, SEG, width)
    segments = (count, SEG, width)
    by_rows = (count, pairs, SEG, two_heads)
    by_lanes = (count, pairs, two_heads, SEG)
    square = (width, width)
    blocks = 2 * SEG // TILE
    half = SEG // TILE
    slot_tall, slot_wide = (pairs, slots, two_heads), (pairs, two_heads, slots)
    per_head = (count, pairs, 2, SEG)
    outs = pl.pallas_call(
        lambda *refs: front_kernel(count, chunks, group, orders, *refs),
        in_specs=[anywhere] * 11 + [sm] + [vm] * 4,
        out_specs=[anywhere] * (10 + EARLY) + [vm] * 11,
        out_shape=[
            struct(segments, BF16), struct(segments, F32), struct(segments, BF16),
            struct(by_lanes, BF16), struct(by_rows, BF16), struct(by_lanes, BF16),
            struct(by_rows, BF16), struct(by_lanes, BF16), struct((count, width, SEG), BF16),
            struct((chunks - EARLY, blocks, TILE, width), BF16),
        ]
        + [struct((blocks, TILE, width), BF16)] * EARLY
        + [
            struct(per_head, F32), struct(per_head, F32), struct(slot_tall, BF16),
            struct(slot_wide, BF16), struct(slot_tall, BF16), struct(slot_tall, BF16),
            struct(slot_wide, BF16), struct((group, 2, slots_here, width), BF16),
            struct((group, 3, slots, width), F32), struct(square, BF16), struct((1, width), F32),
        ],
        scratch_shapes=[
            pltpu.VMEM(segments, BF16), pltpu.VMEM(segments, BF16), pltpu.VMEM(segments, BF16),
            pltpu.VMEM(by_lanes, BF16), pltpu.VMEM(by_rows, BF16), pltpu.VMEM(by_lanes, BF16),
            pltpu.VMEM(by_rows, BF16), pltpu.VMEM(by_lanes, BF16),
            pltpu.VMEM((count, width, SEG), BF16), pltpu.VMEM(segments, BF16),
            pltpu.VMEM((count, width, SEG), BF16), pltpu.VMEM((count, width, SEG), BF16),
            pltpu.VMEM(segments, F32), pltpu.VMEM(segments, F32),
            pltpu.VMEM(square, BF16), pltpu.VMEM(square, BF16), pltpu.VMEM(square, BF16),
            pltpu.VMEM(square, BF16), pltpu.VMEM(square, BF16),
            pltpu.VMEM((chunks, width, SEG), BF16), pltpu.VMEM((chunks, SEG, width), BF16),
            pltpu.VMEM(slot_wide, BF16), pltpu.VMEM((SEG, SEG), F32), pltpu.VMEM(square, F32),
            pltpu.VMEM((width, SEG), F32), pltpu.VMEM((width, SEG), F32),
            pltpu.VMEM(segments, BF16), pltpu.VMEM((chunks - EARLY, blocks, TILE, width), BF16),
            pltpu.VMEM((1, rows), F32),
            pltpu.SemaphoreType.DMA((2 * count + 7 + 2 * chunks,)),
            pltpu.SemaphoreType.DMA((9, count)),
            pltpu.SemaphoreType.DMA((2, 2, group)),
            pltpu.SemaphoreType.DMA((chunks,)),
        ]
        + reduction_scratch([blocks] * EARLY, orders, width),
        compiler_params=params(0),
        name="front",
    )(
        tokens, memory[0], memory_cotangent[0], query_weight, key_weight, value_weight,
        slot_query_weight, out_weight, up_weight, down_weight.reshape(chunks, SEG, width),
        out_cotangent.reshape(segments), doc_lengths, pad, gain1, gain2, gain3,
    )
    layer_out, res_grad, low, q_t, k, k_t, v, v_t, d_t, late = outs[:10]
    early = list(outs[10 : 10 + EARLY])
    (
        lse, inner, slot_k, slot_kt, slot_v, slot_q, slot_qt, mem, stats, dwo, dgain2,
    ) = outs[10 + EARLY :]

    sizes = [blocks] * (chunks - EARLY) + [3 * half]
    n_sum = len(sizes)
    outs = pl.pallas_call(
        lambda *refs: back_kernel(count, group, orders, sizes, *refs),
        in_specs=[anywhere] * 17 + [vm] * 2 + [sm] + [vm] * 12,
        out_specs=[anywhere] * (1 + n_sum) + [vm] * 7,
        out_shape=[struct(segments, F32)]
        + [struct((n, TILE, width), BF16) for n in sizes]
        + [struct(square, BF16)] * 4
        + [
            struct((32, width), F32), struct((slots_here, width), F32), struct((slots_here, width), F32),
        ],
        scratch_shapes=[
            pltpu.VMEM(segments, BF16), pltpu.VMEM(segments, BF16), pltpu.VMEM(by_lanes, BF16),
            pltpu.VMEM(by_rows, BF16), pltpu.VMEM(by_lanes, BF16), pltpu.VMEM(by_rows, BF16),
            pltpu.VMEM(by_lanes, BF16), pltpu.VMEM(by_lanes, BF16), pltpu.VMEM(segments, F32),
            pltpu.VMEM(square, BF16), pltpu.VMEM(square, BF16), pltpu.VMEM(square, BF16),
            pltpu.VMEM(square, BF16), pltpu.VMEM(square, BF16), pltpu.VMEM(square, BF16),
            pltpu.VMEM((count, SEG, SEG), F32), pltpu.VMEM((count, pairs, 3 * two_heads, SEG), BF16),
            pltpu.VMEM((3 * two_heads, width), F32), pltpu.VMEM((width, 3 * width), BF16),
            pltpu.VMEM(slot_wide, F32), pltpu.VMEM(slot_wide, F32), pltpu.VMEM(slot_wide, F32),
            pltpu.VMEM(slot_tall, BF16), pltpu.VMEM(slot_wide, BF16), pltpu.VMEM(slot_tall, F32),
            pltpu.VMEM(slot_tall, F32), pltpu.VMEM((slots, width), F32),
            pltpu.VMEM((group, slots_here, width), F32), pltpu.VMEM((slots, width), BF16),
            pltpu.VMEM((1, width), F32), pltpu.VMEM((1, width), F32), pltpu.VMEM((1, width), F32),
            pltpu.VMEM((group, slots_here, width), F32), pltpu.VMEM((group, slots_here, width), F32),
            pltpu.VMEM((1, rows), F32),
            pltpu.SemaphoreType.DMA((2, group)), pltpu.SemaphoreType.DMA((9, count)),
            pltpu.SemaphoreType.DMA((6 + n_sum,)), pltpu.SemaphoreType.DMA((n_sum,)),
        ]
        + reduction_scratch(sizes + [4 * two_heads // TILE] * pairs + [2], orders, width),
        compiler_params=params(1),
        name="back",
    )(
        tokens, low, q_t, k, k_t, v, v_t, d_t.reshape(by_lanes), res_grad,
        query_weight, key_weight, value_weight, slot_query_weight, gate_weight, write_weight,
        late, tiles(dwo),
        lse, inner, doc_lengths, pad, gain1, gain3, slot_k, slot_kt, slot_v, slot_q, slot_qt, mem, stats,
        gate_bias[None, :], dgain2,
    )
    input_grad = outs[0]
    sums = list(outs[1 : 1 + n_sum])
    dwq, dwk, dwv, dwsq, gains, memory_grad, new_memory = outs[1 + n_sum :]
    ffn = early + sums[:-1]
    low_jobs = 7 + 2 * chunks
    outs = pl.pallas_call(
        lambda *refs: widen_kernel(chunks, half, *refs),
        in_specs=[anywhere] * (chunks + 10),
        out_specs=[anywhere] * 17,
        out_shape=[
            struct(segments, BF16), struct((slots_here, width), F32), struct(segments, F32),
            struct((slots_here, width), F32),
        ]
        + [struct(square, F32)] * 7
        + [struct((width, hidden), F32), struct((hidden, width), F32)]
        + [struct((1, width), F32)] * 4,
        scratch_shapes=[
            pltpu.VMEM(segments, BF16), pltpu.VMEM(segments, F32),
            pltpu.VMEM((2, slots_here, width), F32), pltpu.VMEM((32, width), F32),
            pltpu.VMEM((low_jobs, half, TILE, width), BF16), pltpu.VMEM((low_jobs, width, width), F32),
        ]
        + [pltpu.VMEM((1, width), F32)] * 4
        + [
            pltpu.SemaphoreType.DMA((2 * count + 3 + low_jobs,)),
            pltpu.SemaphoreType.DMA((2 * count + 6 + low_jobs,)),
        ],
        compiler_params=pltpu.CompilerParams(vmem_limit_bytes=63 << 20),
        name="widen",
    )(
        *ffn, sums[-1], tiles(dwq), tiles(dwk), tiles(dwv), tiles(dwsq),
        layer_out, input_grad, new_memory, memory_grad, gains,
    )
    layer_out, new_memory, input_grad, memory_grad = outs[:4]
    dwq, dwk, dwv, dwo, dwsq, dwgate, dwwrite, dwup, dwdown = outs[4:13]
    gain1, gain2, gain3, bias = (r[0] for r in outs[13:])
    return (
        layer_out.reshape(rows, width), new_memory[None], input_grad.reshape(rows, width),
        memory_grad[None], gain1, dwq, dwk, dwv, dwo, gain2, dwup, dwdown, gain3, dwsq, dwgate,
        bias, dwwrite,
    )


def solution(mesh):
    token = P(("dp", "slot"), None)
    slot = P("dp", "slot", None)
    in_specs = (
        (token, slot, P(("dp", "slot"))) + (P(),) * 14 + (token, slot)
    )
    out_specs = (token, slot, token, slot) + (P(),) * 13
    return jax.shard_map(body, mesh=mesh, in_specs=in_specs, out_specs=out_specs, check_vma=False)
```

```python
import jax
import jax.numpy as jnp
from jax import lax
from jax.experimental import pallas as pl
from jax.experimental.pallas import tpu as pltpu
from jax.sharding import PartitionSpec as P

H = 8
DH = 64
SEG = 512
HALF = 256
FILL = -1e30
EPS = 1e-05
SCALE = DH ** (-0.5)
F32 = jnp.float32
BF16 = jnp.bfloat16

TAIL = (
    0.11962928145668905,
    0.12075423000729175,
    0.09991172819365436,
    0.12856765411993218,
    -0.053695489964182386,
    0.20636694099934239,
    -0.15721125090545032,
    0.035676834162404004,
)


def nn(a, b, precision=None):
    return lax.dot_general(
        a, b, (((1,), (0,)), ((), ())), preferred_element_type=F32, precision=precision
    )


def nt(a, b):
    return lax.dot_general(a, b, (((1,), (1,)), ((), ())), preferred_element_type=F32)


def norm(value):
    center = value - jnp.mean(value, -1, keepdims=True)
    inverse = lax.rsqrt(jnp.mean(center * center, -1, keepdims=True) + EPS)
    return center * inverse, inverse


def norm_back(grad, unit, inverse, gain):
    inner = grad * gain
    value_grad = inverse * (
        inner
        - jnp.mean(inner, -1, keepdims=True)
        - unit * jnp.mean(inner * unit, -1, keepdims=True)
    )
    return value_grad, jnp.sum(grad * unit, 0, keepdims=True)


def gelu_pair(x):
    t = 1.0 / (1.0 + 0.3 * jnp.abs(x))
    poly = TAIL[7]
    for c in TAIL[6::-1]:
        poly = poly * t + c
    bell = jnp.exp(-0.5 * (x * x))
    tail = bell * (poly * t)
    cdf = jnp.where(x >= 0, 1.0 - tail, tail)
    return x * cdf, cdf + x * (bell * 0.3989422804014327)


def segment_bias(doc_row, pad_row):
    code = jnp.where(pad_row > 0, doc_row, -1.0)
    key_code = jnp.transpose(jnp.broadcast_to(code, (SEG, SEG)))
    rows = lax.broadcasted_iota(jnp.int32, (SEG, SEG), 0)
    columns = lax.broadcasted_iota(jnp.int32, (SEG, SEG), 1)
    seen = (rows <= columns) & (key_code == doc_row)
    return jnp.where(seen, 0.0, FILL)


def documents(lengths, index, group, rows):
    place = lax.broadcasted_iota(jnp.int32, (1, rows), 1)
    place = place + (index["dp"] * group + index["slot"]) * rows
    end, doc = 0, jnp.zeros((1, rows), F32)
    for n in range(lengths.shape[0]):
        end = end + lengths[n]
        doc = doc + jnp.where(place >= end, 1.0, 0.0)
    return doc


def head_rows(pair, odd):
    zero = jnp.zeros((DH, pair.shape[1]), pair.dtype)
    if odd:
        return jnp.concatenate([zero, pair[DH:]], 0)
    return jnp.concatenate([pair[:DH], zero], 0)


def head_lanes(pair, odd):
    lane = lax.broadcasted_iota(jnp.int32, pair.shape, 1)
    keep = (lane >= DH) if odd else (lane < DH)
    return jnp.where(keep, pair, jnp.zeros_like(pair))


def two(p):
    return slice(p * 2 * DH, (p + 1) * 2 * DH)


def one(h):
    return slice(h * DH, (h + 1) * DH)


BLOCKS = ((0, HALF), (HALF, SEG))


TILE = 16
MESH = pl.DeviceIdType.MESH


PARTS = 2
WHOLE = 2


def bit_orders(sizes):
    dp = [("dp", 1 << n) for n in range(sizes["dp"].bit_length() - 1)]
    slot = [("slot", 1 << n) for n in range(sizes["slot"].bit_length() - 1)]
    first, other = slot[:1], slot[1:]
    return first + other + dp, first + dp[:1] + other + dp[1:]


def plan(blocks, orders):
    parts = min(blocks, len(orders))
    steps, recv = [], 0
    for n, order in enumerate(orders[:parts]):
        size, row = blocks // parts, []
        for level, (axis, stride) in enumerate(order):
            halves = size % 2 == 0 and level < len(order) - WHOLE
            sent = size // 2 if halves else size
            row.append((axis, stride, halves, sent, recv))
            recv += sent
            size = sent
        steps.append((n * (blocks // parts), row))
    return steps, recv


def here():
    return {"dp": lax.axis_index("dp"), "slot": lax.axis_index("slot")}


def across(index, axis, stride):
    bit = (index[axis] // stride) % 2
    peer = dict(index)
    peer[axis] = index[axis] + stride - 2 * bit * stride
    return bit, (peer["dp"], peer["slot"])


def ring(index, offset, group):
    return (index["dp"], (index["slot"] + offset) % group)


def greet(orders, index, group):
    barrier = pltpu.get_barrier_semaphore()
    peers = [ring(index, n, group) for n in range(1, group)] + [
        across(index, axis, stride)[1] for axis, stride in orders[0] if axis == "dp"
    ]
    for peer in peers:
        pl.semaphore_signal(barrier, inc=1, device_id=peer, device_id_type=MESH)
    pl.semaphore_wait(barrier, len(peers))


def gather(ref, sems, index, group):
    own = ref.at[index["slot"]]
    return [
        pltpu.make_async_remote_copy(
            own, own, sems.at[0, n], sems.at[1, n],
            device_id=ring(index, n, group), device_id_type=MESH,
        )
        for n in range(1, group)
    ]


def run_events(step, last, events):
    events = sorted(events, key=lambda event: event[0])
    for when in range(last + 1):
        todo = [e for e in events if e[0] == when or (when == last and e[0] > last)]
        if not todo:
            continue

        @pl.when(step == when)
        def _():
            for _, act, args in todo:
                act(*args)


class Reduction:
    def __init__(self, buf, recv, sems, free, base, orders, index):
        self.buf, self.recv, self.sems, self.free = buf, recv, sems, free
        self.base, self.index = base, index
        self.steps, _ = plan(buf.shape[0], orders)
        self.depth = len(orders[0])
        up = [
            (level, False)
            for level in reversed(range(self.depth))
            if any(row[level][2] for _, row in self.steps)
        ]
        self.moves = [(level, True) for level in range(self.depth)] + up
        self.stages = len(self.moves) + 1

    def copies(self, move):
        level, down = self.moves[move]
        found = []
        for n, (start, row) in enumerate(self.steps):
            for axis, stride, halves, sent, _ in row[: level if down else level + 1]:
                if halves:
                    start = start + across(self.index, axis, stride)[0] * sent
            axis, stride, halves, sent, at = row[level]
            bit, peer = across(self.index, axis, stride)
            slot = self.base + n * self.depth + level
            if down:
                keep = start + bit * sent if halves else start
                give = start + sent - bit * sent if halves else start
                target, ends = self.recv.at[pl.ds(at, sent)], 0
            elif halves:
                keep, give = None, start
                target, ends = self.buf.at[pl.ds(give, sent)], 2
            else:
                continue
            copy = pltpu.make_async_remote_copy(
                self.buf.at[pl.ds(give, sent)], target,
                self.sems.at[ends, slot], self.sems.at[ends + 1, slot],
                device_id=peer, device_id_type=MESH,
            )
            found.append((copy, halves, keep, sent, at, slot, peer))
        return found

    def tick(self, stage):
        if stage > 0:
            down = self.moves[stage - 1][1]
            for copy, halves, keep, sent, at, slot, peer in self.copies(stage - 1):
                copy.wait()
                if not down:
                    continue
                if halves:
                    pl.semaphore_signal(
                        self.free.at[slot], inc=1, device_id=peer, device_id_type=MESH
                    )
                mine = self.buf[pl.ds(keep, sent)].astype(F32)
                self.buf[pl.ds(keep, sent)] = (
                    mine + self.recv[pl.ds(at, sent)].astype(F32)
                ).astype(BF16)
        if stage < len(self.moves):
            down = self.moves[stage][1]
            for copy, halves, keep, sent, at, slot, peer in self.copies(stage):
                if not down:
                    pl.semaphore_wait(self.free.at[slot], 1)
                copy.start()


def reduction_scratch(sizes, orders, width):
    depth = len(orders[0])
    return (
        [pltpu.VMEM((s, TILE, width), BF16) for s in sizes]
        + [pltpu.VMEM((plan(s, orders)[1], TILE, width), BF16) for s in sizes]
        + [
            pltpu.SemaphoreType.DMA((4, len(sizes) * PARTS * depth)),
            pltpu.SemaphoreType.REGULAR((len(sizes) * PARTS * depth,)),
        ]
    )


def reductions(refs, count, orders, index):
    bufs, recvs, (sems, free) = refs[:count], refs[count : 2 * count], refs[2 * count :]
    return [
        Reduction(bufs[n], recvs[n], sems, free, n * PARTS * len(orders[0]), orders, index)
        for n in range(count)
    ]


def tiles(value):
    return value.reshape(value.shape[0] // TILE, TILE, value.shape[1])


EARLY = 2


def front_kernel(
    count, chunks, group, orders,
    x_in, mem_in, mem_cot_in, wq_in, wk_in, wv_in, wsq_in, wo_in, wup_in, wdown_in, cot_in,
    lengths, pad, gain1, gain2, gain3,
    out, res_out, low_out, q_out, k_out, kt_out, v_out, vt_out, d_out, late, *rest,
):
    sums, rest = rest[:EARLY], rest[EARLY:]
    (lse, inner, slot_k, slot_kt, slot_v, slot_q, slot_qt, mem, stats, dwo_out, dgain) = rest[:11]
    (
        x, cot, low, q_t, k, k_t, v, v_t, o_t, second, second_t, cot_t, ffn, grad,
        wq, wk, wv, wsq, wo, wup, wdown, slot_vt, bias, dwo, dwup, dwdown_t, out_low, late_buf, doc,
        loads, stores, gathers, late_sems,
    ) = rest[11:44]
    index = here()
    work = reductions(rest[44:], EARLY, orders, index)
    pairs = H // 2

    def load(n):
        pairs_of = (
            [(x_in.at[i], x.at[i]) for i in range(count)]
            + [(wq_in, wq), (wk_in, wk), (wv_in, wv), (wsq_in, wsq), (wo_in, wo)]
            + [(cot_in.at[i], cot.at[i]) for i in range(count)]
            + [
                (wup_in.at[:, c * SEG : (c + 1) * SEG], wup.at[c]) for c in range(chunks)
            ]
            + [(wdown_in.at[c], wdown.at[c]) for c in range(chunks)]
            + [(mem_in, mem.at[index["slot"], 0]), (mem_cot_in, mem.at[index["slot"], 1])]
        )
        return pltpu.make_async_copy(*pairs_of[n], loads.at[n])

    weights_at = count
    cot_at = count + 5
    up_at = 2 * count + 5
    down_at = up_at + chunks
    mem_at = down_at + chunks
    order = (
        [mem_at, mem_at + 1, 0, weights_at, weights_at + 1, weights_at + 2]
        + list(range(1, count))
        + [weights_at + 3, weights_at + 4]
        + list(range(cot_at, mem_at))
    )
    for n in order:
        load(n).start()
    greet(orders, index, group)
    load(mem_at).wait()
    load(mem_at + 1).wait()
    for copy in gather(mem, gathers.at[0], index, group):
        copy.start()
    doc[...] = documents(lengths, index, group, doc.shape[1])
    dwo[...] = jnp.zeros_like(dwo)
    dwup[...] = jnp.zeros_like(dwup)
    dwdown_t[...] = jnp.zeros_like(dwdown_t)
    dgain[...] = jnp.zeros_like(dgain)
    for n in range(weights_at, weights_at + 3):
        load(n).wait()

    kept = ((low, low_out), (q_t, q_out), (k, k_out), (k_t, kt_out), (v, v_out), (v_t, vt_out))

    def keep(n, i):
        source, target = kept[n]
        return pltpu.make_async_copy(source.at[i], target.at[i], stores.at[n, i])

    @pl.loop(0, count)
    def _(i):
        pltpu.make_async_copy(x_in.at[i], x.at[i], loads.at[i]).wait()
        unit, _ = norm(x[i].astype(F32))
        row = (unit * gain1[...]).astype(BF16)
        low[i] = row
        q_t[i] = jnp.transpose((nn(row, wq[...]) * SCALE).astype(BF16)).reshape(q_t.shape[1:])
        key = nn(row, wk[...]).astype(BF16)
        k_t[i] = jnp.transpose(key).reshape(k_t.shape[1:])
        value = nn(row, wv[...]).astype(BF16)
        v_t[i] = jnp.transpose(value).reshape(v_t.shape[1:])
        for p in range(pairs):
            k[i, p] = key[:, two(p)]
            v[i, p] = value[:, two(p)]
        for n in range(len(kept)):
            keep(n, i).start()

    for copy in gather(mem, gathers.at[0], index, group):
        copy.wait()
    load(weights_at + 3).wait()
    load(weights_at + 4).wait()
    slots = group * mem.shape[2]
    unit, _ = norm(mem[:, 0].reshape(slots, mem.shape[3]).astype(F32))
    row = (unit * gain3[...]).astype(BF16)
    sk = nn(row, wk[...]).astype(BF16)
    sv = nn(row, wv[...]).astype(BF16)
    sq = (nn(row, wsq[...]) * SCALE).astype(BF16)
    lane = lax.broadcasted_iota(jnp.int32, (slots, 2 * DH), 1) < DH
    for p in range(pairs):
        slot_k[p], slot_v[p], slot_q[p] = sk[:, two(p)], sv[:, two(p)], sq[:, two(p)]
        slot_kt[p] = jnp.transpose(sk[:, two(p)])
        slot_vt[p] = jnp.transpose(sv[:, two(p)])
        slot_qt[p] = jnp.transpose(sq[:, two(p)])
        parts = []
        for odd in range(2):
            mine = head_lanes(sq[:, two(p)], odd)
            cs = [
                nn(mine, k_t[i, p]) + jnp.where(pad[:, i * SEG : (i + 1) * SEG] > 0, 0.0, FILL)
                for i in range(count)
            ]
            top = jnp.max(cs[0], 1, keepdims=True)
            for c in cs[1:]:
                top = jnp.maximum(top, jnp.max(c, 1, keepdims=True))
            total, acc = 0.0, 0.0
            for i, c in enumerate(cs):
                w = jnp.exp(c - top)
                total = total + jnp.sum(w, 1, keepdims=True)
                acc = acc + nn(w.astype(BF16), v[i, p])
            parts.append((acc, top, total))
        for n in range(3):
            stats[index["slot"], n, :, two(p)] = jnp.where(lane, parts[0][n], parts[1][n])
    for copy in gather(stats, gathers.at[1], index, group):
        copy.start()

    @pl.loop(0, count)
    def _(i):
        cols = pl.ds(pl.multiple_of(i * SEG, SEG), SEG)
        bias[...] = segment_bias(doc[:, cols], pad[:, cols])
        for h in range(H):
            p, odd = h // 2, h % 2
            own = one(odd)
            qm = head_rows(q_t[i, p], odd)
            for lo, hi in BLOCKS:
                qb = qm[:, lo:hi]
                s = nn(k[i, p, :hi, :], qb) + bias[:hi, lo:hi]
                sm = nn(slot_k[p], qb)
                top = jnp.maximum(jnp.max(s, 0, keepdims=True), jnp.max(sm, 0, keepdims=True))
                e = jnp.exp(s - top)
                em = jnp.exp(sm - top)
                total = jnp.sum(e, 0, keepdims=True) + jnp.sum(em, 0, keepdims=True)
                o = nn(v_t[i, p, own, :hi], e.astype(BF16)) + nn(slot_vt[p, own, :], em.astype(BF16))
                o_t[i, one(h), lo:hi] = (o / total).astype(BF16)
                lse[i, p, odd : odd + 1, lo:hi] = top + jnp.log(total)
        res = x[i].astype(F32) + nn(jnp.transpose(o_t[i]), wo[...])
        ffn[i] = res
        grad[i] = jnp.zeros_like(res)
        unit, _ = norm(res)
        row = (unit * gain2[...]).astype(BF16)
        second[i] = row
        second_t[i] = jnp.transpose(row)
        pltpu.make_async_copy(cot_in.at[i], cot.at[i], loads.at[cot_at + i]).wait()
        cot_t[i] = jnp.transpose(cot[i])

    last = chunks * count + count - 1

    def summed(n, stage):
        work[n].tick(stage)
        if stage == work[n].stages - 1:
            pltpu.make_async_copy(work[n].buf, sums[n], late_sems.at[n]).start()

    events = [
        ((n + 1) * count - 1 + ((4 - n) * stage) // 2, summed, (n, stage))
        for n in range(EARLY)
        for stage in range(work[n].stages)
    ]

    @pl.loop(0, chunks * count)
    def _(step):
        c = step // count
        i = step % count

        @pl.when(i == 0)
        def _():
            for n in range(chunks):

                @pl.when(c == n)
                def _():
                    load(up_at + n).wait()
                    load(down_at + n).wait()

        act, slope = gelu_pair(nn(second[i], wup[c]))
        act = act.astype(BF16)
        ffn[i] += nn(act, wdown[c])
        up_grad = (nt(cot[i], wdown[c]) * slope).astype(BF16)
        dwdown_t[...] += nn(cot_t[i], act)
        dwup[...] += nn(second_t[i], up_grad)
        grad[i] += nt(up_grad, wup[c])

        half = SEG // TILE
        for n in range(chunks):

            @pl.when((i == count - 1) & (c == n))
            def _():
                target = work[n].buf if n < EARLY else late_buf.at[n - EARLY]
                target[:half] = tiles(dwup[...].astype(BF16))
                target[half:] = tiles(jnp.transpose(dwdown_t[...].astype(BF16)))
                dwup[...] = jnp.zeros_like(dwup)
                dwdown_t[...] = jnp.zeros_like(dwdown_t)
                if n >= EARLY:
                    pltpu.make_async_copy(target, late.at[n - EARLY], late_sems.at[n]).start()

        run_events(step, last, [e for e in events if e[0] < chunks * count])

    def finish(n, i):
        source, target = ((out_low, out), (grad, res_out), (o_t, d_out))[n]
        return pltpu.make_async_copy(source.at[i], target.at[i], stores.at[len(kept) + n, i])

    @pl.loop(0, count)
    def _(i):
        res = x[i].astype(F32) + nn(jnp.transpose(o_t[i]), wo[...])
        unit, inverse = norm(res)
        out_low[i] = ffn[i].astype(BF16)
        back, gain_part = norm_back(grad[i], unit, inverse, gain2[...])
        dgain[...] += gain_part
        back = back + cot[i].astype(F32)
        grad[i] = back
        row = back.astype(BF16)
        dwo[...] += nn(o_t[i], row)
        d = nt(wo[...], row).astype(BF16)
        prod = d.astype(F32) * o_t[i].astype(F32)
        for h in range(H):
            inner[i, h // 2, h % 2 : h % 2 + 1, :] = jnp.sum(prod[one(h), :], 0, keepdims=True)
        o_t[i] = d
        for n in range(3):
            finish(n, i).start()
        run_events(i + chunks * count, last, [e for e in events if e[0] >= chunks * count])

    dwo_out[...] = dwo[...].astype(BF16)
    for copy in gather(stats, gathers.at[1], index, group):
        copy.wait()
    for i in range(count):
        for n in range(len(kept)):
            keep(n, i).wait()
        for n in range(3):
            finish(n, i).wait()
    for n in range(EARLY):
        pltpu.make_async_copy(work[n].buf, sums[n], late_sems.at[n]).wait()
    for n in range(EARLY, chunks):
        pltpu.make_async_copy(late_buf.at[n - EARLY], late.at[n - EARLY], late_sems.at[n]).wait()


def update(
    index, stats, mem, slot_q, slot_k, slot_v, wgate, bgate, wwrite,
    new_memory, g_out, g_t, lse, inner_out, sq_acc, sk_acc, sv_acc, direct_out,
    dwgate, dwwrite, dbias, fresh,
):
    group, _, rows, width = mem.shape
    slots = group * rows
    pairs = H // 2
    same = (
        lax.broadcasted_iota(jnp.int32, (width, width), 0) // DH
        == lax.broadcasted_iota(jnp.int32, (width, width), 1) // DH
    ).astype(F32)

    def head_sum(value):
        return nn(value, same, lax.Precision.HIGHEST)

    start = index["slot"] * rows
    row = lax.broadcasted_iota(jnp.int32, (slots, width), 0)
    own = (row >= start) & (row < start + rows)
    sq, sk, sv = (
        jnp.concatenate([r[p] for p in range(pairs)], 1).astype(F32) for r in (slot_q, slot_k, slot_v)
    )
    state = mem[:, 0].reshape(slots, width).astype(F32)
    memory_out = mem[:, 1].reshape(slots, width).astype(F32)
    own_score = head_sum(sq * sk)
    top = own_score
    for n in range(group):
        top = jnp.maximum(top, stats[n, 1])
    power = jnp.exp(own_score - top)
    total = power
    weighted = power.astype(BF16).astype(F32) * sv
    for n in range(group):
        factor = jnp.exp(stats[n, 1] - top)
        total = total + factor * stats[n, 2]
        weighted = weighted + factor * stats[n, 0]
    value = weighted / total
    low = value.astype(BF16)
    gate = jax.nn.sigmoid(nn(low, wgate[...]) + bgate[...])
    written = nn(low, wwrite[...])
    fresh[...] = ((1.0 - gate) * state + gate * written).reshape(fresh.shape)
    new_memory[...] = fresh[index["slot"]]
    gate_grad = memory_out * (written - state) * gate * (1.0 - gate)
    gate_low = gate_grad.astype(BF16)
    written_low = (memory_out * gate).astype(BF16)
    zero = jnp.zeros((slots, width), F32)
    direct_out[...] = jnp.where(own, memory_out * (1.0 - gate), zero)
    mine = jnp.where(own, gate_grad, zero)
    dbias[...] = jnp.sum(mine, 0, keepdims=True)
    low_t = jnp.transpose(low)
    dwgate[...] = tiles(nn(low_t, mine.astype(BF16)).astype(BF16))
    dwwrite[...] = tiles(nn(low_t, jnp.where(own, memory_out * gate, zero).astype(BF16)).astype(BF16))
    g_low = (nt(gate_low, wgate[...]) + nt(written_low, wwrite[...])).astype(BF16)
    g = g_low.astype(F32)
    inner = head_sum(g * value)
    spread = top + jnp.log(total)
    delta = (power / total * (head_sum(g * sv) - inner)).astype(BF16).astype(F32)
    self_q = jnp.where(own, delta * sk, zero)
    self_k = jnp.where(own, delta * sq, zero)
    self_v = jnp.where(own, power.astype(BF16).astype(F32) / total * g, zero)
    for p in range(pairs):
        g_out[p] = g_low[:, two(p)]
        g_t[p] = jnp.transpose(g_low[:, two(p)])
        inner_out[p] = inner[:, two(p)]
        lse[p] = spread[:, two(p)]
        sq_acc[p] = jnp.transpose(self_q[:, two(p)])
        sk_acc[p] = jnp.transpose(self_k[:, two(p)])
        sv_acc[p] = jnp.transpose(self_v[:, two(p)])


def back_kernel(
    count, group, orders, sizes,
    x_in, low_in, q_in, k_in, kt_in, v_in, vt_in, d_in, res_in,
    wq_in, wk_in, wv_in, wsq_in, wgate_in, wwrite_in, late, dwo_in,
    lse, inner, lengths, pad, gain1, mgain, slot_k, slot_kt, slot_v, slot_q, slot_qt, mem, stats, bgate,
    dgain2, *rest,
):
    early = len(sizes)
    input_grad = rest[0]
    sums = rest[1 : 1 + early]
    (
        dwq_out, dwk_out, dwv_out, dwsq_out, gains_out, memory_grad, new_memory,
        x, low, q_t, k, k_t, v, v_t, d_t, res, wq, wk, wv, wsq, wgate, wwrite,
        bias, grads, acc, w_all, sq_acc, sk_acc, sv_acc, g, g_t, wlse, winner, direct, fresh,
        slot_low, dgain, dgain3, dbias, part, part_in, doc, part_sems, block_loads, loads, stores,
    ) = rest[1 + early : 47 + early]
    pairs = H // 2
    index = here()
    work = reductions(rest[47 + early :], early + pairs + 1, orders, index)
    wide = 2 * DH
    third = wo_blocks = wq.shape[0] // TILE

    blocks = (
        (q_in, q_t), (k_in, k), (kt_in, k_t), (v_in, v), (vt_in, v_t), (d_in, d_t), (low_in, low),
        (x_in, x), (res_in, res),
    )
    used = 7

    def block(n, i):
        return pltpu.make_async_copy(blocks[n][0].at[i], blocks[n][1].at[i], block_loads.at[n, i])

    whole = (
        [(wgate_in, wgate), (wwrite_in, wwrite), (wq_in, wq), (wk_in, wk), (wv_in, wv), (wsq_in, wsq)]
        + [(late.at[n], work[n].buf) for n in range(early - 1)]
        + [(dwo_in, work[early - 1].buf.at[:wo_blocks])]
    )

    def load(n):
        return pltpu.make_async_copy(*whole[n], loads.at[n])

    for n in (*range(6, 5 + early), 0, 1):
        load(n).start()
    for n in range(used):
        block(n, 0).start()
    for n in (*range(2, 6), 5 + early):
        load(n).start()
    for i in range(1, count):
        for n in range(used):
            block(n, i).start()
    for i in range(count):
        for n in range(used, len(blocks)):
            block(n, i).start()
    greet(orders, index, group)
    for n in range(early - 1):
        load(6 + n).wait()
        work[n].tick(0)
    doc[...] = documents(lengths, index, group, doc.shape[1])
    load(0).wait()
    load(1).wait()
    update(
        index, stats, mem, slot_q, slot_k, slot_v, wgate, bgate, wwrite,
        new_memory, g, g_t, wlse, winner, sq_acc, sk_acc, sv_acc, direct,
        work[early - 1].buf.at[third : 2 * third], work[early - 1].buf.at[2 * third :], dbias, fresh,
    )
    for n in range(early - 1):
        work[n].tick(1)
    for n in range(2, 6):
        load(n).wait()
    for n in range(pairs):
        for m, w in enumerate((wq, wk, wv)):
            at = (3 * n + m) * wide
            w_all[:, at : at + wide] = w[:, two(n)]
    slots = group * mem.shape[2]
    unit3, inverse3 = norm(mem[:, 0].reshape(slots, mem.shape[3]).astype(F32))
    slot_low[...] = (unit3 * mgain[...]).astype(BF16)
    dgain[...] = jnp.zeros_like(dgain)
    acc[...] = jnp.zeros_like(acc)

    strides = [1 << n for n in reversed(range(group.bit_length() - 1))]

    def scatter(level):
        stride = strides[level]
        start, at = 0, 0
        for s in strides[:level]:
            start = start + across(index, "slot", s)[0] * s
            at += s
        bit, peer = across(index, "slot", stride)
        copy = pltpu.make_async_remote_copy(
            part.at[pl.ds(start + stride - bit * stride, stride)], part_in.at[pl.ds(at, stride)],
            part_sems.at[0, level], part_sems.at[1, level], device_id=peer, device_id_type=MESH,
        )
        return copy, start + bit * stride, at, stride

    def slot_grads(stage):
        if stage == 0:
            unit, inverse = norm(mem[:, 0].reshape(slots, mem.shape[3]).astype(F32))
            grad_t = 0.0
            for p in range(pairs):
                grad_t = (
                    grad_t
                    + nn(wk[:, two(p)], sk_acc[p].astype(BF16))
                    + nn(wv[:, two(p)], sv_acc[p].astype(BF16))
                    + nn(wsq[:, two(p)], (sq_acc[p] * SCALE).astype(BF16))
                )
            back, gain_part = norm_back(jnp.transpose(grad_t), unit, inverse, mgain[...])
            part[...] = (back + direct[...]).reshape(part.shape)
            dgain3[...] = gain_part
        else:
            copy, keep, at, size = scatter(stage - 1)
            copy.wait()
            part[pl.ds(keep, size)] += part_in[pl.ds(at, size)]
        if stage < len(strides):
            scatter(stage)[0].start()
        else:
            memory_grad[...] = part[index["slot"]]

    def gains(stage):
        item = work[early + pairs]
        if stage == 0:
            rows = [jnp.broadcast_to(r[...], (8, dgain.shape[1])) for r in (dgain, dgain3, dgain2, dbias)]
            item.buf[...] = tiles(jnp.concatenate(rows, 0).astype(BF16))
        item.tick(stage)
        if stage == item.stages - 1:
            gains_out[...] = item.buf[...].reshape(gains_out.shape).astype(F32)

    def summed(n, stage):
        item = work[n]
        if n == early - 1 and stage == 0:
            load(6 + n).wait()
        item.tick(stage)
        if stage < item.stages - 1:
            return
        if n < early:
            pltpu.make_async_copy(item.buf, sums[n], stores.at[n]).start()
            return
        per = wide // TILE
        for m, out in enumerate((dwq_out, dwk_out, dwv_out, dwsq_out)):
            rows = item.buf[m * per : (m + 1) * per].reshape(wide, out.shape[0])
            out[:, two(n - early)] = jnp.transpose(rows)

    busy = pairs * count
    last = busy + count - 1
    events = []
    for n in range(early - 1):
        events += [
            (1 + n + (6 - n) * (stage - 2) // 2, summed, (n, stage)) for stage in range(2, work[n].stages)
        ]
    events += [
        (2 + 2 * stage, summed, (early - 1, stage)) for stage in range(work[early - 1].stages)
    ]
    for n in range(pairs):
        events += [
            ((n + 1) * count - 1 + (stage if n > 1 else (4 - n) * stage // 2), summed, (early + n, stage))
            for stage in range(work[early + n].stages)
        ]
    events += [(busy + stage, slot_grads, (stage,)) for stage in range(len(strides) + 1)]
    events += [(busy + stage, gains, (stage,)) for stage in range(work[early + pairs].stages)]

    @pl.loop(0, busy)
    def _(step):
        p = step // count
        i = step % count

        @pl.when(p == 0)
        def _():
            for n in range(used):
                block(n, i).wait()
            cols = pl.ds(pl.multiple_of(i * SEG, SEG), SEG)
            bias[i] = segment_bias(doc[:, cols], pad[:, cols])

        cols = pl.ds(pl.multiple_of(i * SEG, SEG), SEG)
        pad_bias = jnp.where(pad[:, cols] > 0, 0.0, FILL)
        for odd in range(2):
            own = one(odd)
            qm = head_rows(q_t[i, p], odd)
            dm = head_rows(d_t[i, p], odd)
            c = nn(head_lanes(slot_q[p], odd), k_t[i, p]) + pad_bias
            share = jnp.exp(c - wlse[p, :, odd * DH : odd * DH + 1])
            dotted = nn(head_lanes(g[p], odd), v_t[i, p])
            change = (share * (dotted - winner[p, :, odd * DH : odd * DH + 1])).astype(BF16)
            dk = nn(slot_qt[p, own, :], change)
            dv = nn(g_t[p, own, :], share.astype(BF16))
            sq_acc[p, own, :] += nt(k_t[i, p, own, :], change)
            for lo, hi in BLOCKS:
                qb = qm[:, lo:hi]
                db = dm[:, lo:hi]
                qh = q_t[i, p, own, lo:hi]
                dh = d_t[i, p, own, lo:hi]
                l = lse[i, p, odd : odd + 1, lo:hi]
                t = inner[i, p, odd : odd + 1, lo:hi]
                e = jnp.exp(nn(k[i, p, :hi, :], qb) + bias[i, :hi, lo:hi] - l)
                em = jnp.exp(nn(slot_k[p], qb) - l)
                ds = (e * (nn(v[i, p, :hi, :], db) - t)).astype(BF16)
                dsm = (em * (nn(slot_v[p], db) - t)).astype(BF16)
                dq = (nn(k_t[i, p, own, :hi], ds) + nn(slot_kt[p, own, :], dsm)) * SCALE
                grads[i, p, own, lo:hi] = dq.astype(BF16)
                dvp = nt(dh, e.astype(BF16))
                dkp = nt(qh, ds)
                if hi < SEG:
                    dvp = jnp.concatenate([dvp, jnp.zeros((DH, SEG - hi), F32)], 1)
                    dkp = jnp.concatenate([dkp, jnp.zeros((DH, SEG - hi), F32)], 1)
                dv = dv + dvp
                dk = dk + dkp
                sv_acc[p, own, :] += nt(dh, em.astype(BF16))
                sk_acc[p, own, :] += nt(qh, dsm)
            grads[i, p, wide + odd * DH : wide + (odd + 1) * DH, :] = dk.astype(BF16)
            grads[i, p, 2 * wide + odd * DH : 2 * wide + (odd + 1) * DH, :] = dv.astype(BF16)
        acc[...] += nn(grads[i, p], low[i])

        @pl.when(i == count - 1)
        def _():
            rows = jnp.concatenate(
                [
                    acc[:wide],
                    acc[wide : 2 * wide] + nn(sk_acc[p].astype(BF16), slot_low[...]),
                    acc[2 * wide :] + nn(sv_acc[p].astype(BF16), slot_low[...]),
                    nn((sq_acc[p] * SCALE).astype(BF16), slot_low[...]),
                ],
                0,
            )
            rows = tiles(rows.astype(BF16))
            token = acc[...]
            acc[...] = jnp.zeros_like(acc)
            for n in range(pairs):

                @pl.when(p == n)
                def _():
                    w = jnp.transpose(w_all[:, n * 3 * wide : (n + 1) * 3 * wide]).astype(F32)
                    dgain[...] += jnp.sum(token * w, 0, keepdims=True) / gain1[...]
                    work[early + n].buf[...] = rows

        run_events(step, last, [e for e in events if e[0] < busy])

    @pl.loop(0, count)
    def _(i):
        block(used, i).wait()
        block(used + 1, i).wait()
        unit, inverse = norm(x[i].astype(F32))
        grad_t = nn(w_all[...], grads[i].reshape(3 * pairs * wide, SEG))
        back, _ = norm_back(jnp.transpose(grad_t), unit, inverse, gain1[...])
        res[i] += back
        pltpu.make_async_copy(res.at[i], input_grad.at[i], block_loads.at[0, i]).start()
        run_events(i + busy, last, [e for e in events if e[0] >= busy])

    for i in range(count):
        pltpu.make_async_copy(res.at[i], input_grad.at[i], block_loads.at[0, i]).wait()
    for n in range(early):
        pltpu.make_async_copy(work[n].buf, sums[n], stores.at[n]).wait()


def widen_kernel(chunks, half, *refs):
    ffn, rest = refs[:chunks], refs[chunks:]
    own, dwq, dwk, dwv, dwsq, layer_in, grad_in, new_in, mem_in, gains_in = rest[:10]
    (
        layer_out, new_out, grad_out, mem_out,
        dwq_out, dwk_out, dwv_out, dwo_out, dwsq_out, dwgate_out, dwwrite_out, dwup_out, dwdown_out,
    ) = rest[10:23]
    gain_outs = rest[23:27]
    layer, grad, slots, gains, low, wide = rest[27:33]
    rows, loads, stores = rest[33:37], rest[37], rest[38]
    count, seg = layer.shape[:2]

    jobs = [(dwq, dwq_out), (dwk, dwk_out), (dwv, dwv_out), (dwsq, dwsq_out)]
    for n, out in enumerate((dwo_out, dwgate_out, dwwrite_out)):
        jobs.append((own.at[n * half : (n + 1) * half], out))
    for c in range(chunks):
        jobs.append((ffn[c].at[:half], dwup_out.at[:, c * seg : (c + 1) * seg]))
        jobs.append((ffn[c].at[half:], dwdown_out.at[c * seg : (c + 1) * seg, :]))
    passed = [(gains_in, gains, None)]
    passed += [(new_in, slots.at[0], new_out), (mem_in, slots.at[1], mem_out)]
    for i in range(count):
        passed += [
            (grad_in.at[i], grad.at[i], grad_out.at[i]),
            (layer_in.at[i], layer.at[i], layer_out.at[i]),
        ]
    moves = [(source, low.at[n], wide.at[n], target) for n, (source, target) in enumerate(jobs)]
    todo = []
    for n in range(max(len(moves), len(passed))):
        todo += moves[n : n + 1] + passed[n : n + 1]
    copies = [pltpu.make_async_copy(t[0], t[1], loads.at[n]) for n, t in enumerate(todo)]
    for copy in copies:
        copy.start()
    sent = []

    def send(source, target):
        copy = pltpu.make_async_copy(source, target, stores.at[len(sent)])
        copy.start()
        sent.append(copy)

    for copy, t in zip(copies, todo):
        copy.wait()
        if len(t) == 4:
            _, narrow, full, target = t
            per = 4

            @pl.loop(0, half // per)
            def _(b):
                at = pl.ds(pl.multiple_of(b * per * TILE, per * TILE), per * TILE)
                full[at, :] = narrow[pl.ds(b * per, per)].reshape(per * TILE, full.shape[1]).astype(F32)

            send(full, target)
        elif t[2] is None:
            for n, at in enumerate((0, 16, 8, 24)):
                rows[n][...] = gains[at : at + 1, :]
                send(rows[n], gain_outs[n])
        else:
            send(t[1], t[2])
    for copy in sent:
        copy.wait()


def struct(shape, dtype):
    return jax.ShapeDtypeStruct(shape, dtype)


def params(collective_id):
    return pltpu.CompilerParams(
        vmem_limit_bytes=63 << 20, collective_id=collective_id, has_side_effects=True
    )


def body(
    tokens,
    memory,
    pad_mask,
    doc_lengths,
    first_gain,
    query_weight,
    key_weight,
    value_weight,
    out_weight,
    second_gain,
    up_weight,
    down_weight,
    memory_gain,
    slot_query_weight,
    gate_weight,
    gate_bias,
    write_weight,
    out_cotangent,
    memory_cotangent,
):
    rows, width = tokens.shape
    hidden = up_weight.shape[1]
    count = rows // SEG
    chunks = hidden // SEG
    pairs = H // 2
    two_heads = 2 * DH
    slots_here = memory.shape[1]
    group = lax.axis_size("slot")
    slots = slots_here * group
    pad = pad_mask[None, :]
    gain1, gain2, gain3 = (g[None, :] for g in (first_gain, second_gain, memory_gain))
    orders = bit_orders({"dp": lax.axis_size("dp"), "slot": group})

    anywhere = pl.BlockSpec(memory_space=pl.ANY)
    vm = pl.BlockSpec(memory_space=pltpu.VMEM)
    sm = pl.BlockSpec(memory_space=pltpu.SMEM)
    tokens = tokens.reshape(count, SEG, width)
    segments = (count, SEG, width)
    by_rows = (count, pairs, SEG, two_heads)
    by_lanes = (count, pairs, two_heads, SEG)
    square = (width, width)
    blocks = 2 * SEG // TILE
    half = SEG // TILE
    slot_tall, slot_wide = (pairs, slots, two_heads), (pairs, two_heads, slots)
    per_head = (count, pairs, 2, SEG)
    outs = pl.pallas_call(
        lambda *refs: front_kernel(count, chunks, group, orders, *refs),
        in_specs=[anywhere] * 11 + [sm] + [vm] * 4,
        out_specs=[anywhere] * (10 + EARLY) + [vm] * 11,
        out_shape=[
            struct(segments, BF16), struct(segments, F32), struct(segments, BF16),
            struct(by_lanes, BF16), struct(by_rows, BF16), struct(by_lanes, BF16),
            struct(by_rows, BF16), struct(by_lanes, BF16), struct((count, width, SEG), BF16),
            struct((chunks - EARLY, blocks, TILE, width), BF16),
        ]
        + [struct((blocks, TILE, width), BF16)] * EARLY
        + [
            struct(per_head, F32), struct(per_head, F32), struct(slot_tall, BF16),
            struct(slot_wide, BF16), struct(slot_tall, BF16), struct(slot_tall, BF16),
            struct(slot_wide, BF16), struct((group, 2, slots_here, width), BF16),
            struct((group, 3, slots, width), F32), struct(square, BF16), struct((1, width), F32),
        ],
        scratch_shapes=[
            pltpu.VMEM(segments, BF16), pltpu.VMEM(segments, BF16), pltpu.VMEM(segments, BF16),
            pltpu.VMEM(by_lanes, BF16), pltpu.VMEM(by_rows, BF16), pltpu.VMEM(by_lanes, BF16),
            pltpu.VMEM(by_rows, BF16), pltpu.VMEM(by_lanes, BF16),
            pltpu.VMEM((count, width, SEG), BF16), pltpu.VMEM(segments, BF16),
            pltpu.VMEM((count, width, SEG), BF16), pltpu.VMEM((count, width, SEG), BF16),
            pltpu.VMEM(segments, F32), pltpu.VMEM(segments, F32),
            pltpu.VMEM(square, BF16), pltpu.VMEM(square, BF16), pltpu.VMEM(square, BF16),
            pltpu.VMEM(square, BF16), pltpu.VMEM(square, BF16),
            pltpu.VMEM((chunks, width, SEG), BF16), pltpu.VMEM((chunks, SEG, width), BF16),
            pltpu.VMEM(slot_wide, BF16), pltpu.VMEM((SEG, SEG), F32), pltpu.VMEM(square, F32),
            pltpu.VMEM((width, SEG), F32), pltpu.VMEM((width, SEG), F32),
            pltpu.VMEM(segments, BF16), pltpu.VMEM((chunks - EARLY, blocks, TILE, width), BF16),
            pltpu.VMEM((1, rows), F32),
            pltpu.SemaphoreType.DMA((2 * count + 7 + 2 * chunks,)),
            pltpu.SemaphoreType.DMA((9, count)),
            pltpu.SemaphoreType.DMA((2, 2, group)),
            pltpu.SemaphoreType.DMA((chunks,)),
        ]
        + reduction_scratch([blocks] * EARLY, orders, width),
        compiler_params=params(0),
        name="front",
    )(
        tokens, memory[0], memory_cotangent[0], query_weight, key_weight, value_weight,
        slot_query_weight, out_weight, up_weight, down_weight.reshape(chunks, SEG, width),
        out_cotangent.reshape(segments), doc_lengths, pad, gain1, gain2, gain3,
    )
    layer_out, res_grad, low, q_t, k, k_t, v, v_t, d_t, late = outs[:10]
    early = list(outs[10 : 10 + EARLY])
    (
        lse, inner, slot_k, slot_kt, slot_v, slot_q, slot_qt, mem, stats, dwo, dgain2,
    ) = outs[10 + EARLY :]

    sizes = [blocks] * (chunks - EARLY) + [3 * half]
    n_sum = len(sizes)
    outs = pl.pallas_call(
        lambda *refs: back_kernel(count, group, orders, sizes, *refs),
        in_specs=[anywhere] * 17 + [vm] * 2 + [sm] + [vm] * 12,
        out_specs=[anywhere] * (1 + n_sum) + [vm] * 7,
        out_shape=[struct(segments, F32)]
        + [struct((n, TILE, width), BF16) for n in sizes]
        + [struct(square, BF16)] * 4
        + [
            struct((32, width), F32), struct((slots_here, width), F32), struct((slots_here, width), F32),
        ],
        scratch_shapes=[
            pltpu.VMEM(segments, BF16), pltpu.VMEM(segments, BF16), pltpu.VMEM(by_lanes, BF16),
            pltpu.VMEM(by_rows, BF16), pltpu.VMEM(by_lanes, BF16), pltpu.VMEM(by_rows, BF16),
            pltpu.VMEM(by_lanes, BF16), pltpu.VMEM(by_lanes, BF16), pltpu.VMEM(segments, F32),
            pltpu.VMEM(square, BF16), pltpu.VMEM(square, BF16), pltpu.VMEM(square, BF16),
            pltpu.VMEM(square, BF16), pltpu.VMEM(square, BF16), pltpu.VMEM(square, BF16),
            pltpu.VMEM((count, SEG, SEG), F32), pltpu.VMEM((count, pairs, 3 * two_heads, SEG), BF16),
            pltpu.VMEM((3 * two_heads, width), F32), pltpu.VMEM((width, 3 * width), BF16),
            pltpu.VMEM(slot_wide, F32), pltpu.VMEM(slot_wide, F32), pltpu.VMEM(slot_wide, F32),
            pltpu.VMEM(slot_tall, BF16), pltpu.VMEM(slot_wide, BF16), pltpu.VMEM(slot_tall, F32),
            pltpu.VMEM(slot_tall, F32), pltpu.VMEM((slots, width), F32),
            pltpu.VMEM((group, slots_here, width), F32), pltpu.VMEM((slots, width), BF16),
            pltpu.VMEM((1, width), F32), pltpu.VMEM((1, width), F32), pltpu.VMEM((1, width), F32),
            pltpu.VMEM((group, slots_here, width), F32), pltpu.VMEM((group, slots_here, width), F32),
            pltpu.VMEM((1, rows), F32),
            pltpu.SemaphoreType.DMA((2, group)), pltpu.SemaphoreType.DMA((9, count)),
            pltpu.SemaphoreType.DMA((6 + n_sum,)), pltpu.SemaphoreType.DMA((n_sum,)),
        ]
        + reduction_scratch(sizes + [4 * two_heads // TILE] * pairs + [2], orders, width),
        compiler_params=params(1),
        name="back",
    )(
        tokens, low, q_t, k, k_t, v, v_t, d_t.reshape(by_lanes), res_grad,
        query_weight, key_weight, value_weight, slot_query_weight, gate_weight, write_weight,
        late, tiles(dwo),
        lse, inner, doc_lengths, pad, gain1, gain3, slot_k, slot_kt, slot_v, slot_q, slot_qt, mem, stats,
        gate_bias[None, :], dgain2,
    )
    input_grad = outs[0]
    sums = list(outs[1 : 1 + n_sum])
    dwq, dwk, dwv, dwsq, gains, memory_grad, new_memory = outs[1 + n_sum :]
    ffn = early + sums[:-1]
    low_jobs = 7 + 2 * chunks
    outs = pl.pallas_call(
        lambda *refs: widen_kernel(chunks, half, *refs),
        in_specs=[anywhere] * (chunks + 10),
        out_specs=[anywhere] * 17,
        out_shape=[
            struct(segments, BF16), struct((slots_here, width), F32), struct(segments, F32),
            struct((slots_here, width), F32),
        ]
        + [struct(square, F32)] * 7
        + [struct((width, hidden), F32), struct((hidden, width), F32)]
        + [struct((1, width), F32)] * 4,
        scratch_shapes=[
            pltpu.VMEM(segments, BF16), pltpu.VMEM(segments, F32),
            pltpu.VMEM((2, slots_here, width), F32), pltpu.VMEM((32, width), F32),
            pltpu.VMEM((low_jobs, half, TILE, width), BF16), pltpu.VMEM((low_jobs, width, width), F32),
        ]
        + [pltpu.VMEM((1, width), F32)] * 4
        + [
            pltpu.SemaphoreType.DMA((2 * count + 3 + low_jobs,)),
            pltpu.SemaphoreType.DMA((2 * count + 6 + low_jobs,)),
        ],
        compiler_params=pltpu.CompilerParams(vmem_limit_bytes=63 << 20),
        name="widen",
    )(
        *ffn, sums[-1], tiles(dwq), tiles(dwk), tiles(dwv), tiles(dwsq),
        layer_out, input_grad, new_memory, memory_grad, gains,
    )
    layer_out, new_memory, input_grad, memory_grad = outs[:4]
    dwq, dwk, dwv, dwo, dwsq, dwgate, dwwrite, dwup, dwdown = outs[4:13]
    gain1, gain2, gain3, bias = (r[0] for r in outs[13:])
    return (
        layer_out.reshape(rows, width), new_memory[None], input_grad.reshape(rows, width),
        memory_grad[None], gain1, dwq, dwk, dwv, dwo, gain2, dwup, dwdown, gain3, dwsq, dwgate,
        bias, dwwrite,
    )


def solution(mesh):
    token = P(("dp", "slot"), None)
    slot = P("dp", "slot", None)
    in_specs = (
        (token, slot, P(("dp", "slot"))) + (P(),) * 14 + (token, slot)
    )
    out_specs = (token, slot, token, slot) + (P(),) * 13
    return jax.shard_map(body, mesh=mesh, in_specs=in_specs, out_specs=out_specs, check_vma=False)
```
